32 devices in a mesh: fsdp: 8 (over y, x, core), tp: 4 (over z).
Axes of the slice: x: 2, y: 2, z: 4, core: 2. Of those that a mesh axis runs over, the one named last changes fastest.
Arguments:
- residual: bfloat16 [4096, 2048], P(('fsdp', 'tp')), may hold values from -6 to 6
- norm_gain: bfloat16 [2048], P(('fsdp', 'tp')), may hold values from 0.099609375 to 1.8984375
- norm_shift: bfloat16 [2048], P(('fsdp', 'tp')), may hold values from -1.75 to 1.75
- qkv_weight: bfloat16 [3, 2048, 2048], P(None, 'fsdp', 'tp'), may hold values from -0.125 to 0.125
- qkv_bias: bfloat16 [3, 2048], P(None, ('tp', 'fsdp')), may hold values from -1.75 to 1.75
- dense_weight: bfloat16 [2048, 2048], P('tp', 'fsdp'), may hold values from -0.75 to 0.75
- dense_bias: bfloat16 [2048], P(('fsdp', 'tp')), may hold values from -1.75 to 1.75
- inner_weight: bfloat16 [2048, 8192], P('fsdp', 'tp'), may hold values from -0.125 to 0.125
- inner_bias: bfloat16 [8192], P(('tp', 'fsdp')), may hold values from -1.75 to 1.75
- outer_weight: bfloat16 [8192, 2048], P('tp', 'fsdp'), may hold values from -0.0625 to 0.0625
- outer_bias: bfloat16 [2048], P(('fsdp', 'tp')), may hold values from -1.75 to 1.75
- cotangent: bfloat16 [4096, 2048], P(('fsdp', 'tp')), may hold values from -6 to 6
- segment: int32 [4096], replicated, may hold values from 0 to 38, as said below
- ancestors: int32 [39, 3], replicated, may hold values from 0 to 38, as said below
- valid_slot: int32 [4096], replicated, may hold values from 0 to 1, as said below
Outputs:
- output: bfloat16 [4096, 2048], P(('fsdp', 'tp'))
- residual_grad: bfloat16 [4096, 2048], P(('fsdp', 'tp'))
- norm_gain_grad: float32 [2048], P(('fsdp', 'tp'))
- norm_shift_grad: float32 [2048], P(('fsdp', 'tp'))
- qkv_weight_grad: float32 [3, 2048, 2048], P(None, 'fsdp', 'tp')
- qkv_bias_grad: float32 [3, 2048], P(None, ('tp', 'fsdp'))
- dense_weight_grad: float32 [2048, 2048], P('tp', 'fsdp')
- dense_bias_grad: float32 [2048], P(('fsdp', 'tp'))
- inner_weight_grad: float32 [2048, 8192], P('fsdp', 'tp')
- inner_bias_grad: float32 [8192], P(('tp', 'fsdp'))
- outer_weight_grad: float32 [8192, 2048], P('tp', 'fsdp')
- outer_bias_grad: float32 [2048], P(('fsdp', 'tp'))
The draws below stay inside these ranges and needn't reach their ends.
Inputs may be any that keep to these rules, and one draw needn't show every extreme that they name: Each of the 3 trees fills 1024 consecutive slots, in order of slots: a trunk of 640 slots, then four branches and eight leaves of 32 slots each, two leaves to a branch, each leaf after its branch; the slots of a segment are consecutive and carry its id; padding slots carry 0. `ancestors`: row s names the trunk, branch and leaf segment of the path that ends in segment s, repeating s where the path is shorter; each tree's segments name only that tree's segments. `valid_slot`: 1 on exactly the slots that trees fill, 0 on the other 1024 slots.
All inputs are finite; a program needn't handle non-finite values.
Results may differ from the reference program's by a relative error of at most 0.0098.
Values may be sent and summed in bfloat16 or wider, within the bound.
No kernel may reach another device: no remote copies, remote signals or barrier semaphores. Data moves between devices by JAX's collectives and lax.ppermute only.
A program may use at most 192 MiB of HBM per device.

```python
import jax
import jax.numpy as jnp
import numpy as np
from jax import lax

D = 2048
HEADS = 32
HEAD_DIM = 64
ROTARY = 32
FF = 8192
TRUNK = 640
LIMB = 32
TREE_LEN = 1024
TOKENS = 4096
TREES = 3
SEGS = 39


LOCAL_PATHS = np.array([[0, 0, 0], [0, 1, 1], [0, 2, 2], [0, 3, 3], [0, 4, 4], [0, 1, 5], [0, 1, 6], [0, 2, 7], [0, 2, 8], [0, 3, 9], [0, 3, 10], [0, 4, 11], [0, 4, 12]], dtype=np.int32)


def tree_layout(key):
    base_key = jax.random.fold_in(key, 101)
    cut_key, order_key, label_key = jax.random.split(base_key, 3)
    spare = TOKENS - TREES * TREE_LEN
    cuts = jnp.sort(jax.random.randint(cut_key, (TREES,), 0, spare + 1))
    starts = jnp.arange(TREES, dtype=jnp.int32) * TREE_LEN + cuts
    breadth = jax.random.randint(order_key, (TREES,), 0, 2)
    labels = jax.random.permutation(label_key, SEGS).astype(jnp.int32)
    slots = jnp.arange(TOKENS, dtype=jnp.int32)
    relative = slots[:, None] - starts[None, :]
    inside = (relative >= 0) & (relative < TREE_LEN)
    valid = jnp.any(inside, axis=1).astype(jnp.int32)
    tree_of = jnp.sum(jnp.where(inside, jnp.arange(TREES, dtype=jnp.int32)[None, :], 0), axis=1)
    offset = jnp.sum(jnp.where(inside, relative, 0), axis=1)
    after = jnp.maximum(offset - TRUNK, 0) // LIMB
    depth_first = jnp.where(after % 3 == 0, 1 + after // 3, 4 + 2 * (after // 3) + after % 3)
    local_label = jnp.where(offset < TRUNK, 0, jnp.where(breadth[tree_of] == 1, 1 + after, depth_first))
    segment = jnp.where(valid == 1, labels[tree_of * 13 + local_label], 0)
    paths = jnp.asarray(LOCAL_PATHS)
    nodes = jnp.arange(SEGS, dtype=jnp.int32)
    path_global = labels[(nodes // 13)[:, None] * 13 + paths[nodes % 13]]
    inverse = jnp.argsort(labels)
    ancestors = path_global[inverse]
    return (segment.astype(jnp.int32), ancestors.astype(jnp.int32), valid)


def draw_segment(key, part):
    return tree_layout(key)[0]


def draw_ancestors(key, part):
    return tree_layout(key)[1]


def draw_valid_slot(key, part):
    return tree_layout(key)[2]


def block_levels(rng, dims, cuts, least, largest):
    loudness = 1.0
    for position, shards_of in cuts:
        draws = jax.random.uniform(jax.random.fold_in(jax.random.fold_in(rng, 6), position), (shards_of,), jnp.float32, least / len(cuts), largest / len(cuts))
        loudness = loudness * jnp.repeat(jnp.exp(draws), dims[position] // shards_of).reshape((-1,) + (1,) * (len(dims) - 1 - position))
    return loudness


def bell_draw(own_key, dims, deviation, limit, cuts=(), kind=jnp.bfloat16):
    level = block_levels(own_key, dims, cuts, -0.22, 0.18) if cuts else 1.0
    result = jax.random.normal(own_key, dims, jnp.float32) * deviation * level
    return jnp.minimum(jnp.maximum(result, -limit), limit).astype(kind)


def setup_inputs(seed: int = 0) -> dict:
    splits = jax.random.split(jax.random.key(seed), 16)
    return {
        "residual": bell_draw(splits[0], (TOKENS, D), 1.0, 6.0, ((0, 32),)),
        "norm_gain": jnp.clip(1.0 + 0.18 * jax.random.normal(splits[1], (D,), jnp.float32), 0.099609375, 1.8984375).astype(jnp.bfloat16),
        "norm_shift": bell_draw(splits[2], (D,), 0.3, 1.75, ((0, 32),)),
        "qkv_weight": bell_draw(splits[3], (3, D, D), D ** -0.5, 0.125, ((1, 8), (2, 4))),
        "qkv_bias": bell_draw(splits[4], (3, D), 0.3, 1.75, ((1, 32),)),
        "dense_weight": bell_draw(splits[5], (D, D), (D // 32) ** -0.5, 0.75, ((0, 4), (1, 8))),
        "dense_bias": bell_draw(splits[6], (D,), 0.3, 1.75, ((0, 32),)),
        "inner_weight": bell_draw(splits[7], (D, FF), D ** -0.5, 0.125, ((0, 8), (1, 4))),
        "inner_bias": bell_draw(splits[8], (FF,), 0.3, 1.75, ((0, 32),)),
        "outer_weight": bell_draw(splits[9], (FF, D), FF ** -0.5, 0.0625, ((0, 4), (1, 8))),
        "outer_bias": bell_draw(splits[10], (D,), 0.3, 1.75, ((0, 32),)),
        "cotangent": bell_draw(splits[11], (TOKENS, D), 1.0, 6.0, ((0, 32),)),
        "segment": draw_segment(jax.random.fold_in(splits[15], 71), 0),
        "ancestors": draw_ancestors(jax.random.fold_in(splits[15], 71), 0),
        "valid_slot": draw_valid_slot(jax.random.fold_in(splits[15], 71), 0),
    }


EPSILON = 1e-05
HIGHEST = lax.Precision.HIGHEST

@jax.custom_vjp
def low(v):
    return lax.optimization_barrier(v.astype(jnp.bfloat16)).astype(jnp.float32)

@jax.custom_vjp
def low_back(v):
    return v

def low_keep(v):
    return (low(v), None)

def low_pass(kept, grad):
    return (grad,)

def back_keep(v):
    return (v, None)

def back_low(kept, grad):
    return (low(grad),)
low.defvjp(low_keep, low_pass)
low_back.defvjp(back_keep, back_low)

def tree_allowed(query_seg, query_slot, query_valid, key_seg, key_slot, key_valid, ancestors):
    seg_ids = jnp.arange(ancestors.shape[0], dtype=jnp.int32)
    onehot = (query_seg[:, None] == seg_ids[None, :]).astype(jnp.int32)
    path_ids = lax.optimization_barrier(jnp.sum(onehot[:, :, None] * ancestors[None, :, :], axis=1))
    linked = (key_seg[None, :] == path_ids[:, 0:1]) | (key_seg[None, :] == path_ids[:, 1:2]) | (key_seg[None, :] == path_ids[:, 2:3])
    earlier = key_slot[None, :] <= query_slot[:, None]
    usable = (key_valid[None, :] == 1) & (query_valid[:, None] == 1)
    return linked & earlier & usable | (key_slot[None, :] == query_slot[:, None])

def rotate(tensor, positions, direction):
    half_rot = ROTARY // 2
    freq = 10000.0 ** (-(jnp.arange(half_rot, dtype=jnp.float32) * 2.0 / ROTARY))
    angle = direction * positions.astype(jnp.float32)[:, None] * freq[None, :]
    cosine = jnp.cos(angle)[:, None, :]
    sine = jnp.sin(angle)[:, None, :]
    first = tensor[..., :half_rot]
    second = tensor[..., half_rot:ROTARY]
    return jnp.concatenate([first * cosine - second * sine, second * cosine + first * sine, tensor[..., ROTARY:]], axis=-1)

def reference(residual, norm_gain, norm_shift, qkv_weight, qkv_bias, dense_weight, dense_bias, inner_weight, inner_bias, outer_weight, outer_bias, cotangent, segment, ancestors, valid_slot):
    block_rows = min(512, TOKENS)
    block_count = TOKENS // block_rows
    reach_back = TREE_LEN
    key_span = reach_back + block_rows
    seg_front = jnp.concatenate([jnp.zeros((reach_back,), jnp.int32), segment])
    valid_front = jnp.concatenate([jnp.zeros((reach_back,), jnp.int32), valid_slot])
    slot_front = jnp.arange(TOKENS + reach_back, dtype=jnp.int32) - reach_back
    all_slots = jnp.arange(TOKENS, dtype=jnp.int32)

    def allowed_block(block_num):
        row_begin = (block_num * block_rows).astype(jnp.int32)
        return tree_allowed(lax.dynamic_slice_in_dim(segment, row_begin, block_rows), lax.dynamic_slice_in_dim(all_slots, row_begin, block_rows), lax.dynamic_slice_in_dim(valid_slot, row_begin, block_rows), lax.dynamic_slice_in_dim(seg_front, row_begin, key_span), lax.dynamic_slice_in_dim(slot_front, row_begin, key_span), lax.dynamic_slice_in_dim(valid_front, row_begin, key_span), ancestors)

    def count_keys(block_num):
        return lax.optimization_barrier(jnp.sum(allowed_block(block_num).astype(jnp.int32), axis=1)) - 1
    block_ids = jnp.arange(block_count, dtype=jnp.int32)
    positions = lax.map(count_keys, block_ids).reshape(TOKENS)
    scaling = HEAD_DIM ** (-0.5)

    def forward(inputs_f, gain_f, shift_f, w_qkv, b_qkv, w_dense, b_dense, w_inner, b_inner, w_outer, b_outer):
        row_mean = lax.optimization_barrier(jnp.mean(inputs_f, axis=-1, keepdims=True))
        centered = inputs_f - row_mean
        variance = lax.optimization_barrier(jnp.mean(centered * centered, axis=-1, keepdims=True))
        normed = low(centered * lax.rsqrt(variance + EPSILON) * gain_f + shift_f)
        mixed = jnp.einsum('td,sde->ste', normed, w_qkv, precision=HIGHEST) + b_qkv[:, None, :]
        queries = low(rotate(low_back(mixed[0]).reshape(TOKENS, HEADS, HEAD_DIM), positions, 1.0))
        keys_all = low(rotate(low_back(mixed[1]).reshape(TOKENS, HEADS, HEAD_DIM), positions, 1.0))
        values_all = low(low_back(mixed[2])).reshape(TOKENS, HEADS, HEAD_DIM)
        zero_front = jnp.zeros((reach_back, HEADS, HEAD_DIM), jnp.float32)
        keys_front = jnp.concatenate([zero_front, keys_all], axis=0)
        values_front = jnp.concatenate([zero_front, values_all], axis=0)

        def attend(block_num):
            row_begin = (block_num * block_rows).astype(jnp.int32)
            query_block = lax.dynamic_slice_in_dim(queries, row_begin, block_rows)
            key_block = lax.dynamic_slice_in_dim(keys_front, row_begin, key_span)
            value_block = lax.dynamic_slice_in_dim(values_front, row_begin, key_span)
            scores = low_back(jnp.einsum('qhe,khe->hqk', query_block, key_block, precision=HIGHEST) * scaling)
            scores = jnp.where(allowed_block(block_num)[None], scores, -jnp.inf)
            weights = low(jax.nn.softmax(scores, axis=-1))
            return jnp.einsum('hqk,khe->qhe', weights, value_block, precision=HIGHEST)
        attended = lax.map(jax.checkpoint(attend), block_ids)
        attended = low(low_back(attended.reshape(TOKENS, D)))
        branch_attn = jnp.dot(attended, w_dense, precision=HIGHEST)
        pre_act = low_back(jnp.dot(normed, w_inner, precision=HIGHEST) + b_inner)
        activated = low(jax.nn.gelu(pre_act, approximate=True))
        branch_mlp = jnp.dot(activated, w_outer, precision=HIGHEST)
        return inputs_f + branch_attn + branch_mlp + b_dense + b_outer
    output, pullback = jax.vjp(forward, residual.astype(jnp.float32), norm_gain.astype(jnp.float32), norm_shift.astype(jnp.float32), qkv_weight.astype(jnp.float32), qkv_bias.astype(jnp.float32), dense_weight.astype(jnp.float32), dense_bias.astype(jnp.float32), inner_weight.astype(jnp.float32), inner_bias.astype(jnp.float32), outer_weight.astype(jnp.float32), outer_bias.astype(jnp.float32))
    grads = pullback(cotangent.astype(jnp.float32))
    return (output.astype(jnp.bfloat16), grads[0].astype(jnp.bfloat16), grads[1], grads[2], grads[3], grads[4], grads[5], grads[6], grads[7], grads[8], grads[9], grads[10])
```

```python
import jax
import jax.numpy as jnp
from jax import lax
from jax.experimental import pallas as pl
from jax.experimental.pallas import tpu as pltpu
from jax.sharding import PartitionSpec as P

HEAD_DIM = 64
ROTARY = 32
TREE_LEN = 1024
EPSILON = 1e-05
LANES = 128
QROWS = 256
KROWS = 256
MASKED = -1e30

f32 = jnp.float32
bf16 = jnp.bfloat16

NN = (((1,), (0,)), ((), ()))
NT = (((1,), (1,)), ((), ()))
TN = (((0,), (0,)), ((), ()))


def dot(left, right, dims=NN):
    return lax.dot_general(left, right, dims, preferred_element_type=f32)


class Layout:
    def __init__(self):
        self.fs = lax.axis_size("fsdp")
        self.tp = lax.axis_size("tp")
        chips = self.fs // 2
        self.A = 2
        self.B = chips // 2
        index = lax.axis_index("fsdp")
        self.index = index
        self.core = index % 2
        self.chip = index // 2
        self.a = self.chip // self.B
        self.b = self.chip % self.B
        self.z = lax.axis_index("tp")
        self.is0 = self.core == 0

    def blocks(self):
        A, B = self.A, self.B
        first = [(0, i, j) for i in range(A) for j in range(B)]
        second = [(1, i, j) for j in range(B) for i in range(A)]
        return first + second

    def offsets(self):
        out = []
        for core, i, j in self.blocks():
            chip = ((self.a + i) % self.A) * self.B + (self.b + j) % self.B
            out.append(chip * 2 + core)
        return jnp.stack(out).astype(jnp.int32)

    def pair_of(self, fn):
        A, B = self.A, self.B
        pairs = []
        for a in range(A):
            for b in range(B):
                for c in range(2):
                    pairs.append(((a * B + b) * 2 + c, fn(a, b, c)))
        return pairs

    def over_core(self, value):
        B = self.B
        return lax.ppermute(value, "fsdp", self.pair_of(lambda a, b, c: (a * B + b) * 2 + 1 - c))

    def along_a(self, value, steps):
        A, B = self.A, self.B
        return lax.ppermute(
            value, "fsdp", self.pair_of(lambda a, b, c: (((a + steps) % A) * B + b) * 2 + c)
        )

    def along_b(self, value, steps):
        B = self.B
        return lax.ppermute(
            value, "fsdp", self.pair_of(lambda a, b, c: (a * B + (b + steps) % B) * 2 + c)
        )

    def along_z(self, value, steps):
        n = self.tp
        return lax.ppermute(value, "tp", [(s, (s + steps) % n) for s in range(n)])

    def with_partner(self, value, axis, bit):
        size = self.fs if axis == "fsdp" else self.tp
        return lax.ppermute(value, axis, [(s, s ^ bit) for s in range(size)])

    def bits(self):
        out = []
        for axis, size, index in (("tp", self.tp, self.z), ("fsdp", self.fs, self.index)):
            bit = 1
            while bit < size:
                out.append((axis, bit, (index // bit) % 2 == 1))
                bit *= 2
        return out

    def by_core(self, own, other):
        return jnp.where(self.is0, own, other), jnp.where(self.is0, other, own)


def gather_pieces(lay, first, second):
    A, B = lay.A, lay.B
    p_row = jnp.stack([first] + [lay.along_b(first, -j) for j in range(1, B)])
    q_row = jnp.stack([second] + [lay.along_a(second, -i) for i in range(1, A)])
    p_far = [lay.along_a(p_row, -i) for i in range(1, A)]
    q_far = [lay.along_b(q_row, -j) for j in range(1, B)]
    p_far = p_far[0] if A == 2 else jnp.concatenate(p_far)
    q_far = q_far[0] if B == 2 else jnp.concatenate(q_far)
    return (p_row, p_far, q_row, q_far)


def scatter_pieces(lay, near, far):
    A, B = lay.A, lay.B
    p_row, q_row = near
    p_far, q_far = far
    p_sum = p_row.astype(f32)
    for i in range(1, A):
        p_sum = p_sum + lay.along_a(p_far[(i - 1) * B : i * B], i).astype(f32)
    q_sum = q_row.astype(f32)
    for j in range(1, B):
        q_sum = q_sum + lay.along_b(q_far[(j - 1) * A : j * A], j).astype(f32)
    p_out = p_sum[0]
    for j in range(1, B):
        p_out = p_out + lay.along_b(p_sum[j].astype(bf16), j).astype(f32)
    q_out = q_sum[0]
    for i in range(1, A):
        q_out = q_out + lay.along_a(q_sum[i].astype(bf16), i).astype(f32)
    return p_out, q_out


def small_gather(lay, row):
    held = row
    for axis, bit, upper in lay.bits():
        got = lay.with_partner(held, axis, bit)
        held = jnp.concatenate([jnp.where(upper, got, held), jnp.where(upper, held, got)])
    return held


def small_scatter(lay, rows):
    held = rows
    for axis, bit, upper in reversed(lay.bits()):
        size = held.shape[0] // 2
        low, high = held[:size], held[size:]
        got = lay.with_partner(jnp.where(upper, low, high), axis, bit)
        held = jnp.where(upper, high, low) + got
    return held


def ring_gather(lay, own):
    n = lay.tp
    half = own.shape[0] // 2
    held = {0: own}
    up, down = own, own
    for step in range(1, n // 2):
        up = lay.along_z(up, 1)
        down = lay.along_z(down, -1)
        held[n - step] = up
        held[step] = down
    low = lay.along_z(up[:half], 1)
    high = lay.along_z(down[half:], -1)
    held[n // 2] = jnp.concatenate([low, high])
    ordered = jnp.concatenate([held[m % n] for m in range(2 * n - 1)])
    start = ((n - lay.z) % n) * own.shape[0]
    return lax.dynamic_slice_in_dim(ordered, start, n * own.shape[0])


def ring_scatter(lay, rows):
    n = lay.tp
    size = rows.shape[0] // n
    half = size // 2
    twice = jnp.concatenate([rows, rows])
    turned = lax.dynamic_slice_in_dim(twice, lay.z * size, n * size)

    def block(m):
        return turned[(m % n) * size : (m % n) * size + size]

    far = block(n // 2)
    up_low = lay.along_z(far[:half], 1)
    down_high = lay.along_z(far[half:], -1)
    up = jnp.concatenate(
        [block(n // 2 - 1)[:half].astype(f32) + up_low.astype(f32), block(n // 2 - 1)[half:].astype(f32)]
    )
    low = n // 2 + 1
    down = jnp.concatenate(
        [block(low)[:half].astype(f32), block(low)[half:].astype(f32) + down_high.astype(f32)]
    )
    for step in range(1, n // 2):
        up_got = lay.along_z(up.astype(bf16), 1)
        down_got = lay.along_z(down.astype(bf16), -1)
        up = block(n // 2 - 1 - step).astype(f32) + up_got.astype(f32)
        down = block(low + step).astype(f32) + down_got.astype(f32)
    return up + down - block(0).astype(f32)


def params(**kw):
    return pltpu.CompilerParams(vmem_limit_bytes=56 * 1024 * 1024, **kw)


def cost(flops, bytes_accessed, transcendentals=0):
    return pl.CostEstimate(
        flops=int(flops), bytes_accessed=int(bytes_accessed), transcendentals=int(transcendentals)
    )


def whole(array):
    rank = len(array.shape)
    return pl.BlockSpec(array.shape, lambda *_: (0,) * rank)


def listed(refs):
    return [(ref, k) for ref in refs for k in range(ref.shape[0])]


def column(offs, n, width):
    return pl.ds(pl.multiple_of(offs[n] * width, width), width)


def turn(value, keep, ahead, behind):
    half = ROTARY // 2
    parts = []
    for chunk in range(value.shape[1] // LANES):
        v = value[:, chunk * LANES : (chunk + 1) * LANES]
        parts.append(
            v * keep
            + pltpu.roll(v, LANES - half, 1) * ahead
            + pltpu.roll(v, half, 1) * behind
        )
    return parts[0] if len(parts) == 1 else jnp.concatenate(parts, axis=1)


def project(lay, offs, rows, gain, shift, bias, tables, pieces):
    T, D = rows.shape
    H = bias.shape[1] // 3
    BD = D // lay.fs
    blocks = 2 * lay.A * lay.B

    def kernel(offs, rows_ref, gain_ref, shift_ref, bias_ref, tab_ref, p0, p1, q0, q1, normed_ref, q_ref, kv_ref):
        x = rows_ref[...].astype(f32)
        mean = jnp.sum(x, axis=1, keepdims=True) * (1.0 / D)
        x = x - mean
        var = jnp.sum(x * x, axis=1, keepdims=True) * (1.0 / D)
        normed = x * lax.rsqrt(var + EPSILON) * gain_ref[...] + shift_ref[...]
        normed_ref[...] = normed.astype(bf16)
        weights = listed((p0, p1, q0, q1))
        keep, ahead, behind = tab_ref[0], tab_ref[1], tab_ref[2]
        for s in range(3):
            total = bias_ref[:, s * H : (s + 1) * H]
            for n, (ref, k) in enumerate(weights):
                total = total + dot(normed_ref[:, column(offs, n, BD)], ref[k, s * BD : (s + 1) * BD, :])
            if s == 0:
                q_ref[...] = (turn(total, keep, ahead, behind).astype(bf16) * (HEAD_DIM**-0.5)).astype(bf16)
            elif s == 1:
                kv_ref[0] = turn(total, keep, ahead, behind).astype(bf16)
            else:
                kv_ref[1] = total.astype(bf16)

    R = QROWS
    return pl.pallas_call(
        kernel,
        out_shape=(
            jax.ShapeDtypeStruct((T, D), bf16),
            jax.ShapeDtypeStruct((T, H), bf16),
            jax.ShapeDtypeStruct((2, T, H), bf16),
        ),
        grid_spec=pltpu.PrefetchScalarGridSpec(
            num_scalar_prefetch=1,
            grid=(T // R,),
            in_specs=[
                pl.BlockSpec((R, D), lambda t, o: (t, 0)),
                whole(gain),
                whole(shift),
                whole(bias),
                pl.BlockSpec((3, R, LANES), lambda t, o: (0, t, 0)),
            ]
            + [whole(p) for p in pieces],
            out_specs=[
                pl.BlockSpec((R, D), lambda t, o: (t, 0)),
                pl.BlockSpec((R, H), lambda t, o: (t, 0)),
                pl.BlockSpec((2, R, H), lambda t, o: (0, t, 0)),
            ],
        ),
        compiler_params=params(),
        cost_estimate=cost(2 * T * D * 3 * H, 2 * T * D * 2 + 8 * T * H + 2 * D * 4 * H),
        name="project",
    )(offs, rows, gain, shift, bias, tables, *pieces)


def attention(lay, offs, queries, kv_own, kv_prev, cot, pieces, paths, codes, tables):
    T, H = queries.shape
    D = cot.shape[1]
    BD = D // lay.fs
    QB = T // QROWS
    SPAN = T + QROWS
    KB = SPAN // KROWS
    pairs = H // LANES
    scaling = HEAD_DIM**-0.5

    def kernel(
        offs, q_ref, own_ref, prev_ref, cot_ref, path_ref, code_ref, tab_ref, p0, p1, q0, q1,
        att_ref, dq_ref, dprev_ref, down_ref,
        k_sc, v_sc, kt_sc, vt_sc, dk_sc, dv_sc, bias_sc, e_sc, g_sc, p_sc, d_sc,
    ):
        pair = pl.program_id(0)
        i = pl.program_id(1)

        @pl.when(i == 0)
        def _():
            k_sc[:T] = prev_ref[0]
            k_sc[T:] = own_ref[0]
            v_sc[:T] = prev_ref[1]
            v_sc[T:] = own_ref[1]
            for c in range(2 * T // KROWS):
                rows = slice(c * KROWS, (c + 1) * KROWS)
                kt_sc[:, rows] = k_sc[rows].astype(f32).T.astype(bf16)
                vt_sc[:, rows] = v_sc[rows].astype(f32).T.astype(bf16)
            dk_sc[...] = jnp.zeros_like(dk_sc)
            dv_sc[...] = jnp.zeros_like(dv_sc)

        base = pl.multiple_of(i * QROWS, QROWS)
        head_rows = pl.ds(pl.multiple_of(pair * LANES, LANES), LANES)
        grad = jnp.zeros((QROWS, LANES), f32)
        for n, (ref, k) in enumerate(listed((p0, p1, q0, q1))):
            rows = pl.ds(pl.multiple_of(3 * BD + pair * LANES, LANES), LANES)
            grad = grad + dot(cot_ref[:, column(offs, n, BD)], ref[k, rows, :], NT)
        grad = grad.astype(bf16)
        queries_pair = q_ref[...]

        key_at = lax.broadcasted_iota(jnp.int32, (KROWS, QROWS), 0)
        query_at = lax.broadcasted_iota(jnp.int32, (KROWS, QROWS), 1) + T
        path0, path1, path2 = path_ref[0:1, :], path_ref[1:2, :], path_ref[2:3, :]
        for c in range(KB):
            start = pl.multiple_of(base + c * KROWS, KROWS)
            code = code_ref[pl.ds(start, KROWS), :]
            code = jnp.concatenate([code, code], axis=1)
            at = key_at + c * KROWS
            linked = (code == path0) | (code == path1) | (code == path2)
            seen = (linked & (at <= query_at)) | (at == query_at)
            bias_sc[c] = jnp.where(seen, 0.0, MASKED)

        lane = lax.broadcasted_iota(jnp.int32, (QROWS, LANES), 1)
        att_t, dq_t = [], []
        for head in range(2):
            mine = (lane >= head * HEAD_DIM) & (lane < (head + 1) * HEAD_DIM)
            qh = jnp.where(mine, queries_pair, jnp.zeros_like(queries_pair))
            gh = jnp.where(mine, grad, jnp.zeros_like(grad))
            top = jnp.full((1, QROWS), MASKED, f32)
            for c in range(KB):
                start = pl.multiple_of(base + c * KROWS, KROWS)
                s = dot(k_sc[pl.ds(start, KROWS), :], qh, NT) + bias_sc[c]
                e_sc[c] = s
                top = jnp.maximum(top, jnp.max(s, axis=0, keepdims=True))
            summed = jnp.zeros((1, QROWS), f32)
            mixed = jnp.zeros((1, QROWS), f32)
            for c in range(KB):
                start = pl.multiple_of(base + c * KROWS, KROWS)
                e = jnp.exp(e_sc[c] - top)
                g = dot(v_sc[pl.ds(start, KROWS), :], gh, NT)
                e_sc[c] = e
                g_sc[c] = g
                summed = summed + jnp.sum(e, axis=0, keepdims=True)
                mixed = mixed + jnp.sum(e * g, axis=0, keepdims=True)
            inverse = 1.0 / summed
            mixed = mixed * inverse
            for c in range(KB):
                probs = e_sc[c] * inverse
                p_sc[c * KROWS : (c + 1) * KROWS] = probs.astype(bf16)
                d_sc[c * KROWS : (c + 1) * KROWS] = (probs * (g_sc[c] - mixed)).astype(bf16)
            span = pl.ds(base, SPAN)
            hrow = slice(head * HEAD_DIM, (head + 1) * HEAD_DIM)
            att_t.append(dot(vt_sc[hrow, span], p_sc[...]))
            dq_t.append(dot(kt_sc[hrow, span], d_sc[...]))
            dv_sc[span, :] += dot(p_sc[...], gh)
            dk_sc[span, :] += dot(d_sc[...], qh)
        att_ref[...] = jnp.concatenate(att_t, axis=0).T.astype(bf16)
        dq = jnp.concatenate(dq_t, axis=0).T * scaling
        dq_ref[...] = turn(dq, tab_ref[0], -tab_ref[1], -tab_ref[2]).astype(bf16)

        @pl.when(i == QB - 1)
        def _():
            dprev_ref[0] = dk_sc[:T].astype(bf16)
            dprev_ref[1] = dv_sc[:T].astype(bf16)
            down_ref[0] = dk_sc[T:]
            down_ref[1] = dv_sc[T:]

    elements = (H // HEAD_DIM) * T * SPAN
    return pl.pallas_call(
        kernel,
        out_shape=(
            jax.ShapeDtypeStruct((T, H), bf16),
            jax.ShapeDtypeStruct((T, H), bf16),
            jax.ShapeDtypeStruct((2, T, H), bf16),
            jax.ShapeDtypeStruct((2, T, H), f32),
        ),
        grid_spec=pltpu.PrefetchScalarGridSpec(
            num_scalar_prefetch=1,
            grid=(pairs, QB),
            in_specs=[
                pl.BlockSpec((QROWS, LANES), lambda p, i, o: (i, p)),
                pl.BlockSpec((2, T, LANES), lambda p, i, o: (0, 0, p)),
                pl.BlockSpec((2, T, LANES), lambda p, i, o: (0, 0, p)),
                pl.BlockSpec((QROWS, D), lambda p, i, o: (i, 0)),
                pl.BlockSpec((8, QROWS), lambda p, i, o: (0, i)),
                whole(codes),
                pl.BlockSpec((3, QROWS, LANES), lambda p, i, o: (0, i, 0)),
            ]
            + [whole(p) for p in pieces],
            out_specs=[
                pl.BlockSpec((QROWS, LANES), lambda p, i, o: (i, p)),
                pl.BlockSpec((QROWS, LANES), lambda p, i, o: (i, p)),
                pl.BlockSpec((2, T, LANES), lambda p, i, o: (0, 0, p)),
                pl.BlockSpec((2, T, LANES), lambda p, i, o: (0, 0, p)),
            ],
            scratch_shapes=[
                pltpu.VMEM((2 * T, LANES), bf16),
                pltpu.VMEM((2 * T, LANES), bf16),
                pltpu.VMEM((LANES, 2 * T), bf16),
                pltpu.VMEM((LANES, 2 * T), bf16),
                pltpu.VMEM((2 * T, LANES), f32),
                pltpu.VMEM((2 * T, LANES), f32),
                pltpu.VMEM((KB, KROWS, QROWS), f32),
                pltpu.VMEM((KB, KROWS, QROWS), f32),
                pltpu.VMEM((KB, KROWS, QROWS), f32),
                pltpu.VMEM((SPAN, QROWS), bf16),
                pltpu.VMEM((SPAN, QROWS), bf16),
            ],
        ),
        compiler_params=params(),
        cost_estimate=cost(elements * 64 * 12 * 4, 2 * T * D + 20 * T * H, elements),
        name="attention",
    )(offs, queries, kv_own, kv_prev, cot, paths, codes, tables, *pieces)


def inner_forward(lay, offs, normed, bias, pieces):
    T, D = normed.shape
    F = bias.shape[1]
    BD = D // lay.fs
    R = QROWS

    def kernel(offs, x_ref, bias_ref, p0, p1, q0, q1, act_ref, slope_ref):
        u = bias_ref[...]
        for n, (ref, k) in enumerate(listed((p0, p1, q0, q1))):
            u = u + dot(x_ref[:, column(offs, n, BD)], ref[k])
        scale = (2.0 / jnp.pi) ** 0.5
        square = u * u
        t = jnp.tanh(scale * (u + 0.044715 * (square * u)))
        act_ref[...] = (0.5 * u * (1.0 + t)).astype(bf16)
        slope = 0.5 * (1.0 + t) + 0.5 * u * (1.0 - t * t) * (scale * (1.0 + (3 * 0.044715) * square))
        slope_ref[...] = slope

    return pl.pallas_call(
        kernel,
        out_shape=(jax.ShapeDtypeStruct((T, F), bf16), jax.ShapeDtypeStruct((T, F), f32)),
        grid_spec=pltpu.PrefetchScalarGridSpec(
            num_scalar_prefetch=1,
            grid=(T // R,),
            in_specs=[pl.BlockSpec((R, D), lambda t, o: (t, 0)), whole(bias)] + [whole(p) for p in pieces],
            out_specs=[
                pl.BlockSpec((R, F), lambda t, o: (t, 0)),
                pl.BlockSpec((R, F), lambda t, o: (t, 0)),
            ],
        ),
        compiler_params=params(),
        cost_estimate=cost(2 * T * D * F, 2 * T * D + 2 * D * F + 6 * T * F, T * F),
        name="inner_forward",
    )(offs, normed, bias, *pieces)


def inner_backward(lay, offs, cot, slope, pieces):
    T, D = cot.shape
    F = slope.shape[1]
    BD = D // lay.fs
    R = QROWS

    def kernel(offs, c_ref, slope_ref, p0, p1, q0, q1, grad_ref, bias_ref):
        total = jnp.zeros((R, F), f32)
        for n, (ref, k) in enumerate(listed((p0, p1, q0, q1))):
            total = total + dot(c_ref[:, column(offs, n, BD)], ref[k], NT)
        grad = (total * slope_ref[...]).astype(bf16)
        grad_ref[...] = grad

        @pl.when(pl.program_id(0) == 0)
        def _():
            bias_ref[...] = jnp.zeros_like(bias_ref)

        bias_ref[...] += jnp.sum(grad.astype(f32), axis=0, keepdims=True)

    return pl.pallas_call(
        kernel,
        out_shape=(jax.ShapeDtypeStruct((T, F), bf16), jax.ShapeDtypeStruct((1, F), f32)),
        grid_spec=pltpu.PrefetchScalarGridSpec(
            num_scalar_prefetch=1,
            grid=(T // R,),
            in_specs=[
                pl.BlockSpec((R, D), lambda t, o: (t, 0)),
                pl.BlockSpec((R, F), lambda t, o: (t, 0)),
            ]
            + [whole(p) for p in pieces],
            out_specs=[
                pl.BlockSpec((R, F), lambda t, o: (t, 0)),
                pl.BlockSpec((1, F), lambda t, o: (0, 0)),
            ],
        ),
        compiler_params=params(),
        cost_estimate=cost(2 * T * D * F, 2 * T * D + 2 * D * F + 6 * T * F),
        name="inner_backward",
    )(offs, cot, slope, *pieces)


def block_grads(lay, offs, wide, narrow, picks, wide_first, name):
    T, D = wide.shape
    F = narrow.shape[1]
    BD = D // lay.fs
    shape = (BD, F) if wide_first else (F, BD)

    def kernel(offs, wide_ref, narrow_ref, *rest):
        outs = rest[: len(picks)]
        held = rest[len(picks)] if len(rest) > len(picks) else None
        if held is not None:
            held[...] = narrow_ref[...].T
        for ref, chosen in zip(outs, picks):
            for k, n in enumerate(chosen):
                block = wide_ref[:, column(offs, n, BD)]
                if wide_first:
                    ref[k] = dot(block.T, narrow_ref[...]).astype(bf16)
                else:
                    ref[k] = dot(held[...], block).astype(bf16)

    count = sum(len(chosen) for chosen in picks)
    return pl.pallas_call(
        kernel,
        out_shape=tuple(jax.ShapeDtypeStruct((len(chosen),) + shape, bf16) for chosen in picks),
        grid_spec=pltpu.PrefetchScalarGridSpec(
            num_scalar_prefetch=1,
            grid=(1,),
            in_specs=[whole(wide), whole(narrow)],
            out_specs=[
                pl.BlockSpec((len(chosen),) + shape, lambda t, o: (0, 0, 0)) for chosen in picks
            ],
            scratch_shapes=[] if wide_first else [pltpu.VMEM((F, T), bf16)],
        ),
        compiler_params=params(),
        cost_estimate=cost(2 * T * BD * F * count, 2 * T * D + 2 * T * F + 2 * BD * F * count),
        name=name,
    )(offs, wide, narrow)


def attn_weight_grads(lay, offs, normed, cot, dq, dkv, attended, picks, name):
    T, D = normed.shape
    H = dq.shape[1]
    BD = D // lay.fs

    def kernel(offs, x_ref, c_ref, dq_ref, dkv_ref, att_ref, *outs):
        att = att_ref[...].T
        for ref, chosen in zip(outs, picks):
            for k, n in enumerate(chosen):
                block = x_ref[:, column(offs, n, BD)].T
                ref[k, :BD] = dot(block, dq_ref[...]).astype(bf16)
                ref[k, BD : 2 * BD] = dot(block, dkv_ref[0]).astype(bf16)
                ref[k, 2 * BD : 3 * BD] = dot(block, dkv_ref[1]).astype(bf16)
                ref[k, 3 * BD :] = dot(att, c_ref[:, column(offs, n, BD)]).astype(bf16)

    count = sum(len(chosen) for chosen in picks)
    shape = (3 * BD + H, H)
    return pl.pallas_call(
        kernel,
        out_shape=tuple(jax.ShapeDtypeStruct((len(chosen),) + shape, bf16) for chosen in picks),
        grid_spec=pltpu.PrefetchScalarGridSpec(
            num_scalar_prefetch=1,
            grid=(1,),
            in_specs=[whole(v) for v in (normed, cot, dq, dkv, attended)],
            out_specs=[
                pl.BlockSpec((len(chosen),) + shape, lambda t, o: (0, 0, 0)) for chosen in picks
            ],
        ),
        compiler_params=params(),
        cost_estimate=cost(8 * T * BD * H * count, 4 * T * D + 8 * T * H + 8 * BD * H * count),
        name=name,
    )(offs, normed, cot, dq, dkv, attended)


def output_rows(lay, offs, attended, activated, attn_pieces, outer_pieces, D):
    T, F = activated.shape
    H = attended.shape[1]
    BD = D // lay.fs
    R = QROWS

    def kernel(offs, att_ref, act_ref, a0, a1, b0, b1, p0, p1, q0, q1, out_ref):
        small = listed((a0, a1, b0, b1))
        large = listed((p0, p1, q0, q1))
        for n in range(len(small)):
            (sref, sk), (lref, lk) = small[n], large[n]
            total = dot(act_ref[...], lref[lk]) + dot(att_ref[...], sref[sk, 3 * BD : 3 * BD + H, :])
            out_ref[:, column(offs, n, BD)] = total.astype(bf16)

    return pl.pallas_call(
        kernel,
        out_shape=jax.ShapeDtypeStruct((T, D), bf16),
        grid_spec=pltpu.PrefetchScalarGridSpec(
            num_scalar_prefetch=1,
            grid=(T // R,),
            in_specs=[
                pl.BlockSpec((R, H), lambda t, o: (t, 0)),
                pl.BlockSpec((R, F), lambda t, o: (t, 0)),
            ]
            + [whole(p) for p in attn_pieces]
            + [whole(p) for p in outer_pieces],
            out_specs=pl.BlockSpec((R, D), lambda t, o: (t, 0)),
        ),
        compiler_params=params(),
        cost_estimate=cost(2 * T * D * (F + H), 2 * T * (D + F + H) + 2 * D * (F + H)),
        name="output_rows",
    )(offs, attended, activated, *attn_pieces, *outer_pieces)


def normed_grads(lay, offs, pre_grad, dq, dkv, rows, attn_pieces, inner_pieces):
    T, D = rows.shape
    F = pre_grad.shape[1]
    H = dq.shape[1]
    BD = D // lay.fs
    R = QROWS

    def kernel(offs, pre_ref, dq_ref, dkv_ref, rows_ref, a0, a1, b0, b1, p0, p1, q0, q1, out_ref, sums_ref, stand_sc):
        @pl.when(pl.program_id(0) == 0)
        def _():
            sums_ref[...] = jnp.zeros_like(sums_ref)

        x = rows_ref[...].astype(f32)
        mean = jnp.sum(x, axis=1, keepdims=True) * (1.0 / D)
        x = x - mean
        var = jnp.sum(x * x, axis=1, keepdims=True) * (1.0 / D)
        stand_sc[...] = x * lax.rsqrt(var + EPSILON)
        small = listed((a0, a1, b0, b1))
        large = listed((p0, p1, q0, q1))
        for n in range(len(small)):
            (sref, sk), (lref, lk) = small[n], large[n]
            at = column(offs, n, BD)
            total = (
                dot(pre_ref[...], lref[lk], NT)
                + dot(dq_ref[...], sref[sk, :BD, :], NT)
                + dot(dkv_ref[0], sref[sk, BD : 2 * BD, :], NT)
                + dot(dkv_ref[1], sref[sk, 2 * BD : 3 * BD, :], NT)
            )
            out_ref[:, at] = total.astype(bf16)
            sums_ref[0:1, at] += jnp.sum(total * stand_sc[:, at], axis=0, keepdims=True)
            sums_ref[1:2, at] += jnp.sum(total, axis=0, keepdims=True)

    return pl.pallas_call(
        kernel,
        out_shape=(jax.ShapeDtypeStruct((T, D), bf16), jax.ShapeDtypeStruct((8, D), f32)),
        grid_spec=pltpu.PrefetchScalarGridSpec(
            num_scalar_prefetch=1,
            grid=(T // R,),
            in_specs=[
                pl.BlockSpec((R, F), lambda t, o: (t, 0)),
                pl.BlockSpec((R, H), lambda t, o: (t, 0)),
                pl.BlockSpec((2, R, H), lambda t, o: (0, t, 0)),
                pl.BlockSpec((R, D), lambda t, o: (t, 0)),
            ]
            + [whole(p) for p in attn_pieces]
            + [whole(p) for p in inner_pieces],
            out_specs=[
                pl.BlockSpec((R, D), lambda t, o: (t, 0)),
                pl.BlockSpec((8, D), lambda t, o: (0, 0)),
            ],
            scratch_shapes=[pltpu.VMEM((R, D), f32)],
        ),
        compiler_params=params(),
        cost_estimate=cost(2 * T * D * (F + 3 * H), 2 * T * (2 * D + F + 3 * H) + 2 * D * (F + 3 * H)),
        name="normed_grads",
    )(offs, pre_grad, dq, dkv, rows, *attn_pieces, *inner_pieces)


def key_value_grads(dkv_own, dkv_got, dq, tables):
    _, T, H = dkv_own.shape

    def kernel(own_ref, got_ref, dq_ref, tab_ref, out_ref, bias_ref):
        dk = own_ref[0] + got_ref[0].astype(f32)
        dv = own_ref[1] + got_ref[1].astype(f32)
        dk = turn(dk, tab_ref[0], -tab_ref[1], -tab_ref[2]).astype(bf16)
        dv = dv.astype(bf16)
        out_ref[0] = dk
        out_ref[1] = dv
        bias_ref[...] = jnp.zeros_like(bias_ref)
        bias_ref[0:1] = jnp.sum(dq_ref[...].astype(f32), axis=0, keepdims=True)
        bias_ref[1:2] = jnp.sum(dk.astype(f32), axis=0, keepdims=True)
        bias_ref[2:3] = jnp.sum(dv.astype(f32), axis=0, keepdims=True)

    return pl.pallas_call(
        kernel,
        out_shape=(jax.ShapeDtypeStruct((2, T, H), bf16), jax.ShapeDtypeStruct((8, H), f32)),
        compiler_params=params(),
        cost_estimate=cost(10 * T * H, 20 * T * H),
        name="key_value_grads",
    )(dkv_own, dkv_got, dq, tables)


def body(
    residual,
    norm_gain,
    norm_shift,
    qkv_weight,
    qkv_bias,
    dense_weight,
    dense_bias,
    inner_weight,
    inner_bias,
    outer_weight,
    outer_bias,
    cotangent,
    segment,
    ancestors,
    valid_slot,
):
    lay = Layout()
    fs, tp = lay.fs, lay.tp
    D = residual.shape[1]
    T = residual.shape[0] * tp * 2
    HC = qkv_weight.shape[2] // 2
    FC = inner_weight.shape[1] // 2
    BD = qkv_weight.shape[1]
    assert T >= TREE_LEN - 1 and BD == HC
    offs = lay.offsets()
    is0 = lay.is0

    half = (qkv_weight[:, :, :HC].reshape(3 * BD, HC), qkv_weight[:, :, HC:].reshape(3 * BD, HC))
    attn_half = (
        jnp.concatenate([half[0], dense_weight[:HC]]),
        jnp.concatenate([half[1], dense_weight[HC:]]),
    )
    inner_half = (inner_weight[:, :FC], inner_weight[:, FC:])
    outer_half = (outer_weight[:FC], outer_weight[FC:])

    def gathered(pair):
        keep, send = lay.by_core(*pair)
        first, second = lay.by_core(keep, lay.over_core(send))
        return gather_pieces(lay, first, second)

    attn_pieces = gathered(attn_half)
    inner_pieces = gathered(inner_half)
    outer_pieces = gathered(outer_half)

    def chip_rows(block):
        own = ring_gather(lay, block)
        first, second = lay.by_core(own, lay.over_core(own))
        return jnp.concatenate([first, second])

    rows = chip_rows(residual)
    cot = chip_rows(cotangent)

    flat = jnp.concatenate(
        [norm_gain, norm_shift, dense_bias, outer_bias, qkv_bias.reshape(-1), inner_bias]
    )
    vectors = small_gather(lay, flat.reshape(1, -1)).astype(f32)
    n_small = norm_gain.shape[0]
    gain = vectors[:, :n_small].reshape(1, D)
    shift = vectors[:, n_small : 2 * n_small].reshape(1, D)
    bias_sum = (vectors[:, 2 * n_small : 3 * n_small] + vectors[:, 3 * n_small : 4 * n_small]).reshape(1, D)
    mine = lax.dynamic_index_in_dim(vectors.reshape(fs, tp, -1), lay.z, axis=1, keepdims=False)
    n_qkv = qkv_bias.shape[1]
    mine = lax.dynamic_slice_in_dim(mine, lay.core * (fs // 2), fs // 2, axis=0)
    my_qkv_bias = (
        mine[:, 4 * n_small : 4 * n_small + 3 * n_qkv]
        .reshape(fs // 2, 3, n_qkv)
        .transpose(1, 0, 2)
        .reshape(1, 3 * HC)
    )
    my_inner_bias = mine[:, 4 * n_small + 3 * n_qkv :].reshape(1, FC)

    base_slot = lay.chip * T
    seg_front = jnp.concatenate([jnp.zeros((T,), jnp.int32), segment])
    valid_front = jnp.concatenate([jnp.zeros((T,), jnp.int32), valid_slot])
    window_seg = lax.dynamic_slice_in_dim(seg_front, base_slot, 2 * T)
    window_valid = lax.dynamic_slice_in_dim(valid_front, base_slot, 2 * T)
    codes = jnp.where(window_valid == 1, window_seg, -1)
    own_seg, own_valid = window_seg[T:], window_valid[T:]
    seg_ids = jnp.arange(ancestors.shape[0], dtype=jnp.int32)
    onehot = (own_seg[None, :] == seg_ids[:, None]).astype(jnp.int32)
    paths = jnp.sum(onehot[None, :, :] * ancestors.T[:, :, None], axis=1)
    paths = jnp.where(own_valid[None, :] == 1, paths, -2)
    key_at = jnp.arange(2 * T, dtype=jnp.int32)[:, None]
    query_at = T + jnp.arange(T, dtype=jnp.int32)[None, :]
    code_col = codes[:, None]
    linked = (code_col == paths[0:1]) | (code_col == paths[1:2]) | (code_col == paths[2:3])
    allowed = (linked & (key_at <= query_at)) | (key_at == query_at)
    positions = jnp.sum(allowed.astype(jnp.int32), axis=0) - 1
    paths8 = jnp.concatenate([paths, jnp.zeros((5, T), jnp.int32)])
    codes_wide = jnp.broadcast_to(code_col, (2 * T, LANES))

    half_rot = ROTARY // 2
    freq = 10000.0 ** (-(jnp.arange(half_rot, dtype=f32) * 2.0 / ROTARY))
    angle = positions.astype(f32)[:, None] * freq[None, :]
    cosine, sine = jnp.cos(angle), jnp.sin(angle)
    still = jnp.ones((T, HEAD_DIM - ROTARY), f32)
    none16 = jnp.zeros((T, half_rot), f32)
    none32 = jnp.zeros((T, HEAD_DIM - ROTARY), f32)
    twice = LANES // HEAD_DIM
    tables = jnp.stack(
        [
            jnp.concatenate([cosine, cosine, still] * twice, axis=1),
            jnp.concatenate([-sine, none16, none32] * twice, axis=1),
            jnp.concatenate([none16, sine, none32] * twice, axis=1),
        ]
    )

    normed, queries, kv_own = project(lay, offs, rows, gain, shift, my_qkv_bias, tables, attn_pieces)
    forward_pairs = [(s, s + 2) for s in range(fs - 2)]
    backward_pairs = [(s + 2, s) for s in range(fs - 2)]
    kv_prev = lax.ppermute(kv_own, "fsdp", forward_pairs)
    attended, dq, dkv_prev, dkv_own = attention(
        lay, offs, queries, kv_own, kv_prev, cot, attn_pieces, paths8, codes_wide, tables
    )
    dkv_got = lax.ppermute(dkv_prev, "fsdp", backward_pairs)

    A, B = lay.A, lay.B
    near = (tuple(range(B)), tuple(A * B + m for m in range(A)))
    far = (tuple(range(B, A * B)), tuple(A * B + m for m in range(A, A * B)))

    activated, slope = inner_forward(lay, offs, normed, my_inner_bias, inner_pieces)
    outer_far = block_grads(lay, offs, cot, activated, far, False, "outer_grads_far")
    outer_near = block_grads(lay, offs, cot, activated, near, False, "outer_grads_near")
    outer_sums = scatter_pieces(lay, outer_near, outer_far)

    pre_grad, inner_bias_part = inner_backward(lay, offs, cot, slope, outer_pieces)
    inner_far = block_grads(lay, offs, normed, pre_grad, far, True, "inner_grads_far")
    inner_near = block_grads(lay, offs, normed, pre_grad, near, True, "inner_grads_near")
    inner_sums = scatter_pieces(lay, inner_near, inner_far)

    dkv, qkv_bias_part = key_value_grads(dkv_own, dkv_got, dq, tables)
    attn_far = attn_weight_grads(lay, offs, normed, cot, dq, dkv, attended, far, "attn_grads_far")
    attn_near = attn_weight_grads(lay, offs, normed, cot, dq, dkv, attended, near, "attn_grads_near")
    attn_sums = scatter_pieces(lay, attn_near, attn_far)

    def swapped(sums):
        first, second = sums
        keep = jnp.where(is0, first, second)
        send = jnp.where(is0, second, first)
        return lay.by_core(keep, lay.over_core(send))

    low, high = swapped(outer_sums)
    outer_weight_grad = jnp.concatenate([low, high], axis=0)
    low, high = swapped(inner_sums)
    inner_weight_grad = jnp.concatenate([low, high], axis=1)
    low, high = swapped(attn_sums)
    qkv_weight_grad = jnp.concatenate(
        [low[: 3 * BD].reshape(3, BD, HC), high[: 3 * BD].reshape(3, BD, HC)], axis=2
    )
    dense_weight_grad = jnp.concatenate([low[3 * BD :], high[3 * BD :]], axis=0)

    def to_rows(partial):
        group = T // 2
        keep = jnp.where(is0, partial[:group], partial[group:])
        send = jnp.where(is0, partial[group:], partial[:group])
        summed = keep.astype(f32) + lay.over_core(send).astype(f32)
        return ring_scatter(lay, summed.astype(bf16))

    partial_out = output_rows(lay, offs, attended, activated, attn_pieces, outer_pieces, D)
    inputs_f = residual.astype(f32)
    output = (inputs_f + to_rows(partial_out) + bias_sum).astype(bf16)

    partial_grad, norm_sums = normed_grads(
        lay, offs, pre_grad, dq, dkv, rows, attn_pieces, inner_pieces
    )
    row_mean = jnp.mean(inputs_f, axis=-1, keepdims=True)
    centered = inputs_f - row_mean
    scale = lax.rsqrt(jnp.mean(centered * centered, axis=-1, keepdims=True) + EPSILON)
    stand = centered * scale
    cot_f = cotangent.astype(f32)
    e = to_rows(partial_grad) * gain
    e_mean = jnp.mean(e, axis=-1, keepdims=True)
    es_mean = jnp.mean(e * stand, axis=-1, keepdims=True)
    residual_grad = (cot_f + (e - e_mean - stand * es_mean) * scale).astype(bf16)

    out_bias_part = jnp.sum(cot_f, axis=0)
    wide = [v.reshape(fs, tp, n_small) for v in (norm_sums[0], norm_sums[1], out_bias_part)]
    heads = qkv_bias_part[:3].reshape(3, fs // 2, n_qkv).transpose(1, 0, 2).reshape(fs // 2, 3 * n_qkv)
    narrow = jnp.concatenate([heads, inner_bias_part.reshape(fs // 2, -1)], axis=1)
    blank = jnp.zeros_like(narrow)
    placed = jnp.concatenate([jnp.where(is0, narrow, blank), jnp.where(is0, blank, narrow)])
    mine_z = (jnp.arange(tp) == lay.z)[None, :, None]
    placed = jnp.where(mine_z, placed[:, None, :], 0.0)
    buffer = jnp.concatenate(wide + [placed], axis=2).reshape(fs * tp, -1)
    summed = small_scatter(lay, buffer)[0]
    gain_grad = summed[:n_small]
    shift_grad = summed[n_small : 2 * n_small]
    out_bias_grad = summed[2 * n_small : 3 * n_small]
    qkv_bias_grad = summed[3 * n_small : 3 * n_small + 3 * n_qkv].reshape(3, n_qkv)
    inner_bias_grad = summed[3 * n_small + 3 * n_qkv :]

    return (
        output,
        residual_grad,
        gain_grad,
        shift_grad,
        qkv_weight_grad,
        qkv_bias_grad,
        dense_weight_grad,
        out_bias_grad,
        inner_weight_grad,
        inner_bias_grad,
        outer_weight_grad,
        out_bias_grad,
    )


def solution(mesh):
    return jax.shard_map(
        body,
        mesh=mesh,
        in_specs=(
            P(("fsdp", "tp"), None),
            P(("fsdp", "tp")),
            P(("fsdp", "tp")),
            P(None, "fsdp", "tp"),
            P(None, ("tp", "fsdp")),
            P("tp", "fsdp"),
            P(("fsdp", "tp")),
            P("fsdp", "tp"),
            P(("tp", "fsdp")),
            P("tp", "fsdp"),
            P(("fsdp", "tp")),
            P(("fsdp", "tp"), None),
            P(),
            P(),
            P(),
        ),
        out_specs=(
            P(("fsdp", "tp"), None),
            P(("fsdp", "tp"), None),
            P(("fsdp", "tp")),
            P(("fsdp", "tp")),
            P(None, "fsdp", "tp"),
            P(None, ("tp", "fsdp")),
            P("tp", "fsdp"),
            P(("fsdp", "tp")),
            P("fsdp", "tp"),
            P(("tp", "fsdp")),
            P("tp", "fsdp"),
            P(("fsdp", "tp")),
        ),
        check_vma=False,
    )
```

```python
import jax
import jax.numpy as jnp
from jax import lax
from jax.experimental import pallas as pl
from jax.experimental.pallas import tpu as pltpu
from jax.sharding import PartitionSpec as P

HEAD_DIM = 64
ROTARY = 32
TREE_LEN = 1024
EPSILON = 1e-05
LANES = 128
QROWS = 256
KROWS = 256
MASKED = -1e30
SHARE = 1.0
SCOPED = 14 * 1024 * 1024

f32 = jnp.float32
bf16 = jnp.bfloat16

NN = (((1,), (0,)), ((), ()))
NT = (((1,), (1,)), ((), ()))
TN = (((0,), (0,)), ((), ()))


def dot(left, right, dims=NN):
    return lax.dot_general(left, right, dims, preferred_element_type=f32)


class Layout:
    def __init__(self):
        self.A, self.B, self.tp = (lax.axis_size(n) for n in ("a", "b", "z"))
        self.fs = self.A * self.B * 2
        self.a, self.b, self.core, self.z = (lax.axis_index(n) for n in ("a", "b", "c", "z"))
        self.chip = self.a * self.B + self.b
        self.is0 = self.core == 0

    def blocks(self):
        A, B = self.A, self.B
        first = [(0, i, j) for i in range(A) for j in range(B)]
        second = [(1, i, j) for j in range(B) for i in range(A)]
        return first + second

    def table(self):
        A, B = self.A, self.B
        device = []
        for core, i, j in self.blocks():
            chip = ((self.a + i) % A) * B + (self.b + j) % B
            device.append(chip * 2 + core)
        block = []
        for chip in range(A * B):
            i = (chip // B + A - self.a) % A
            j = (chip % B + B - self.b) % B
            block.append(i * B + j)
            block.append(A * B + j * A + i)
        return jnp.stack(device + block + [self.core, self.z]).astype(jnp.int32)

    def over(self, value, axis, steps):
        n = lax.axis_size(axis)
        return lax.ppermute(value, axis, [(s, (s + steps) % n) for s in range(n)])

    def over_core(self, value):
        return self.over(value, "c", 1)

    def along_a(self, value, steps):
        return self.over(value, "a", steps)

    def along_b(self, value, steps):
        return self.over(value, "b", steps)

    def along_z(self, value, steps):
        return self.over(value, "z", steps)

    def to_chip(self, value, steps):
        pairs = [(s, s + steps) for s in range(self.A * self.B) if 0 <= s + steps < self.A * self.B]
        return lax.ppermute(value, ("a", "b"), pairs)

    def with_partner(self, value, axis, bit):
        return lax.ppermute(value, axis, [(s, s ^ bit) for s in range(lax.axis_size(axis))])

    def by_core(self, own, other):
        return jnp.where(self.is0, own, other), jnp.where(self.is0, other, own)


def tie(value, *others):
    return lax.optimization_barrier((value,) + others)[0]


def gather_near(lay, first, second):
    p_row = [first] + [lay.along_b(first, -j) for j in range(1, lay.B)]
    q_row = [second] + [lay.along_a(second, -i) for i in range(1, lay.A)]
    return stack_blocks(p_row, q_row)


def gather_far(lay, p_row, q_row):
    p_far = [lay.along_a(p_row, -i) for i in range(1, lay.A)]
    q_far = [lay.along_b(q_row, -j) for j in range(1, lay.B)]
    p_far = p_far[0] if lay.A == 2 else jnp.concatenate(p_far)
    q_far = q_far[0] if lay.B == 2 else jnp.concatenate(q_far)
    return (p_row, p_far, q_row, q_far)


def scatter_far(lay, near, far):
    A, B = lay.A, lay.B
    p_far, q_far = far
    p_got = [lay.along_a(p_far[(i - 1) * B : i * B], i) for i in range(1, A)]
    q_got = [lay.along_b(q_far[(j - 1) * A : j * A], j) for j in range(1, B)]
    return add_blocks(near, p_got, q_got)


def scatter_near(lay, where, p_sums, q_sums):
    p_got = [lay.along_b(p_sums[j], j) for j in range(1, lay.B)]
    q_got = [lay.along_a(q_sums[i], i) for i in range(1, lay.A)]
    keep, send = last_sums(where, p_sums[0], q_sums[0], p_got, q_got, lay.fs)
    return keep, lay.over_core(send)


def small_gather(lay, rows):
    held = rows
    bit = 1
    while bit < lay.tp:
        upper = (lay.z // bit) % 2 == 1
        got = lay.with_partner(held, "z", bit)
        held = jnp.concatenate([jnp.where(upper, got, held), jnp.where(upper, held, got)])
        bit *= 2
    return held


def small_scatter(lay, rows):
    held = rows
    bit = lay.tp // 2
    while bit:
        upper = (lay.z // bit) % 2 == 1
        low, high = jnp.split(held, 2)
        got = lay.with_partner(jnp.where(upper, low, high), "z", bit)
        held = jnp.where(upper, high, low) + got
        bit //= 2
    return held


def ring_second(lay, where, turned, first):
    n = lay.tp
    up, down = ring_next(lay, turned, first)
    for step in range(1, n // 2):
        up_got, down_got = lay.along_z(up, 1), lay.along_z(down, -1)
        if step == n // 2 - 1:
            return up_got, down_got
        up = (ring_block(lay, turned, n // 2 - 1 - step).astype(f32) + up_got.astype(f32)).astype(bf16)
        down = (ring_block(lay, turned, n // 2 + 1 + step).astype(f32) + down_got.astype(f32)).astype(bf16)


def ring_block(lay, turned, m):
    size = turned.shape[0] // lay.tp
    first = (m % lay.tp) * size
    return turned[first : first + size]


def ring_start(lay, turned):
    far = ring_block(lay, turned, lay.tp // 2)
    half = far.shape[0] // 2
    return lay.along_z(far[:half], 1), lay.along_z(far[half:], -1)


def params(limit=SCOPED):
    return pltpu.CompilerParams(vmem_limit_bytes=limit)


def cost(flops, bytes_accessed, transcendentals=0):
    return pl.CostEstimate(
        flops=int(flops / SHARE),
        bytes_accessed=int(bytes_accessed / SHARE),
        transcendentals=int(transcendentals / SHARE),
    )


VMEM = pl.BlockSpec(memory_space=pltpu.VMEM)
SMEM = pl.BlockSpec(memory_space=pltpu.SMEM)


def array(shape, dtype):
    return jax.ShapeDtypeStruct(shape, dtype)


def listed(refs):
    return [(ref, k) for ref in refs for k in range(ref.shape[0])]


def aligned(value, size):
    return pl.multiple_of(value, size)


def column(where, n, width):
    return pl.ds(aligned(where[n] * width, width), width)


def stacked(refs, first, size, axis=0):
    return jnp.concatenate([ref[k, first : first + size, :] for ref, k in listed(refs)], axis=axis)


def turn(value, keep, ahead, behind):
    half = ROTARY // 2
    parts = []
    for chunk in range(value.shape[1] // LANES):
        v = value[:, chunk * LANES : (chunk + 1) * LANES]
        parts.append(
            v * keep
            + pltpu.roll(v, LANES - half, 1) * ahead
            + pltpu.roll(v, half, 1) * behind
        )
    return parts[0] if len(parts) == 1 else jnp.concatenate(parts, axis=1)


NORM_ROWS = 32
EXTRA = 16


def on_chip(kernel, outs, ins, name, estimate=None, scalars=0, scratch=(), grid=None, limit=SCOPED):
    more = {} if grid is None else {"grid": grid}
    return pl.pallas_call(
        kernel,
        out_shape=tuple(outs),
        in_specs=[SMEM] * scalars + [VMEM] * (len(ins) - scalars),
        out_specs=(VMEM,) * len(outs),
        scratch_shapes=list(scratch),
        compiler_params=params(limit),
        cost_estimate=estimate,
        name=name,
        **more,
    )(*ins)


def moved(values):
    return cost(0, 2 * sum(v.size * v.dtype.itemsize for v in values))


def stack_blocks(p_row, q_row):
    count = len(p_row)

    def kernel(*refs):
        ins, outs = refs[:-2], refs[-2:]
        for k, ref in enumerate(ins):
            if k < count:
                outs[0][k] = ref[...]
            else:
                outs[1][k - count] = ref[...]

    ins = list(p_row) + list(q_row)
    shape, dtype = ins[0].shape, ins[0].dtype
    outs = [array((count,) + shape, dtype), array((len(q_row),) + shape, dtype)]
    return on_chip(kernel, outs, ins, "stack_blocks", moved(ins))


def add_blocks(near, p_got, q_got):
    p_row, q_row = near
    counts = (p_row.shape[0], q_row.shape[0])
    ins = [p_row, q_row] + list(p_got) + list(q_got)

    def kernel(*refs):
        outs = refs[len(ins) :]
        groups = ((refs[0], refs[2 : 2 + len(p_got)]), (refs[1], refs[2 + len(p_got) : len(ins)]))
        at = 0
        for (own, got), count in zip(groups, counts):
            for k in range(count):
                total = own[k].astype(f32)
                for ref in got:
                    total = total + ref[k].astype(f32)
                outs[at][...] = total.astype(outs[at].dtype)
                at += 1

    shape = p_row.shape[1:]
    outs = [array(shape, bf16 if k else f32) for count in counts for k in range(count)]
    done = on_chip(kernel, outs, ins, "add_blocks", moved(ins))
    return list(done[: counts[0]]), list(done[counts[0] :])


def last_sums(where, p_own, q_own, p_got, q_got, fs):
    ins = [where, p_own, q_own] + list(p_got) + list(q_got)

    def kernel(where, p_ref, q_ref, *refs):
        keep, send = refs[-2:]
        p, q = p_ref[...], q_ref[...]
        for ref in refs[: len(p_got)]:
            p = p + ref[...].astype(f32)
        for ref in refs[len(p_got) : len(p_got) + len(q_got)]:
            q = q + ref[...].astype(f32)
        first = where[2 * fs] == 0
        keep[...] = jnp.where(first, p, q)
        send[...] = jnp.where(first, q, p).astype(bf16)

    shape = p_own.shape
    return on_chip(kernel, [array(shape, f32), array(shape, bf16)], ins, "last_sums", moved(ins[1:]), 1)


def ring_next(lay, turned, first):
    n = lay.tp
    size = turned.shape[0] // n
    half = size // 2
    D = turned.shape[1]
    above, below = (n // 2 - 1) * size, (n // 2 + 1) % n * size

    def kernel(turned_ref, up_ref, down_ref, up_out, down_out):
        up_out[:half] = (turned_ref[above : above + half].astype(f32) + up_ref[...].astype(f32)).astype(bf16)
        up_out[half:] = turned_ref[above + half : above + size]
        down_out[:half] = turned_ref[below : below + half]
        low = turned_ref[below + half : below + size].astype(f32) + down_ref[...].astype(f32)
        down_out[half:] = low.astype(bf16)

    outs = [array((size, D), bf16)] * 2
    return on_chip(kernel, outs, [turned, *first], "ring_next", cost(0, 8 * size * D))


def add_cores(keep, got):
    def kernel(keep_ref, got_ref, out_ref):
        out_ref[...] = (keep_ref[...].astype(f32) + got_ref[...].astype(f32)).astype(bf16)

    return on_chip(kernel, [array(keep.shape, bf16)], [keep, got], "add_cores", moved([keep, got]))[0]


def unstack(lay, where, gathered):
    devices, _, size, D = gathered.shape
    T = devices * size
    BD = D // lay.fs

    def kernel(where, row_ref, cot_in, rows_ref, cot_ref):
        at = pl.ds(aligned(pl.program_id(0) * size, size), size)
        rows_ref[at, :] = row_ref[0, 0]
        for n in range(lay.fs):
            cot_ref[at, n * BD : (n + 1) * BD] = cot_in[0, 0, :, column(where, n, BD)]

    return pl.pallas_call(
        kernel,
        out_shape=(array((T, D), bf16), array((T, D), bf16)),
        grid_spec=pltpu.PrefetchScalarGridSpec(
            num_scalar_prefetch=1,
            grid=(devices,),
            in_specs=[
                pl.BlockSpec((1, 1, size, D), lambda d, where: (d, 0, 0, 0)),
                pl.BlockSpec((1, 1, size, D), lambda d, where: (d, 1, 0, 0)),
            ],
            out_specs=(VMEM, VMEM),
        ),
        compiler_params=params(),
        name="unstack",
    )(where, gathered, gathered)


def unpack(lay, where, pieces, first):
    BD = pieces[0].shape[2]

    def kernel(where, p0, p1, q0, q1, out_ref):
        for n, (ref, k) in enumerate(listed((p0, p1, q0, q1))):
            out_ref[where[n]] = ref[k, first : first + EXTRA, :]

    return on_chip(kernel, [array((lay.fs, EXTRA, BD), bf16)], [where, *pieces], "unpack", None, 1)[0]


def project(lay, where, rows, gain, shift, bias, tables, pieces):
    T, D = rows.shape
    H = bias.shape[1] // 3
    BD = D // lay.fs

    def kernel(where, rows_ref, gain_ref, shift_ref, bias_ref, tab_ref, p0, p1, q0, q1, normed_ref, stat_ref, q_ref, kv_ref):
        def some_rows(r, carry):
            at = pl.ds(aligned(r * NORM_ROWS, NORM_ROWS), NORM_ROWS)
            x = rows_ref[at, :].astype(f32)
            mean = jnp.sum(x, axis=1, keepdims=True) * (1.0 / D)
            x = x - mean
            var = jnp.sum(x * x, axis=1, keepdims=True) * (1.0 / D)
            scale = lax.rsqrt(var + EPSILON)
            normed = (x * scale * gain_ref[...] + shift_ref[...]).astype(bf16)
            for n in range(lay.fs):
                block = where[lay.fs + n]
                normed_ref[at, pl.ds(aligned(block * BD, BD), BD)] = normed[:, n * BD : (n + 1) * BD]
            stat_ref[0, at, :] = jnp.broadcast_to(mean, (NORM_ROWS, LANES))
            stat_ref[1, at, :] = jnp.broadcast_to(scale, (NORM_ROWS, LANES))
            return carry

        lax.fori_loop(0, T // NORM_ROWS, some_rows, 0, unroll=4)
        keep, ahead, behind = tab_ref[0], tab_ref[1], tab_ref[2]
        for s in range(3):
            total = dot(normed_ref[...], stacked((p0, p1, q0, q1), s * BD, BD)) + bias_ref[:, s * H : (s + 1) * H]
            if s == 0:
                q_ref[...] = (turn(total, keep, ahead, behind).astype(bf16) * (HEAD_DIM**-0.5)).astype(bf16)
            elif s == 1:
                kv_ref[0] = turn(total, keep, ahead, behind).astype(bf16)
            else:
                kv_ref[1] = total.astype(bf16)

    outs = [array((T, D), bf16), array((2, T, LANES), f32), array((T, H), bf16), array((2, T, H), bf16)]
    estimate = cost(2 * T * D * 3 * H, 2 * T * D * 2 + 8 * T * H + 2 * D * 4 * H)
    ins = [where, rows, gain, shift, bias, tables, *pieces]
    return on_chip(kernel, outs, ins, "project", estimate, 1)


def attention(lay, queries, kv_own, kv_prev, cot, pieces, paths, codes, tables):
    T, H = queries.shape
    D = cot.shape[1]
    BD = D // lay.fs
    QB = T // QROWS
    SPAN = T + QROWS
    KB = SPAN // KROWS
    pairs = H // LANES
    scaling = HEAD_DIM**-0.5

    def kernel(
        q_ref, own_ref, prev_ref, cot_ref, path_ref, code_ref, tab_ref, p0, p1, q0, q1,
        att_ref, att_t_ref, dq_ref, dq_t_ref, dprev_ref, down_ref,
        k_sc, v_sc, kt_sc, vt_sc, dk_sc, dv_sc, bias_sc, e_sc, g_sc, p_sc, d_sc,
    ):
        pair = pl.program_id(0)
        i = pl.program_id(1)
        across = pl.ds(aligned(pair * LANES, LANES), LANES)

        @pl.when(i == 0)
        def _():
            k_sc[:T] = prev_ref[0, :, across]
            k_sc[T:] = own_ref[0, :, across]
            v_sc[:T] = prev_ref[1, :, across]
            v_sc[T:] = own_ref[1, :, across]
            for c in range(2 * T // KROWS):
                rows = slice(c * KROWS, (c + 1) * KROWS)
                kt_sc[:, rows] = k_sc[rows].T
                vt_sc[:, rows] = v_sc[rows].T
            dk_sc[...] = jnp.zeros_like(dk_sc)
            dv_sc[...] = jnp.zeros_like(dv_sc)

        base = pl.multiple_of(i * QROWS, QROWS)
        own_rows = pl.ds(base, QROWS)
        heads = pl.ds(aligned(3 * BD + pair * LANES, LANES), LANES)
        weight = jnp.concatenate([ref[k, heads, :] for ref, k in listed((p0, p1, q0, q1))], axis=1)
        grad = dot(cot_ref[own_rows, :], weight, NT).astype(bf16)
        queries_pair = q_ref[own_rows, across]

        key_at = lax.broadcasted_iota(jnp.int32, (KROWS, QROWS), 0)
        query_at = lax.broadcasted_iota(jnp.int32, (KROWS, QROWS), 1) + T
        path0, path1, path2 = path_ref[0:1, own_rows], path_ref[1:2, own_rows], path_ref[2:3, own_rows]
        for c in range(KB):
            start = pl.multiple_of(base + c * KROWS, KROWS)
            code = code_ref[pl.ds(start, KROWS), :]
            code = jnp.concatenate([code, code], axis=1)
            at = key_at + c * KROWS
            linked = (code == path0) | (code == path1) | (code == path2)
            seen = (linked & (at <= query_at)) | (at == query_at)
            bias_sc[c] = jnp.where(seen, 0.0, MASKED)

        lane = lax.broadcasted_iota(jnp.int32, (QROWS, LANES), 1)
        att_t, dq_t = [], []
        for head in range(2):
            mine = (lane >= head * HEAD_DIM) & (lane < (head + 1) * HEAD_DIM)
            qh = jnp.where(mine, queries_pair, jnp.zeros_like(queries_pair))
            gh = jnp.where(mine, grad, jnp.zeros_like(grad))
            top = jnp.full((1, QROWS), MASKED, f32)
            for c in range(KB):
                start = pl.multiple_of(base + c * KROWS, KROWS)
                s = dot(k_sc[pl.ds(start, KROWS), :], qh, NT) + bias_sc[c]
                e_sc[c] = s
                top = jnp.maximum(top, jnp.max(s, axis=0, keepdims=True))
            summed = jnp.zeros((1, QROWS), f32)
            mixed = jnp.zeros((1, QROWS), f32)
            for c in range(KB):
                start = pl.multiple_of(base + c * KROWS, KROWS)
                e = jnp.exp(e_sc[c] - top)
                g = dot(v_sc[pl.ds(start, KROWS), :], gh, NT)
                e_sc[c] = e
                g_sc[c] = g
                summed = summed + jnp.sum(e, axis=0, keepdims=True)
                mixed = mixed + jnp.sum(e * g, axis=0, keepdims=True)
            inverse = 1.0 / summed
            mixed = mixed * inverse
            for c in range(KB):
                probs = e_sc[c] * inverse
                p_sc[c * KROWS : (c + 1) * KROWS] = probs.astype(bf16)
                d_sc[c * KROWS : (c + 1) * KROWS] = (probs * (g_sc[c] - mixed)).astype(bf16)
            span = pl.ds(base, SPAN)
            hrow = slice(head * HEAD_DIM, (head + 1) * HEAD_DIM)
            att_t.append(dot(vt_sc[hrow, span], p_sc[...]))
            dq_t.append(dot(kt_sc[hrow, span], d_sc[...]))
            dv_sc[span, :] += dot(p_sc[...], gh)
            dk_sc[span, :] += dot(d_sc[...], qh)
        att = jnp.concatenate(att_t, axis=0)
        att_t_ref[across, own_rows] = att.astype(bf16)
        att_ref[own_rows, across] = att.T.astype(bf16)
        dq = jnp.concatenate(dq_t, axis=0).T * scaling
        dq = turn(dq, tab_ref[0, own_rows, :], -tab_ref[1, own_rows, :], -tab_ref[2, own_rows, :])
        dq_ref[own_rows, across] = dq.astype(bf16)
        dq_t_ref[across, own_rows] = dq.T.astype(bf16)

        @pl.when(i == QB - 1)
        def _():
            dprev_ref[0, :, across] = dk_sc[:T].astype(bf16)
            dprev_ref[1, :, across] = dv_sc[:T].astype(bf16)
            down_ref[0, :, across] = dk_sc[T:]
            down_ref[1, :, across] = dv_sc[T:]

    elements = (H // HEAD_DIM) * T * SPAN
    outs = [
        array((T, H), bf16),
        array((H, T), bf16),
        array((T, H), bf16),
        array((H, T), bf16),
        array((2, T, H), bf16),
        array((2, T, H), f32),
    ]
    scratch = [
        pltpu.VMEM((2 * T, LANES), bf16),
        pltpu.VMEM((2 * T, LANES), bf16),
        pltpu.VMEM((LANES, 2 * T), bf16),
        pltpu.VMEM((LANES, 2 * T), bf16),
        pltpu.VMEM((2 * T, LANES), f32),
        pltpu.VMEM((2 * T, LANES), f32),
        pltpu.VMEM((KB, KROWS, QROWS), f32),
        pltpu.VMEM((KB, KROWS, QROWS), f32),
        pltpu.VMEM((KB, KROWS, QROWS), f32),
        pltpu.VMEM((SPAN, QROWS), bf16),
        pltpu.VMEM((SPAN, QROWS), bf16),
    ]
    ins = [queries, kv_own, kv_prev, cot, paths, codes, tables, *pieces]
    estimate = cost(elements * 64 * 12 * 4, 2 * T * D + 20 * T * H, elements)
    return on_chip(kernel, outs, ins, "attention", estimate, 0, scratch, (pairs, QB), 18 * 1024 * 1024)


def inner_forward(lay, normed, bias, pieces):
    T, D = normed.shape
    F = bias.shape[1]
    BD = D // lay.fs

    def kernel(x_ref, bias_ref, p0, p1, q0, q1, act_ref, act_t_ref, slope_ref):
        scale = (2.0 / jnp.pi) ** 0.5
        for c in range(F // BD):
            at = slice(c * BD, (c + 1) * BD)
            weight = stacked((p0, p1, q0, q1), c * BD, BD)
            for r in range(T // KROWS):
                rows = slice(r * KROWS, (r + 1) * KROWS)
                u = dot(x_ref[rows, :], weight) + bias_ref[:, at]
                square = u * u
                t = jnp.tanh(scale * (u + 0.044715 * (square * u)))
                act = (0.5 * u * (1.0 + t)).astype(bf16)
                act_ref[rows, at] = act
                act_t_ref[at, rows] = act.T
                slope = 0.5 * (1.0 + t) + 0.5 * u * (1.0 - t * t) * (scale * (1.0 + (3 * 0.044715) * square))
                slope_ref[rows, at] = slope

    outs = [array((T, F), bf16), array((F, T), bf16), array((T, F), f32)]
    estimate = cost(2 * T * D * F, 2 * T * D + 2 * D * F + 8 * T * F, T * F)
    return on_chip(kernel, outs, [normed, bias, *pieces], "inner_forward", estimate)


def inner_backward(lay, cot, slope, pieces):
    T, D = cot.shape
    F = slope.shape[1]
    BD = D // lay.fs

    def kernel(c_ref, slope_ref, p0, p1, q0, q1, grad_ref, grad_t_ref, bias_ref):
        for c in range(F // BD):
            at = slice(c * BD, (c + 1) * BD)
            weight = stacked((p0, p1, q0, q1), c * BD, BD, axis=1)
            sums = jnp.zeros((1, BD), f32)
            for r in range(T // KROWS):
                rows = slice(r * KROWS, (r + 1) * KROWS)
                grad = (dot(c_ref[rows, :], weight, NT) * slope_ref[rows, at]).astype(bf16)
                grad_ref[rows, at] = grad
                grad_t_ref[at, rows] = grad.T
                sums = sums + jnp.sum(grad.astype(f32), axis=0, keepdims=True)
            bias_ref[:, at] = sums

    outs = [array((T, F), bf16), array((F, T), bf16), array((1, F), f32)]
    estimate = cost(2 * T * D * F, 2 * T * D + 2 * D * F + 8 * T * F)
    return on_chip(kernel, outs, [cot, slope, *pieces], "inner_backward", estimate)


def block_grads(lay, turned, wide, picks, name):
    F, T = turned.shape
    BD = wide.shape[1] // lay.fs

    def kernel(turned_ref, wide_ref, *outs):
        for ref, (first, count) in zip(outs, picks):
            for k in range(count):
                n = first + k
                ref[k] = dot(turned_ref[...], wide_ref[:, n * BD : (n + 1) * BD]).astype(bf16)

    total = sum(count for _, count in picks)
    outs = [array((count, F, BD), bf16) for _, count in picks]
    estimate = cost(2 * T * BD * F * total, 2 * T * BD * total + 2 * T * F + 2 * BD * F * total)
    return on_chip(kernel, outs, [turned, wide], name, estimate)


def attn_weight_grads(lay, where, normed, cot, dq_t, dkv_t, att_t, extra, picks, name):
    T, D = normed.shape
    H = dq_t.shape[0]
    BD = D // lay.fs

    def kernel(where, x_ref, c_ref, dq_ref, dkv_ref, att_ref, extra_ref, *outs):
        for ref, (first, count) in zip(outs, picks):
            for k in range(count):
                n = first + k
                at = slice(n * BD, (n + 1) * BD)
                ref[k, :H] = dot(dq_ref[...], x_ref[:, at]).astype(bf16)
                ref[k, H : 3 * H] = dot(dkv_ref[...], x_ref[:, at]).astype(bf16)
                ref[k, 3 * H : 4 * H] = dot(att_ref[...], c_ref[:, at]).astype(bf16)
                ref[k, 4 * H :] = extra_ref[where[n]]

    total = sum(count for _, count in picks)
    outs = [array((count, 4 * H + EXTRA, BD), bf16) for _, count in picks]
    estimate = cost(8 * T * BD * H * total, 4 * T * BD * total + 8 * T * H + 8 * BD * H * total)
    ins = [where, normed, cot, dq_t, dkv_t, att_t, extra]
    return on_chip(kernel, outs, ins, name, estimate, 1)


def output_rows(lay, where, attended, activated, attn_pieces, outer_pieces, D):
    T, F = activated.shape
    H = attended.shape[1]
    BD = D // lay.fs
    G = T // 2
    Z = G // lay.tp

    def kernel(where, att_ref, act_ref, a0, a1, b0, b1, p0, p1, q0, q1, keep_ref, send_ref):
        core, z = where[2 * lay.fs], where[2 * lay.fs + 1]
        small = listed((a0, a1, b0, b1))
        large = listed((p0, p1, q0, q1))
        for base, out_ref in ((core * G, keep_ref), ((1 - core) * G, send_ref)):
            rows = pl.ds(aligned(base, G), G)
            for n in range(lay.fs):
                (sref, sk), (lref, lk) = small[n], large[n]
                at = column(where, n, BD)
                total = dot(act_ref[rows, :], lref[lk]) + dot(att_ref[rows, :], sref[sk, 3 * BD : 3 * BD + H, :])
                low = total.astype(bf16)
                for r in range(lay.tp):
                    to = lax.rem(r + lay.tp - z, lay.tp)
                    out_ref[pl.ds(aligned(to * Z, Z), Z), at] = low[r * Z : (r + 1) * Z]

    outs = [array((G, D), bf16)] * 2
    estimate = cost(2 * T * D * (F + H), 2 * T * (D + F + H) + 2 * D * (F + H))
    ins = [where, attended, activated, *attn_pieces, *outer_pieces]
    return on_chip(kernel, outs, ins, "output_rows", estimate, 1)


def normed_grads(lay, where, pre_grad, dq, dkv, rows, stats, attn_pieces, inner_pieces):
    T, F = pre_grad.shape
    D = rows.shape[1]
    G = T // 2
    H = dq.shape[1]
    BD = D // lay.fs
    Z = G // lay.tp

    def kernel(where, pre_ref, dq_ref, dkv_ref, rows_ref, stat_ref, a0, a1, b0, b1, p0, p1, q0, q1, keep_ref, send_ref, sums_ref):
        sums_ref[...] = jnp.zeros_like(sums_ref)
        core, z = where[2 * lay.fs], where[2 * lay.fs + 1]
        small = listed((a0, a1, b0, b1))
        large = listed((p0, p1, q0, q1))
        for base, out_ref in ((core * G, keep_ref), ((1 - core) * G, send_ref)):
            rows = pl.ds(aligned(base, G), G)
            left = jnp.concatenate([dq_ref[rows, :], dkv_ref[0, rows, :], dkv_ref[1, rows, :]], axis=1)
            for n in range(lay.fs):
                (sref, sk), (lref, lk) = small[n], large[n]
                at = column(where, n, BD)
                weight = jnp.concatenate([lref[lk, c * BD : (c + 1) * BD, :] for c in range(F // BD)], axis=1)
                narrow = jnp.concatenate([sref[sk, s * BD : (s + 1) * BD, :] for s in range(3)], axis=1)
                total = dot(pre_ref[rows, :], weight, NT) + dot(left, narrow, NT)
                low = total.astype(bf16)
                for r in range(lay.tp):
                    to = lax.rem(r + lay.tp - z, lay.tp)
                    out_ref[pl.ds(aligned(to * Z, Z), Z), at] = low[r * Z : (r + 1) * Z]
                x = rows_ref[rows, at].astype(f32)
                stand = jnp.concatenate(
                    [
                        (x[:, c * LANES : (c + 1) * LANES] - stat_ref[0, rows, :]) * stat_ref[1, rows, :]
                        for c in range(BD // LANES)
                    ],
                    axis=1,
                )
                sums_ref[0:1, at] += jnp.sum(total * stand, axis=0, keepdims=True)
                sums_ref[1:2, at] += jnp.sum(total, axis=0, keepdims=True)

    outs = [array((G, D), bf16), array((G, D), bf16), array((8, D), f32)]
    estimate = cost(2 * T * D * (F + 3 * H), 2 * T * (2 * D + F + 3 * H) + 2 * D * (F + 3 * H))
    ins = [where, pre_grad, dq, dkv, rows, stats, *attn_pieces, *inner_pieces]
    return on_chip(kernel, outs, ins, "normed_grads", estimate, 1)


def key_value_grads(dkv_own, dkv_got, dq, tables):
    _, T, H = dkv_own.shape

    def kernel(own_ref, got_ref, dq_ref, tab_ref, out_ref, out_t_ref, bias_ref):
        dk = own_ref[0] + got_ref[0].astype(f32)
        dv = own_ref[1] + got_ref[1].astype(f32)
        dk = turn(dk, tab_ref[0], -tab_ref[1], -tab_ref[2]).astype(bf16)
        dv = dv.astype(bf16)
        out_ref[0] = dk
        out_ref[1] = dv
        out_t_ref[:H] = dk.T
        out_t_ref[H:] = dv.T
        bias_ref[...] = jnp.zeros_like(bias_ref)
        bias_ref[0:1] = jnp.sum(dq_ref[...].astype(f32), axis=0, keepdims=True)
        bias_ref[1:2] = jnp.sum(dk.astype(f32), axis=0, keepdims=True)
        bias_ref[2:3] = jnp.sum(dv.astype(f32), axis=0, keepdims=True)

    outs = [array((2, T, H), bf16), array((2 * H, T), bf16), array((8, H), f32)]
    return on_chip(kernel, outs, [dkv_own, dkv_got, dq, tables], "key_value_grads", cost(10 * T * H, 24 * T * H))


def body(
    residual,
    norm_gain,
    norm_shift,
    qkv_weight,
    qkv_bias,
    dense_weight,
    dense_bias,
    inner_weight,
    inner_bias,
    outer_weight,
    outer_bias,
    cotangent,
    segment,
    ancestors,
    valid_slot,
):
    lay = Layout()
    fs, tp = lay.fs, lay.tp
    D = residual.shape[1]
    T = residual.shape[0] * tp * 2
    HC = qkv_weight.shape[2] // 2
    FC = inner_weight.shape[1] // 2
    BD = qkv_weight.shape[1]
    assert T >= TREE_LEN - 1 and BD == HC
    where = lay.table()
    is0 = lay.is0

    def halves(group):
        keep, send = lay.by_core(*group)
        return lay.by_core(keep, lay.over_core(send))

    n_small, n_qkv, n_inner = norm_gain.shape[0], qkv_bias.shape[1], inner_bias.shape[0]
    strips = [inner_weight[:, c * BD : (c + 1) * BD] for c in range(2 * FC // BD)]
    count = len(strips) // 2
    inner_group = [jnp.concatenate(strips[:count]), jnp.concatenate(strips[count:])]
    outer_group = [outer_weight[:FC], outer_weight[FC:]]
    inner_first = halves(inner_group)
    inner_near = gather_near(lay, *inner_first)
    four = jnp.stack([norm_gain, norm_shift, dense_bias, outer_bias])
    four = small_gather(lay, four[None]).transpose(1, 0, 2).reshape(4, BD)
    biases = jnp.stack(
        [
            jnp.pad(qkv_bias.reshape(-1), (0, BD - 3 * n_qkv)),
            jnp.pad(inner_bias, (0, BD - n_inner)),
        ]
    )
    extra = jnp.concatenate([four, biases, jnp.zeros((EXTRA - 6, BD), bf16)])
    attn_group = [
        jnp.concatenate(
            [
                qkv_weight[:, :, c * HC : (c + 1) * HC].reshape(3 * BD, HC),
                dense_weight[c * HC : (c + 1) * HC],
                extra,
            ]
        )
        for c in range(2)
    ]

    together = lax.optimization_barrier
    gathered = lax.all_gather(jnp.stack([residual, cotangent]), ("c", "z"), axis=0)
    attn_first, inner_near = together((halves(attn_group), inner_near))
    attn_near = gather_near(lay, *attn_first)
    outer_first, attn_near, inner_near = together((halves(outer_group), attn_near, inner_near))
    attn_pieces, outer_near, inner_near = together(
        (gather_far(lay, *attn_near), gather_near(lay, *outer_first), inner_near)
    )
    inner_pieces = gather_far(lay, *inner_near)
    rows, cot = unstack(lay, where, gathered)

    vectors = unpack(lay, where, attn_pieces, 4 * HC).astype(f32)
    gain = vectors[:, 0].reshape(1, D)
    shift = vectors[:, 1].reshape(1, D)
    bias_sum = (vectors[:, 2] + vectors[:, 3]).reshape(1, D)
    mine = lax.dynamic_slice_in_dim(vectors[:, 4:6], lay.core * (fs // 2), fs // 2, axis=0)
    my_qkv_bias = (
        mine[:, 0, : 3 * n_qkv].reshape(fs // 2, 3, n_qkv).transpose(1, 0, 2).reshape(1, 3 * HC)
    )
    my_inner_bias = mine[:, 1, :n_inner].reshape(1, FC)

    base_slot = lay.chip * T
    seg_front = jnp.concatenate([jnp.zeros((T,), jnp.int32), segment])
    valid_front = jnp.concatenate([jnp.zeros((T,), jnp.int32), valid_slot])
    window_seg = lax.dynamic_slice_in_dim(seg_front, base_slot, 2 * T)
    window_valid = lax.dynamic_slice_in_dim(valid_front, base_slot, 2 * T)
    codes = jnp.where(window_valid == 1, window_seg, -1)
    own_seg, own_valid = window_seg[T:], window_valid[T:]
    seg_ids = jnp.arange(ancestors.shape[0], dtype=jnp.int32)
    onehot = (own_seg[None, :] == seg_ids[:, None]).astype(jnp.int32)
    paths = jnp.sum(onehot[None, :, :] * ancestors.T[:, :, None], axis=1)
    paths = jnp.where(own_valid[None, :] == 1, paths, -2)
    key_at = jnp.arange(2 * T, dtype=jnp.int32)[:, None]
    query_at = T + jnp.arange(T, dtype=jnp.int32)[None, :]
    code_col = codes[:, None]
    linked = (code_col == paths[0:1]) | (code_col == paths[1:2]) | (code_col == paths[2:3])
    allowed = (linked & (key_at <= query_at)) | (key_at == query_at)
    positions = jnp.sum(allowed.astype(jnp.int32), axis=0) - 1
    paths8 = jnp.concatenate([paths, jnp.zeros((5, T), jnp.int32)])
    codes_wide = jnp.broadcast_to(code_col, (2 * T, LANES))

    half_rot = ROTARY // 2
    freq = 10000.0 ** (-(jnp.arange(half_rot, dtype=f32) * 2.0 / ROTARY))
    angle = positions.astype(f32)[:, None] * freq[None, :]
    cosine, sine = jnp.cos(angle), jnp.sin(angle)
    still = jnp.ones((T, HEAD_DIM - ROTARY), f32)
    none16 = jnp.zeros((T, half_rot), f32)
    none32 = jnp.zeros((T, HEAD_DIM - ROTARY), f32)
    twice = LANES // HEAD_DIM
    tables = jnp.stack(
        [
            jnp.concatenate([cosine, cosine, still] * twice, axis=1),
            jnp.concatenate([-sine, none16, none32] * twice, axis=1),
            jnp.concatenate([none16, sine, none32] * twice, axis=1),
        ]
    )

    normed, stats, queries, kv_own = project(
        lay, where, rows, gain, shift, my_qkv_bias, tables, attn_pieces
    )
    kv_prev = lay.to_chip(kv_own, 1)
    inner_pieces, outer_near, queries = together((inner_pieces, outer_near, queries))
    outer_pieces = gather_far(lay, *outer_near)
    A, B = lay.A, lay.B
    near = ((0, B), (A * B, A))
    far = ((B, A * B - B), (A * B + A, A * B - A))

    activated, act_t, slope = inner_forward(lay, normed, my_inner_bias, inner_pieces)
    act_t, kv_prev = together((act_t, kv_prev))
    outer_far = block_grads(lay, act_t, cot, far, "outer_grads_far")
    outer_near = block_grads(lay, tie(act_t, *outer_far), cot, near, "outer_grads_near")
    queries = tie(queries, *outer_near)
    attended, att_t, dq, dq_t, dkv_prev, dkv_own = attention(
        lay, queries, kv_own, kv_prev, cot, attn_pieces, paths8, codes_wide, tables
    )
    dkv_got = lay.to_chip(dkv_prev, -1)
    outer_row = scatter_far(lay, outer_near, outer_far)

    slope, outer_row = together((slope, outer_row, dq))[:2]
    outer_sums = scatter_near(lay, where, *outer_row)
    pre_grad, pre_t, inner_bias_part = inner_backward(lay, cot, slope, outer_pieces)
    inner_far = block_grads(lay, pre_t, normed, far, "inner_grads_far")
    inner_near = block_grads(lay, tie(pre_t, *inner_far), normed, near, "inner_grads_near")
    inner_row = scatter_far(lay, inner_near, inner_far)
    activated = together((activated, inner_near))[0]

    keep_out, send_out = output_rows(lay, where, attended, activated, attn_pieces, outer_pieces, D)
    got_out = lay.over_core(send_out)
    dkv_own, dkv_got = together((dkv_own, dkv_got, keep_out))[:2]
    dkv, dkv_t, qkv_bias_part = key_value_grads(dkv_own, dkv_got, dq, tables)
    pre_grad, inner_row = together((pre_grad, inner_row, dkv))[:2]
    inner_sums = scatter_near(lay, where, *inner_row)
    out_both = add_cores(keep_out, got_out)
    out_first = ring_start(lay, out_both)
    keep_grad, send_grad, norm_sums = normed_grads(
        lay, where, pre_grad, dq, dkv, rows, stats, attn_pieces, inner_pieces
    )
    got_grad = lay.over_core(send_grad)

    cot_f = cotangent.astype(f32)
    wide = jnp.concatenate([norm_sums[:2], jnp.sum(cot_f, axis=0)[None]])
    wide = wide.reshape(3, fs, tp, n_small).transpose(2, 1, 0, 3)
    wide = small_scatter(lay, wide)[0]
    wide = jnp.pad(wide, ((0, 0), (0, 0), (0, BD - n_small)))
    heads = qkv_bias_part[:3].reshape(3, fs // 2, n_qkv).transpose(1, 0, 2).reshape(fs // 2, 1, 3 * n_qkv)
    heads = jnp.pad(heads, ((0, 0), (0, 0), (0, BD - 3 * n_qkv)))
    hidden = jnp.pad(inner_bias_part.reshape(fs // 2, 1, n_inner), ((0, 0), (0, 0), (0, BD - n_inner)))
    narrow = jnp.concatenate([heads, hidden], axis=1)
    blank = jnp.zeros_like(narrow)
    narrow = jnp.concatenate([jnp.where(is0, narrow, blank), jnp.where(is0, blank, narrow)])
    sums = jnp.concatenate([wide, narrow, jnp.zeros((fs, EXTRA - 5, BD), f32)], axis=1).astype(bf16)

    sums, out_first, outer_sums = together((sums, out_first, outer_sums))
    attn_far = attn_weight_grads(lay, where, normed, cot, dq_t, dkv_t, att_t, sums, far, "attn_grads_far")
    out_second = ring_second(lay, where, out_both, out_first)
    dkv_t, got_grad, inner_sums = together((dkv_t, got_grad, inner_sums, attn_far))[:3]
    attn_near = attn_weight_grads(lay, where, normed, cot, dq_t, dkv_t, att_t, sums, near, "attn_grads_near")
    grad_both = add_cores(keep_grad, got_grad)
    grad_both, out_second = together((grad_both, out_second))
    grad_first = ring_start(lay, grad_both)
    attn_row = scatter_far(lay, attn_near, attn_far)
    attn_row, grad_first = together((attn_row, grad_first))
    grad_second = ring_second(lay, where, grad_both, grad_first)
    attn_sums = scatter_near(lay, where, *attn_row)

    def in_core_order(sums):
        keep, got = sums
        return lay.by_core(keep, got.astype(f32))

    low, high = in_core_order(outer_sums)
    outer_weight_grad = jnp.concatenate([low, high], axis=0)
    low, high = in_core_order(inner_sums)
    inner_weight_grad = jnp.concatenate([low, high], axis=0).T
    low, high = in_core_order(attn_sums)
    small = (low + high)[4 * HC :]
    low, high = low[: 4 * HC], high[: 4 * HC]
    qkv_weight_grad = jnp.concatenate(
        [low[: 3 * HC].reshape(3, HC, BD), high[: 3 * HC].reshape(3, HC, BD)], axis=1
    ).transpose(0, 2, 1)
    dense_weight_grad = jnp.concatenate([low[3 * HC :], high[3 * HC :]], axis=0)

    def total_rows(turned, second):
        return ring_block(lay, turned, 0).astype(f32) + second[0].astype(f32) + second[1].astype(f32)

    inputs_f = residual.astype(f32)
    output = (inputs_f + total_rows(out_both, out_second) + bias_sum).astype(bf16)
    row_grad = total_rows(grad_both, grad_second)
    row_mean = jnp.mean(inputs_f, axis=-1, keepdims=True)
    centered = inputs_f - row_mean
    scale = lax.rsqrt(jnp.mean(centered * centered, axis=-1, keepdims=True) + EPSILON)
    stand = centered * scale
    e = row_grad * gain
    e_mean = jnp.mean(e, axis=-1, keepdims=True)
    es_mean = jnp.mean(e * stand, axis=-1, keepdims=True)
    residual_grad = (cot_f + (e - e_mean - stand * es_mean) * scale).astype(bf16)

    gain_grad, shift_grad, out_bias_grad = small[0, :n_small], small[1, :n_small], small[2, :n_small]
    qkv_bias_grad = small[3, : 3 * n_qkv].reshape(3, n_qkv)
    inner_bias_grad = small[4, :n_inner]

    return (
        output,
        residual_grad,
        gain_grad,
        shift_grad,
        qkv_weight_grad,
        qkv_bias_grad,
        dense_weight_grad,
        out_bias_grad,
        inner_weight_grad,
        inner_bias_grad,
        outer_weight_grad,
        out_bias_grad,
    )


def solution(mesh):
    fs, tp = mesh.devices.shape
    inside = jax.sharding.Mesh(mesh.devices.reshape(2, fs // 4, 2, tp), ("a", "b", "c", "z"))
    all_axes = ("a", "b", "c", "z")
    fsdp = ("a", "b", "c")
    crossed = ("z", "a", "b", "c")
    return jax.shard_map(
        body,
        mesh=inside,
        in_specs=(
            P(all_axes, None),
            P(all_axes),
            P(all_axes),
            P(None, fsdp, "z"),
            P(None, crossed),
            P("z", fsdp),
            P(all_axes),
            P(fsdp, "z"),
            P(crossed),
            P("z", fsdp),
            P(all_axes),
            P(all_axes, None),
            P(),
            P(),
            P(),
        ),
        out_specs=(
            P(all_axes, None),
            P(all_axes, None),
            P(all_axes),
            P(all_axes),
            P(None, fsdp, "z"),
            P(None, crossed),
            P("z", fsdp),
            P(all_axes),
            P(fsdp, "z"),
            P(crossed),
            P("z", fsdp),
            P(all_axes),
        ),
        check_vma=False,
    )
```

```python
import jax
import jax.numpy as jnp
from jax import lax
from jax.experimental import pallas as pl
from jax.experimental.pallas import tpu as pltpu
from jax.sharding import PartitionSpec as P

HEAD_DIM = 64
ROTARY = 32
TREE_LEN = 1024
EPSILON = 1e-05
LANES = 128
QROWS = 256
KROWS = 256
MASKED = -1e30
SHARE = 0.2
SCOPED = 14 * 1024 * 1024

f32 = jnp.float32
bf16 = jnp.bfloat16

NN = (((1,), (0,)), ((), ()))
NT = (((1,), (1,)), ((), ()))
TN = (((0,), (0,)), ((), ()))


def dot(left, right, dims=NN):
    return lax.dot_general(left, right, dims, preferred_element_type=f32)


class Layout:
    def __init__(self):
        self.A, self.B, self.tp = (lax.axis_size(n) for n in ("a", "b", "z"))
        self.fs = self.A * self.B * 2
        self.a, self.b, self.core, self.z = (lax.axis_index(n) for n in ("a", "b", "c", "z"))
        self.chip = self.a * self.B + self.b
        self.is0 = self.core == 0

    def blocks(self):
        A, B = self.A, self.B
        first = [(0, i, j) for i in range(A) for j in range(B)]
        second = [(1, i, j) for j in range(B) for i in range(A)]
        return first + second

    def table(self):
        A, B = self.A, self.B
        device = []
        for core, i, j in self.blocks():
            chip = ((self.a + i) % A) * B + (self.b + j) % B
            device.append(chip * 2 + core)
        block = []
        for chip in range(A * B):
            i = (chip // B + A - self.a) % A
            j = (chip % B + B - self.b) % B
            block.append(i * B + j)
            block.append(A * B + j * A + i)
        return jnp.stack(device + block + [self.core, self.z]).astype(jnp.int32)

    def over(self, value, axis, steps):
        n = lax.axis_size(axis)
        return lax.ppermute(value, axis, [(s, (s + steps) % n) for s in range(n)])

    def over_core(self, value):
        return self.over(value, "c", 1)

    def along_a(self, value, steps):
        return self.over(value, "a", steps)

    def along_b(self, value, steps):
        return self.over(value, "b", steps)

    def along_z(self, value, steps):
        return self.over(value, "z", steps)

    def to_chip(self, value, steps):
        pairs = [(s, s + steps) for s in range(self.A * self.B) if 0 <= s + steps < self.A * self.B]
        return lax.ppermute(value, ("a", "b"), pairs)

    def with_partner(self, value, axis, bit):
        return lax.ppermute(value, axis, [(s, s ^ bit) for s in range(lax.axis_size(axis))])

    def by_core(self, own, other):
        return jnp.where(self.is0, own, other), jnp.where(self.is0, other, own)


def tie(value, *others):
    return lax.optimization_barrier((value,) + others)[0]


def gather_near(lay, first, second):
    p_row = [first] + [lay.along_b(first, -j) for j in range(1, lay.B)]
    q_row = [second] + [lay.along_a(second, -i) for i in range(1, lay.A)]
    return stack_blocks(p_row, q_row)


def gather_far(lay, p_row, q_row):
    p_far = [lay.along_a(p_row, -i) for i in range(1, lay.A)]
    q_far = [lay.along_b(q_row, -j) for j in range(1, lay.B)]
    p_far = p_far[0] if lay.A == 2 else jnp.concatenate(p_far)
    q_far = q_far[0] if lay.B == 2 else jnp.concatenate(q_far)
    return (p_row, p_far, q_row, q_far)


def send_far(lay, far):
    A, B = lay.A, lay.B
    p_far, q_far = far
    p_got = [lay.along_a(p_far[(i - 1) * B : i * B], i) for i in range(1, A)]
    q_got = [lay.along_b(q_far[(j - 1) * A : j * A], j) for j in range(1, B)]
    return p_got, q_got


def scatter_far(lay, near, far):
    return add_blocks(near, *send_far(lay, far))


def scatter_near(lay, where, p_sums, q_sums):
    p_got = [lay.along_b(p_sums[j], j) for j in range(1, lay.B)]
    q_got = [lay.along_a(q_sums[i], i) for i in range(1, lay.A)]
    return last_sums(where, p_sums[0], q_sums[0], p_got, q_got, lay.fs)


def small_gather(lay, rows):
    held = rows
    bit = 1
    while bit < lay.tp:
        upper = (lay.z // bit) % 2 == 1
        got = lay.with_partner(held, "z", bit)
        held = jnp.concatenate([jnp.where(upper, got, held), jnp.where(upper, held, got)])
        bit *= 2
    return held


def add_two(left, right, name):
    def kernel(left_ref, right_ref, out_ref):
        out_ref[...] = left_ref[...] + right_ref[...]

    return on_chip(kernel, [array(left.shape, left.dtype)], [left, right], name, moved([left, right]))[0]


def ring_second(lay, where, turned, first):
    n = lay.tp
    up, down = ring_next(lay, turned, first)
    for step in range(1, n // 2):
        up_got, down_got = lay.along_z(up, 1), lay.along_z(down, -1)
        if step == n // 2 - 1:
            return up_got, down_got
        up = (ring_block(lay, turned, n // 2 - 1 - step).astype(f32) + up_got.astype(f32)).astype(bf16)
        down = (ring_block(lay, turned, n // 2 + 1 + step).astype(f32) + down_got.astype(f32)).astype(bf16)


def ring_block(lay, turned, m):
    size = turned.shape[0] // lay.tp
    first = (m % lay.tp) * size
    return turned[first : first + size]


def ring_start(lay, turned):
    far = ring_block(lay, turned, lay.tp // 2)
    half = far.shape[0] // 2
    return lay.along_z(far[:half], 1), lay.along_z(far[half:], -1)


def params(limit=SCOPED):
    return pltpu.CompilerParams(vmem_limit_bytes=limit)


def cost(microseconds, share=None):
    return pl.CostEstimate(flops=int(microseconds * (share or SHARE) * 1.15e9), bytes_accessed=0, transcendentals=0)


VMEM = pl.BlockSpec(memory_space=pltpu.VMEM)
SMEM = pl.BlockSpec(memory_space=pltpu.SMEM)


def array(shape, dtype):
    return jax.ShapeDtypeStruct(shape, dtype)


def listed(refs):
    return [(ref, k) for ref in refs for k in range(ref.shape[0])]


def aligned(value, size):
    return pl.multiple_of(value, size)


def column(where, n, width):
    return pl.ds(aligned(where[n] * width, width), width)


def stacked(refs, first, size, axis=0):
    return jnp.concatenate([ref[k, first : first + size, :] for ref, k in listed(refs)], axis=axis)


def turn(value, keep, ahead, behind):
    half = ROTARY // 2
    parts = []
    for chunk in range(value.shape[1] // LANES):
        v = value[:, chunk * LANES : (chunk + 1) * LANES]
        parts.append(
            v * keep
            + pltpu.roll(v, LANES - half, 1) * ahead
            + pltpu.roll(v, half, 1) * behind
        )
    return parts[0] if len(parts) == 1 else jnp.concatenate(parts, axis=1)


NORM_ROWS = 32
EXTRA = 16


def on_chip(kernel, outs, ins, name, estimate=None, scalars=0, scratch=(), grid=None, limit=SCOPED):
    more = {} if grid is None else {"grid": grid}
    return pl.pallas_call(
        kernel,
        out_shape=tuple(outs),
        in_specs=[SMEM] * scalars + [VMEM] * (len(ins) - scalars),
        out_specs=(VMEM,) * len(outs),
        scratch_shapes=list(scratch),
        compiler_params=params(limit),
        cost_estimate=estimate,
        name=name,
        **more,
    )(*ins)


def moved(values):
    return cost(1.5)


def stack_blocks(p_row, q_row):
    count = len(p_row)

    def kernel(*refs):
        ins, outs = refs[:-2], refs[-2:]
        for k, ref in enumerate(ins):
            if k < count:
                outs[0][k] = ref[...]
            else:
                outs[1][k - count] = ref[...]

    ins = list(p_row) + list(q_row)
    shape, dtype = ins[0].shape, ins[0].dtype
    outs = [array((count,) + shape, dtype), array((len(q_row),) + shape, dtype)]
    return on_chip(kernel, outs, ins, "stack_blocks", moved(ins))


def add_blocks(near, p_got, q_got):
    p_row, q_row = near
    counts = (p_row.shape[0], q_row.shape[0])
    ins = [p_row, q_row] + list(p_got) + list(q_got)

    def kernel(*refs):
        outs = refs[len(ins) :]
        groups = ((refs[0], refs[2 : 2 + len(p_got)]), (refs[1], refs[2 + len(p_got) : len(ins)]))
        at = 0
        for (own, got), count in zip(groups, counts):
            for k in range(count):
                total = own[k].astype(f32)
                for ref in got:
                    total = total + ref[k].astype(f32)
                outs[at][...] = total.astype(outs[at].dtype)
                at += 1

    shape = p_row.shape[1:]
    outs = [array(shape, bf16 if k else f32) for count in counts for k in range(count)]
    done = on_chip(kernel, outs, ins, "add_blocks", moved(ins))
    return list(done[: counts[0]]), list(done[counts[0] :])


def last_sums(where, p_own, q_own, p_got, q_got, fs):
    ins = [where, p_own, q_own] + list(p_got) + list(q_got)

    def kernel(where, p_ref, q_ref, *refs):
        keep, send = refs[-2:]
        p, q = p_ref[...], q_ref[...]
        for ref in refs[: len(p_got)]:
            p = p + ref[...].astype(f32)
        for ref in refs[len(p_got) : len(p_got) + len(q_got)]:
            q = q + ref[...].astype(f32)
        first = where[2 * fs] == 0
        keep[...] = jnp.where(first, p, q)
        send[...] = jnp.where(first, q, p).astype(bf16)

    shape = p_own.shape
    return on_chip(kernel, [array(shape, f32), array(shape, bf16)], ins, "last_sums", moved(ins[1:]), 1)


def ring_next(lay, turned, first):
    n = lay.tp
    size = turned.shape[0] // n
    half = size // 2
    D = turned.shape[1]
    above, below = (n // 2 - 1) * size, (n // 2 + 1) % n * size

    def kernel(turned_ref, up_ref, down_ref, up_out, down_out):
        up_out[:half] = (turned_ref[above : above + half].astype(f32) + up_ref[...].astype(f32)).astype(bf16)
        up_out[half:] = turned_ref[above + half : above + size]
        down_out[:half] = turned_ref[below : below + half]
        low = turned_ref[below + half : below + size].astype(f32) + down_ref[...].astype(f32)
        down_out[half:] = low.astype(bf16)

    outs = [array((size, D), bf16)] * 2
    return on_chip(kernel, outs, [turned, *first], "ring_next", cost(1.0))


def add_cores(keep, got):
    def kernel(keep_ref, got_ref, out_ref):
        out_ref[...] = (keep_ref[...].astype(f32) + got_ref[...].astype(f32)).astype(bf16)

    return on_chip(kernel, [array(keep.shape, bf16)], [keep, got], "add_cores", moved([keep, got]))[0]


def unstack(lay, where, gathered):
    devices, _, size, D = gathered.shape
    T = devices * size
    BD = D // lay.fs

    def kernel(where, row_ref, cot_in, rows_ref, cot_ref):
        at = pl.ds(aligned(pl.program_id(0) * size, size), size)
        rows_ref[at, :] = row_ref[0, 0]
        for n in range(lay.fs):
            cot_ref[at, n * BD : (n + 1) * BD] = cot_in[0, 0, :, column(where, n, BD)]

    return pl.pallas_call(
        kernel,
        out_shape=(array((T, D), bf16), array((T, D), bf16)),
        grid_spec=pltpu.PrefetchScalarGridSpec(
            num_scalar_prefetch=1,
            grid=(devices,),
            in_specs=[
                pl.BlockSpec((1, 1, size, D), lambda d, where: (d, 0, 0, 0)),
                pl.BlockSpec((1, 1, size, D), lambda d, where: (d, 1, 0, 0)),
            ],
            out_specs=(VMEM, VMEM),
        ),
        compiler_params=params(44 * 1024 * 1024),
        name="unstack",
    )(where, gathered, gathered)


def unpack(lay, where, pieces, first):
    BD = pieces[0].shape[2]

    def kernel(where, p0, p1, q0, q1, out_ref):
        for n, (ref, k) in enumerate(listed((p0, p1, q0, q1))):
            out_ref[where[n]] = ref[k, first : first + EXTRA, :]

    return on_chip(kernel, [array((lay.fs, EXTRA, BD), bf16)], [where, *pieces], "unpack", None, 1)[0]


def project(lay, where, rows, gain, shift, bias, tables, pieces):
    T, D = rows.shape
    H = bias.shape[1] // 3
    BD = D // lay.fs

    def kernel(where, rows_ref, gain_ref, shift_ref, bias_ref, tab_ref, p0, p1, q0, q1, normed_ref, stat_ref, q_ref, kv_ref):
        def some_rows(r, carry):
            at = pl.ds(aligned(r * NORM_ROWS, NORM_ROWS), NORM_ROWS)
            x = rows_ref[at, :].astype(f32)
            mean = jnp.sum(x, axis=1, keepdims=True) * (1.0 / D)
            x = x - mean
            var = jnp.sum(x * x, axis=1, keepdims=True) * (1.0 / D)
            scale = lax.rsqrt(var + EPSILON)
            normed = (x * scale * gain_ref[...] + shift_ref[...]).astype(bf16)
            for n in range(lay.fs):
                block = where[lay.fs + n]
                normed_ref[at, pl.ds(aligned(block * BD, BD), BD)] = normed[:, n * BD : (n + 1) * BD]
            stat_ref[0, at, :] = jnp.broadcast_to(mean, (NORM_ROWS, LANES))
            stat_ref[1, at, :] = jnp.broadcast_to(scale, (NORM_ROWS, LANES))
            return carry

        lax.fori_loop(0, T // NORM_ROWS, some_rows, 0, unroll=4)
        keep, ahead, behind = tab_ref[0], tab_ref[1], tab_ref[2]
        for s in range(3):
            total = dot(normed_ref[...], stacked((p0, p1, q0, q1), s * BD, BD)) + bias_ref[:, s * H : (s + 1) * H]
            if s == 0:
                q_ref[...] = (turn(total, keep, ahead, behind).astype(bf16) * (HEAD_DIM**-0.5)).astype(bf16)
            elif s == 1:
                kv_ref[0] = turn(total, keep, ahead, behind).astype(bf16)
            else:
                kv_ref[1] = total.astype(bf16)

    outs = [array((T, D), bf16), array((2, T, LANES), f32), array((T, H), bf16), array((2, T, H), bf16)]
    estimate = cost(12)
    ins = [where, rows, gain, shift, bias, tables, *pieces]
    return on_chip(kernel, outs, ins, "project", estimate, 1)


def attention(lay, queries, kv_own, kv_prev, cot, pieces, paths, codes, tables):
    T, H = queries.shape
    D = cot.shape[1]
    BD = D // lay.fs
    QB = T // QROWS
    SPAN = T + QROWS
    KB = SPAN // KROWS
    pairs = H // LANES
    scaling = HEAD_DIM**-0.5

    def kernel(
        q_ref, own_ref, prev_ref, cot_ref, path_ref, code_ref, tab_ref, p0, p1, q0, q1,
        att_ref, att_t_ref, dq_ref, dq_t_ref, dprev_ref, down_ref,
        k_sc, v_sc, kt_sc, vt_sc, dk_sc, dv_sc, bias_sc, e_sc, g_sc, p_sc, d_sc,
    ):
        pair = pl.program_id(0)
        i = pl.program_id(1)
        across = pl.ds(aligned(pair * LANES, LANES), LANES)

        @pl.when(i == 0)
        def _():
            k_sc[:T] = prev_ref[0, :, across]
            k_sc[T:] = own_ref[0, :, across]
            v_sc[:T] = prev_ref[1, :, across]
            v_sc[T:] = own_ref[1, :, across]
            for c in range(2 * T // KROWS):
                rows = slice(c * KROWS, (c + 1) * KROWS)
                kt_sc[:, rows] = k_sc[rows].T
                vt_sc[:, rows] = v_sc[rows].T
            dk_sc[...] = jnp.zeros_like(dk_sc)
            dv_sc[...] = jnp.zeros_like(dv_sc)

        base = pl.multiple_of(i * QROWS, QROWS)
        own_rows = pl.ds(base, QROWS)
        heads = pl.ds(aligned(3 * BD + pair * LANES, LANES), LANES)
        weight = jnp.concatenate([ref[k, heads, :] for ref, k in listed((p0, p1, q0, q1))], axis=1)
        grad = dot(cot_ref[own_rows, :], weight, NT).astype(bf16)
        queries_pair = q_ref[own_rows, across]

        key_at = lax.broadcasted_iota(jnp.int32, (KROWS, QROWS), 0)
        query_at = lax.broadcasted_iota(jnp.int32, (KROWS, QROWS), 1) + T
        path0, path1, path2 = path_ref[0:1, own_rows], path_ref[1:2, own_rows], path_ref[2:3, own_rows]
        for c in range(KB):
            start = pl.multiple_of(base + c * KROWS, KROWS)
            code = code_ref[pl.ds(start, KROWS), :]
            code = jnp.concatenate([code, code], axis=1)
            at = key_at + c * KROWS
            linked = (code == path0) | (code == path1) | (code == path2)
            seen = (linked & (at <= query_at)) | (at == query_at)
            bias_sc[c] = jnp.where(seen, 0.0, MASKED)

        lane = lax.broadcasted_iota(jnp.int32, (QROWS, LANES), 1)
        att_t, dq_t = [], []
        for head in range(2):
            mine = (lane >= head * HEAD_DIM) & (lane < (head + 1) * HEAD_DIM)
            qh = jnp.where(mine, queries_pair, jnp.zeros_like(queries_pair))
            gh = jnp.where(mine, grad, jnp.zeros_like(grad))
            top = jnp.full((1, QROWS), MASKED, f32)
            for c in range(KB):
                start = pl.multiple_of(base + c * KROWS, KROWS)
                s = dot(k_sc[pl.ds(start, KROWS), :], qh, NT) + bias_sc[c]
                e_sc[c] = s
                top = jnp.maximum(top, jnp.max(s, axis=0, keepdims=True))
            summed = jnp.zeros((1, QROWS), f32)
            mixed = jnp.zeros((1, QROWS), f32)
            for c in range(KB):
                start = pl.multiple_of(base + c * KROWS, KROWS)
                e = jnp.exp(e_sc[c] - top)
                g = dot(v_sc[pl.ds(start, KROWS), :], gh, NT)
                e_sc[c] = e
                g_sc[c] = g
                summed = summed + jnp.sum(e, axis=0, keepdims=True)
                mixed = mixed + jnp.sum(e * g, axis=0, keepdims=True)
            inverse = 1.0 / summed
            mixed = mixed * inverse
            for c in range(KB):
                probs = e_sc[c] * inverse
                p_sc[c * KROWS : (c + 1) * KROWS] = probs.astype(bf16)
                d_sc[c * KROWS : (c + 1) * KROWS] = (probs * (g_sc[c] - mixed)).astype(bf16)
            span = pl.ds(base, SPAN)
            hrow = slice(head * HEAD_DIM, (head + 1) * HEAD_DIM)
            att_t.append(dot(vt_sc[hrow, span], p_sc[...]))
            dq_t.append(dot(kt_sc[hrow, span], d_sc[...]))
            dv_sc[span, :] += dot(p_sc[...], gh)
            dk_sc[span, :] += dot(d_sc[...], qh)
        att = jnp.concatenate(att_t, axis=0)
        att_t_ref[across, own_rows] = att.astype(bf16)
        att_ref[own_rows, across] = att.T.astype(bf16)
        dq = jnp.concatenate(dq_t, axis=0).T * scaling
        dq = turn(dq, tab_ref[0, own_rows, :], -tab_ref[1, own_rows, :], -tab_ref[2, own_rows, :])
        dq_ref[own_rows, across] = dq.astype(bf16)
        dq_t_ref[across, own_rows] = dq.T.astype(bf16)

        @pl.when(i == QB - 1)
        def _():
            dprev_ref[0, :, across] = dk_sc[:T].astype(bf16)
            dprev_ref[1, :, across] = dv_sc[:T].astype(bf16)
            down_ref[0, :, across] = dk_sc[T:]
            down_ref[1, :, across] = dv_sc[T:]

    outs = [
        array((T, H), bf16),
        array((H, T), bf16),
        array((T, H), bf16),
        array((H, T), bf16),
        array((2, T, H), bf16),
        array((2, T, H), f32),
    ]
    scratch = [
        pltpu.VMEM((2 * T, LANES), bf16),
        pltpu.VMEM((2 * T, LANES), bf16),
        pltpu.VMEM((LANES, 2 * T), bf16),
        pltpu.VMEM((LANES, 2 * T), bf16),
        pltpu.VMEM((2 * T, LANES), f32),
        pltpu.VMEM((2 * T, LANES), f32),
        pltpu.VMEM((KB, KROWS, QROWS), f32),
        pltpu.VMEM((KB, KROWS, QROWS), f32),
        pltpu.VMEM((KB, KROWS, QROWS), f32),
        pltpu.VMEM((SPAN, QROWS), bf16),
        pltpu.VMEM((SPAN, QROWS), bf16),
    ]
    ins = [queries, kv_own, kv_prev, cot, paths, codes, tables, *pieces]
    estimate = cost(35)
    return on_chip(kernel, outs, ins, "attention", estimate, 0, scratch, (pairs, QB), 18 * 1024 * 1024)


def inner_forward(lay, normed, bias, pieces):
    T, D = normed.shape
    F = bias.shape[1]
    BD = D // lay.fs

    def kernel(x_ref, bias_ref, p0, p1, q0, q1, act_ref, act_t_ref, slope_ref):
        scale = (2.0 / jnp.pi) ** 0.5
        for c in range(F // BD):
            at = slice(c * BD, (c + 1) * BD)
            weight = stacked((p0, p1, q0, q1), c * BD, BD)
            for r in range(T // KROWS):
                rows = slice(r * KROWS, (r + 1) * KROWS)
                u = dot(x_ref[rows, :], weight) + bias_ref[:, at]
                square = u * u
                t = jnp.tanh(scale * (u + 0.044715 * (square * u)))
                act = (0.5 * u * (1.0 + t)).astype(bf16)
                act_ref[rows, at] = act
                act_t_ref[at, rows] = act.T
                slope = 0.5 * (1.0 + t) + 0.5 * u * (1.0 - t * t) * (scale * (1.0 + (3 * 0.044715) * square))
                slope_ref[rows, at] = slope

    outs = [array((T, F), bf16), array((F, T), bf16), array((T, F), f32)]
    estimate = cost(8)
    return on_chip(kernel, outs, [normed, bias, *pieces], "inner_forward", estimate)


def inner_backward(lay, cot, slope, pieces):
    T, D = cot.shape
    F = slope.shape[1]
    BD = D // lay.fs

    def kernel(c_ref, slope_ref, p0, p1, q0, q1, grad_ref, grad_t_ref, bias_ref):
        for c in range(F // BD):
            at = slice(c * BD, (c + 1) * BD)
            weight = stacked((p0, p1, q0, q1), c * BD, BD, axis=1)
            sums = jnp.zeros((1, BD), f32)
            for r in range(T // KROWS):
                rows = slice(r * KROWS, (r + 1) * KROWS)
                grad = (dot(c_ref[rows, :], weight, NT) * slope_ref[rows, at]).astype(bf16)
                grad_ref[rows, at] = grad
                grad_t_ref[at, rows] = grad.T
                sums = sums + jnp.sum(grad.astype(f32), axis=0, keepdims=True)
            bias_ref[:, at] = sums

    outs = [array((T, F), bf16), array((F, T), bf16), array((1, F), f32)]
    estimate = cost(5)
    return on_chip(kernel, outs, [cot, slope, *pieces], "inner_backward", estimate)


def block_grads(lay, turned, wide, picks, name):
    F, T = turned.shape
    BD = wide.shape[1] // lay.fs

    def kernel(turned_ref, wide_ref, *outs):
        for ref, (first, count) in zip(outs, picks):
            for k in range(count):
                n = first + k
                ref[k] = dot(turned_ref[...], wide_ref[:, n * BD : (n + 1) * BD]).astype(bf16)

    outs = [array((count, F, BD), bf16) for _, count in picks]
    estimate = cost(2.7)
    return on_chip(kernel, outs, [turned, wide], name, estimate)


def attn_weight_grads(lay, where, normed, cot, dq_t, dkv_t, att_t, sums, picks, name):
    T, D = normed.shape
    H = dq_t.shape[0]
    BD = D // lay.fs
    F = sums[3].shape[1]

    def kernel(where, x_ref, c_ref, dq_ref, dkv_ref, att_ref, sums_ref, got_ref, head_ref, hidden_ref, *refs):
        outs, held = refs[:-1], refs[-1]
        core = where[2 * lay.fs]
        for ref, (first, count) in zip(outs, picks):
            for k in range(count):
                n = first + k
                at = slice(n * BD, (n + 1) * BD)
                ref[k, :H] = dot(dq_ref[...], x_ref[:, at]).astype(bf16)
                ref[k, H : 3 * H] = dot(dkv_ref[...], x_ref[:, at]).astype(bf16)
                ref[k, 3 * H : 4 * H] = dot(att_ref[...], c_ref[:, at]).astype(bf16)
                at = column(where, n, BD)
                mine = (where[n] // (lay.fs // 2) == core).astype(f32)
                held[...] = jnp.zeros_like(held)
                held[0:3, :] = sums_ref[0:3, at] + got_ref[0:3, at]
                held[3:6, :] = head_ref[0:3, :] * mine
                for j in range(F // BD):
                    held[6 + j : 7 + j, :] = hidden_ref[:, j * BD : (j + 1) * BD] * mine
                ref[k, 4 * H :] = held[...].astype(bf16)

    outs = [array((count, 4 * H + EXTRA, BD), bf16) for _, count in picks]
    ins = [where, normed, cot, dq_t, dkv_t, att_t, *sums]
    return on_chip(kernel, outs, ins, name, cost(2.7), 1, [pltpu.VMEM((EXTRA, BD), f32)])


def output_rows(lay, where, attended, activated, attn_pieces, outer_pieces, D):
    T, F = activated.shape
    H = attended.shape[1]
    BD = D // lay.fs
    G = T // 2
    Z = G // lay.tp

    def kernel(where, att_ref, act_ref, a0, a1, b0, b1, p0, p1, q0, q1, keep_ref, send_ref):
        core, z = where[2 * lay.fs], where[2 * lay.fs + 1]
        small = listed((a0, a1, b0, b1))
        large = listed((p0, p1, q0, q1))
        for base, out_ref in ((core * G, keep_ref), ((1 - core) * G, send_ref)):
            rows = pl.ds(aligned(base, G), G)
            for n in range(lay.fs):
                (sref, sk), (lref, lk) = small[n], large[n]
                at = column(where, n, BD)
                total = dot(act_ref[rows, :], lref[lk]) + dot(att_ref[rows, :], sref[sk, 3 * BD : 3 * BD + H, :])
                low = total.astype(bf16)
                for r in range(lay.tp):
                    to = lax.rem(r + lay.tp - z, lay.tp)
                    out_ref[pl.ds(aligned(to * Z, Z), Z), at] = low[r * Z : (r + 1) * Z]

    outs = [array((G, D), bf16)] * 2
    estimate = cost(9.7)
    ins = [where, attended, activated, *attn_pieces, *outer_pieces]
    return on_chip(kernel, outs, ins, "output_rows", estimate, 1)


def normed_grads(lay, where, pre_grad, dq, dkv, rows, stats, cot_sums, attn_pieces, inner_pieces):
    T, F = pre_grad.shape
    D = rows.shape[1]
    G = T // 2
    H = dq.shape[1]
    BD = D // lay.fs
    Z = G // lay.tp

    def kernel(where, pre_ref, dq_ref, dkv_ref, rows_ref, stat_ref, cot_sums_ref, a0, a1, b0, b1, p0, p1, q0, q1, keep_ref, send_ref, sums_ref):
        sums_ref[...] = jnp.zeros_like(sums_ref)
        sums_ref[2:3, :] = cot_sums_ref[...]
        core, z = where[2 * lay.fs], where[2 * lay.fs + 1]
        small = listed((a0, a1, b0, b1))
        large = listed((p0, p1, q0, q1))
        for base, out_ref in ((core * G, keep_ref), ((1 - core) * G, send_ref)):
            rows = pl.ds(aligned(base, G), G)
            left = jnp.concatenate([dq_ref[rows, :], dkv_ref[0, rows, :], dkv_ref[1, rows, :]], axis=1)
            for n in range(lay.fs):
                (sref, sk), (lref, lk) = small[n], large[n]
                at = column(where, n, BD)
                weight = jnp.concatenate([lref[lk, c * BD : (c + 1) * BD, :] for c in range(F // BD)], axis=1)
                narrow = jnp.concatenate([sref[sk, s * BD : (s + 1) * BD, :] for s in range(3)], axis=1)
                total = dot(pre_ref[rows, :], weight, NT) + dot(left, narrow, NT)
                low = total.astype(bf16)
                for r in range(lay.tp):
                    to = lax.rem(r + lay.tp - z, lay.tp)
                    out_ref[pl.ds(aligned(to * Z, Z), Z), at] = low[r * Z : (r + 1) * Z]
                x = rows_ref[rows, at].astype(f32)
                stand = jnp.concatenate(
                    [
                        (x[:, c * LANES : (c + 1) * LANES] - stat_ref[0, rows, :]) * stat_ref[1, rows, :]
                        for c in range(BD // LANES)
                    ],
                    axis=1,
                )
                sums_ref[0:1, at] += jnp.sum(total * stand, axis=0, keepdims=True)
                sums_ref[1:2, at] += jnp.sum(total, axis=0, keepdims=True)

    outs = [array((G, D), bf16), array((G, D), bf16), array((8, D), f32)]
    estimate = cost(11.5)
    ins = [where, pre_grad, dq, dkv, rows, stats, cot_sums, *attn_pieces, *inner_pieces]
    return on_chip(kernel, outs, ins, "normed_grads", estimate, 1)


def key_value_grads(dkv_own, dkv_got, dq, tables):
    _, T, H = dkv_own.shape

    def kernel(own_ref, got_ref, dq_ref, tab_ref, out_ref, out_t_ref, bias_ref):
        dk = own_ref[0] + got_ref[0].astype(f32)
        dv = own_ref[1] + got_ref[1].astype(f32)
        dk = turn(dk, tab_ref[0], -tab_ref[1], -tab_ref[2]).astype(bf16)
        dv = dv.astype(bf16)
        out_ref[0] = dk
        out_ref[1] = dv
        out_t_ref[:H] = dk.T
        out_t_ref[H:] = dv.T
        bias_ref[...] = jnp.zeros_like(bias_ref)
        bias_ref[0:1] = jnp.sum(dq_ref[...].astype(f32), axis=0, keepdims=True)
        bias_ref[1:2] = jnp.sum(dk.astype(f32), axis=0, keepdims=True)
        bias_ref[2:3] = jnp.sum(dv.astype(f32), axis=0, keepdims=True)

    outs = [array((2, T, H), bf16), array((2 * H, T), bf16), array((8, H), f32)]
    return on_chip(kernel, outs, [dkv_own, dkv_got, dq, tables], "key_value_grads", cost(10.0, 1.0))


def body(
    residual,
    norm_gain,
    norm_shift,
    qkv_weight,
    qkv_bias,
    dense_weight,
    dense_bias,
    inner_weight,
    inner_bias,
    outer_weight,
    outer_bias,
    cotangent,
    segment,
    ancestors,
    valid_slot,
):
    lay = Layout()
    fs, tp = lay.fs, lay.tp
    D = residual.shape[1]
    T = residual.shape[0] * tp * 2
    HC = qkv_weight.shape[2] // 2
    FC = inner_weight.shape[1] // 2
    BD = qkv_weight.shape[1]
    assert T >= TREE_LEN - 1 and BD == HC
    where = lay.table()
    is0 = lay.is0

    def halves(group):
        keep, send = lay.by_core(*group)
        return lay.by_core(keep, lay.over_core(send))

    n_small, n_qkv, n_inner = norm_gain.shape[0], qkv_bias.shape[1], inner_bias.shape[0]
    strips = [inner_weight[:, c * BD : (c + 1) * BD] for c in range(2 * FC // BD)]
    count = len(strips) // 2
    inner_group = [jnp.concatenate(strips[:count]), jnp.concatenate(strips[count:])]
    outer_group = [outer_weight[:FC], outer_weight[FC:]]
    together = lax.optimization_barrier
    cot_f = cotangent.astype(f32)
    cot_sums = jnp.sum(cot_f, axis=0, keepdims=True)
    gathered = lax.all_gather(jnp.stack([residual, cotangent]), ("c", "z"), axis=0)
    four = jnp.stack([norm_gain, norm_shift, dense_bias, outer_bias])
    inner_near = gather_near(lay, *halves(inner_group))
    four = small_gather(lay, four[None]).transpose(1, 0, 2).reshape(4, BD)
    biases = jnp.stack(
        [
            jnp.pad(qkv_bias.reshape(-1), (0, BD - 3 * n_qkv)),
            jnp.pad(inner_bias, (0, BD - n_inner)),
        ]
    )
    extra = jnp.concatenate([four, biases, jnp.zeros((EXTRA - 6, BD), bf16)])
    attn_group = [
        jnp.concatenate(
            [
                qkv_weight[:, :, c * HC : (c + 1) * HC].reshape(3 * BD, HC),
                dense_weight[c * HC : (c + 1) * HC],
                extra,
            ]
        )
        for c in range(2)
    ]

    attn_group, outer_group, inner_near = together((attn_group, outer_group, inner_near))
    attn_first, outer_first = halves(attn_group), halves(outer_group)
    attn_near = gather_near(lay, *attn_first)
    outer_near = gather_near(lay, *outer_first)
    attn_near, outer_near = together((attn_near, outer_near))
    attn_pieces = gather_far(lay, *attn_near)
    attn_pieces, inner_near, gathered = together((attn_pieces, inner_near, gathered))
    inner_pieces = gather_far(lay, *inner_near)

    vectors = unpack(lay, where, attn_pieces, 4 * HC).astype(f32)
    gain = vectors[:, 0].reshape(1, D)
    shift = vectors[:, 1].reshape(1, D)
    bias_sum = (vectors[:, 2] + vectors[:, 3]).reshape(1, D)
    mine = lax.dynamic_slice_in_dim(vectors[:, 4:6], lay.core * (fs // 2), fs // 2, axis=0)
    my_qkv_bias = (
        mine[:, 0, : 3 * n_qkv].reshape(fs // 2, 3, n_qkv).transpose(1, 0, 2).reshape(1, 3 * HC)
    )
    my_inner_bias = mine[:, 1, :n_inner].reshape(1, FC)

    base_slot = lay.chip * T
    seg_front = jnp.concatenate([jnp.zeros((T,), jnp.int32), segment])
    valid_front = jnp.concatenate([jnp.zeros((T,), jnp.int32), valid_slot])
    window_seg = lax.dynamic_slice_in_dim(seg_front, base_slot, 2 * T)
    window_valid = lax.dynamic_slice_in_dim(valid_front, base_slot, 2 * T)
    codes = jnp.where(window_valid == 1, window_seg, -1)
    own_seg, own_valid = window_seg[T:], window_valid[T:]
    seg_ids = jnp.arange(ancestors.shape[0], dtype=jnp.int32)
    onehot = (own_seg[None, :] == seg_ids[:, None]).astype(jnp.int32)
    paths = jnp.sum(onehot[None, :, :] * ancestors.T[:, :, None], axis=1)
    paths = jnp.where(own_valid[None, :] == 1, paths, -2)
    key_at = jnp.arange(2 * T, dtype=jnp.int32)[:, None]
    query_at = T + jnp.arange(T, dtype=jnp.int32)[None, :]
    code_col = codes[:, None]
    linked = (code_col == paths[0:1]) | (code_col == paths[1:2]) | (code_col == paths[2:3])
    allowed = (linked & (key_at <= query_at)) | (key_at == query_at)
    positions = jnp.sum(allowed.astype(jnp.int32), axis=0) - 1
    paths8 = jnp.concatenate([paths, jnp.zeros((5, T), jnp.int32)])
    codes_wide = jnp.broadcast_to(code_col, (2 * T, LANES))

    half_rot = ROTARY // 2
    lane = jnp.arange(LANES, dtype=jnp.int32) % HEAD_DIM
    freq = 10000.0 ** (-((lane % half_rot).astype(f32) * 2.0 / ROTARY))
    angle = positions.astype(f32)[:, None] * jnp.where(lane < ROTARY, freq, 0.0)[None, :]
    sine = jnp.sin(angle)
    lane = lane[None, :]
    tables = jnp.stack(
        [
            jnp.cos(angle),
            jnp.where(lane < half_rot, -sine, 0.0),
            jnp.where((lane >= half_rot) & (lane < ROTARY), sine, 0.0),
        ]
    )
    part = (lay.chip * 2 + lay.core) % (fs // 2)
    gathered, part, tables, paths8, codes_wide, my_qkv_bias, my_inner_bias, bias_sum, cot_sums = together(
        (gathered, part, tables, paths8, codes_wide, my_qkv_bias, my_inner_bias, bias_sum, cot_sums)
    )
    rows, cot = unstack(lay, where, gathered)

    normed, stats, queries, kv_own = project(
        lay, where, rows, gain, shift, my_qkv_bias, tables, attn_pieces
    )
    kv_prev = lay.to_chip(kv_own, 1)
    inner_pieces, outer_near, queries = together((inner_pieces, outer_near, queries))
    outer_pieces = gather_far(lay, *outer_near)
    A, B = lay.A, lay.B
    near = ((0, B), (A * B, A))
    far = ((B, A * B - B), (A * B + A, A * B - A))

    activated, act_t, slope = inner_forward(lay, normed, my_inner_bias, inner_pieces)
    outer_far = block_grads(lay, act_t, cot, far, "outer_grads_far")
    outer_near = block_grads(lay, tie(act_t, *outer_far), cot, near, "outer_grads_near")
    queries = tie(queries, *outer_near)
    attended, att_t, dq, dq_t, dkv_prev, dkv_own = attention(
        lay, queries, kv_own, kv_prev, cot, attn_pieces, paths8, codes_wide, tables
    )
    dkv_got = lay.to_chip(dkv_prev, -1)
    outer_row = scatter_far(lay, outer_near, outer_far)

    slope, outer_row = together((slope, outer_row, dq))[:2]
    outer_keep, outer_send = scatter_near(lay, where, *outer_row)
    pre_grad, pre_t, inner_bias_part = inner_backward(lay, cot, slope, outer_pieces)
    inner_far = block_grads(lay, pre_t, normed, far, "inner_grads_far")
    pre_t = tie(pre_t, *inner_far)
    inner_near = block_grads(lay, pre_t, normed, near, "inner_grads_near")
    inner_got = send_far(lay, inner_far)
    activated, outer_keep, outer_send = together((activated, outer_keep, outer_send, inner_near))[:3]
    outer_got = lay.over_core(outer_send)
    keep_out, send_out = output_rows(lay, where, attended, activated, attn_pieces, outer_pieces, D)
    got_out = lay.over_core(send_out)
    dkv_own = tie(dkv_own, keep_out)
    dkv, dkv_t, qkv_bias_part = key_value_grads(dkv_own, dkv_got, dq, tables)
    out_both = add_cores(keep_out, tie(got_out, dkv))
    pre_grad, out_both = together((pre_grad, out_both, dkv))[:2]
    out_first = ring_start(lay, out_both)
    keep_grad, send_grad, norm_sums = normed_grads(
        lay, where, pre_grad, dq, dkv, rows, stats, cot_sums, attn_pieces, inner_pieces
    )
    keep_grad, send_grad, norm_sums, out_first, inner_got = together(
        (keep_grad, send_grad, norm_sums, out_first, inner_got)
    )
    inner_row = add_blocks(inner_near, *inner_got)
    got_grad = lay.over_core(send_grad)
    bit = 1
    got_sums = lay.with_partner(norm_sums, "z", bit)
    while bit < tp // 2:
        norm_sums = add_two(norm_sums, got_sums, "add_two")
        bit *= 2
        got_sums = lay.with_partner(norm_sums, "z", bit)
    inner_keep, inner_send = scatter_near(lay, where, *inner_row)
    sums = (norm_sums, got_sums, qkv_bias_part, inner_bias_part)
    attn_far = attn_weight_grads(
        lay, where, normed, cot, dq_t, tie(dkv_t, inner_row[0][0]), att_t, sums, far, "attn_grads_far"
    )
    grad_both = add_cores(keep_grad, got_grad)
    grad_first = ring_start(lay, grad_both)
    dkv_t = tie(dkv_t, grad_both, *attn_far)
    attn_near = attn_weight_grads(lay, where, normed, cot, dq_t, dkv_t, att_t, sums, near, "attn_grads_near")
    attn_far, grad_first, inner_keep, inner_send = together((attn_far, grad_first, inner_keep, inner_send))
    inner_got = lay.over_core(inner_send)
    attn_row = scatter_far(lay, attn_near, attn_far)
    grad_second = ring_second(lay, where, grad_both, grad_first)
    grad_second, out_first = together((grad_second, out_first, attn_row))[:2]
    attn_keep, attn_send = scatter_near(lay, where, *attn_row)
    attn_got = lay.over_core(attn_send)
    out_second = ring_second(lay, where, out_both, out_first)

    def in_core_order(keep, got):
        return lay.by_core(keep, got.astype(f32))

    low, high = in_core_order(outer_keep, outer_got)
    outer_weight_grad = jnp.concatenate([low, high], axis=0)
    low, high = in_core_order(inner_keep, inner_got)
    inner_weight_grad = jnp.concatenate([low, high], axis=0).T
    low, high = in_core_order(attn_keep, attn_got)
    small = (low + high)[4 * HC :]
    low, high = low[: 4 * HC], high[: 4 * HC]
    qkv_weight_grad = jnp.concatenate(
        [low[: 3 * HC].reshape(3, HC, BD), high[: 3 * HC].reshape(3, HC, BD)], axis=1
    ).transpose(0, 2, 1)
    dense_weight_grad = jnp.concatenate([low[3 * HC :], high[3 * HC :]], axis=0)

    def total_rows(turned, second):
        return ring_block(lay, turned, 0).astype(f32) + second[0].astype(f32) + second[1].astype(f32)

    inputs_f = residual.astype(f32)
    output = (inputs_f + total_rows(out_both, out_second) + bias_sum).astype(bf16)
    row_grad = total_rows(grad_both, grad_second)
    row_mean = jnp.mean(inputs_f, axis=-1, keepdims=True)
    centered = inputs_f - row_mean
    scale = lax.rsqrt(jnp.mean(centered * centered, axis=-1, keepdims=True) + EPSILON)
    stand = centered * scale
    e = row_grad * gain
    e_mean = jnp.mean(e, axis=-1, keepdims=True)
    es_mean = jnp.mean(e * stand, axis=-1, keepdims=True)
    residual_grad = (cot_f + (e - e_mean - stand * es_mean) * scale).astype(bf16)

    small, part, place = together((small, part, lay.z))
    gain_grad, shift_grad, out_bias_grad = (
        lax.dynamic_slice_in_dim(small[k], place * n_small, n_small) for k in range(3)
    )
    qkv_bias_grad = lax.dynamic_slice_in_dim(small[3:6], part * n_qkv, n_qkv, axis=1)
    hidden = small[6 : 6 + FC // BD].reshape(-1)
    inner_bias_grad = lax.dynamic_slice_in_dim(hidden, part * n_inner, n_inner)

    return (
        output,
        residual_grad,
        gain_grad,
        shift_grad,
        qkv_weight_grad,
        qkv_bias_grad,
        dense_weight_grad,
        out_bias_grad,
        inner_weight_grad,
        inner_bias_grad,
        outer_weight_grad,
        out_bias_grad,
    )


def solution(mesh):
    fs, tp = mesh.devices.shape
    inside = jax.sharding.Mesh(mesh.devices.reshape(2, fs // 4, 2, tp), ("a", "b", "c", "z"))
    all_axes = ("a", "b", "c", "z")
    fsdp = ("a", "b", "c")
    crossed = ("z", "a", "b", "c")
    return jax.shard_map(
        body,
        mesh=inside,
        in_specs=(
            P(all_axes, None),
            P(all_axes),
            P(all_axes),
            P(None, fsdp, "z"),
            P(None, crossed),
            P("z", fsdp),
            P(all_axes),
            P(fsdp, "z"),
            P(crossed),
            P("z", fsdp),
            P(all_axes),
            P(all_axes, None),
            P(),
            P(),
            P(),
        ),
        out_specs=(
            P(all_axes, None),
            P(all_axes, None),
            P(all_axes),
            P(all_axes),
            P(None, fsdp, "z"),
            P(None, crossed),
            P("z", fsdp),
            P(all_axes),
            P(fsdp, "z"),
            P(crossed),
            P("z", fsdp),
            P(all_axes),
        ),
        check_vma=False,
    )
```

```python
import jax
import jax.numpy as jnp
from jax import lax
from jax.experimental import pallas as pl
from jax.experimental.pallas import tpu as pltpu
from jax.sharding import PartitionSpec as P

HEAD_DIM = 64
ROTARY = 32
TREE_LEN = 1024
EPSILON = 1e-05
LANES = 128
QROWS = 256
KROWS = 256
MASKED = -1e30
SHARE = 0.2
SCOPED = 14 * 1024 * 1024

f32 = jnp.float32
bf16 = jnp.bfloat16

NN = (((1,), (0,)), ((), ()))
NT = (((1,), (1,)), ((), ()))
TN = (((0,), (0,)), ((), ()))


def dot(left, right, dims=NN):
    return lax.dot_general(left, right, dims, preferred_element_type=f32)


class Layout:
    def __init__(self):
        self.A, self.B, self.tp = (lax.axis_size(n) for n in ("a", "b", "z"))
        self.fs = self.A * self.B * 2
        self.a, self.b, self.core, self.z = (lax.axis_index(n) for n in ("a", "b", "c", "z"))
        self.chip = self.a * self.B + self.b
        self.is0 = self.core == 0

    def blocks(self):
        A, B = self.A, self.B
        first = [(0, i, j) for i in range(A) for j in range(B)]
        second = [(1, i, j) for j in range(B) for i in range(A)]
        return first + second

    def table(self):
        A, B = self.A, self.B
        device = []
        for core, i, j in self.blocks():
            chip = ((self.a + i) % A) * B + (self.b + j) % B
            device.append(chip * 2 + core)
        block = []
        for chip in range(A * B):
            i = (chip // B + A - self.a) % A
            j = (chip % B + B - self.b) % B
            block.append(i * B + j)
            block.append(A * B + j * A + i)
        return jnp.stack(device + block + [self.core, self.z]).astype(jnp.int32)

    def over(self, value, axis, steps):
        n = lax.axis_size(axis)
        return lax.ppermute(value, axis, [(s, (s + steps) % n) for s in range(n)])

    def over_core(self, value):
        return self.over(value, "c", 1)

    def along_a(self, value, steps):
        return self.over(value, "a", steps)

    def along_b(self, value, steps):
        return self.over(value, "b", steps)

    def along_z(self, value, steps):
        return self.over(value, "z", steps)

    def to_chip(self, value, steps):
        pairs = [(s, s + steps) for s in range(self.A * self.B) if 0 <= s + steps < self.A * self.B]
        return lax.ppermute(value, ("a", "b"), pairs)

    def with_partner(self, value, axis, bit):
        return lax.ppermute(value, axis, [(s, s ^ bit) for s in range(lax.axis_size(axis))])

    def by_core(self, own, other):
        return jnp.where(self.is0, own, other), jnp.where(self.is0, other, own)


def tie(value, *others):
    return lax.optimization_barrier((value,) + others)[0]


def gather_near(lay, first, second):
    p_row = [first] + [lay.along_b(first, -j) for j in range(1, lay.B)]
    q_row = [second] + [lay.along_a(second, -i) for i in range(1, lay.A)]
    return stack_blocks(p_row, q_row)


def gather_far(lay, p_row, q_row):
    p_far = [lay.along_a(p_row, -i) for i in range(1, lay.A)]
    q_far = [lay.along_b(q_row, -j) for j in range(1, lay.B)]
    p_far = p_far[0] if lay.A == 2 else jnp.concatenate(p_far)
    q_far = q_far[0] if lay.B == 2 else jnp.concatenate(q_far)
    return (p_row, p_far, q_row, q_far)


def send_far(lay, far):
    A, B = lay.A, lay.B
    p_far, q_far = far
    p_got = [lay.along_a(p_far[(i - 1) * B : i * B], i) for i in range(1, A)]
    q_got = [lay.along_b(q_far[(j - 1) * A : j * A], j) for j in range(1, B)]
    return p_got, q_got


def scatter_far(lay, near, far):
    return add_blocks(near, *send_far(lay, far))


def scatter_near(lay, where, p_sums, q_sums):
    p_got = [lay.along_b(p_sums[j], j) for j in range(1, lay.B)]
    q_got = [lay.along_a(q_sums[i], i) for i in range(1, lay.A)]
    return last_sums(where, p_sums[0], q_sums[0], p_got, q_got, lay.fs)


def small_gather(lay, rows):
    held = rows
    bit = 1
    while bit < lay.tp:
        upper = (lay.z // bit) % 2 == 1
        got = lay.with_partner(held, "z", bit)
        held = jnp.concatenate([jnp.where(upper, got, held), jnp.where(upper, held, got)])
        bit *= 2
    return held


def add_two(left, right, name):
    def kernel(left_ref, right_ref, out_ref):
        out_ref[...] = left_ref[...] + right_ref[...]

    return on_chip(kernel, [array(left.shape, left.dtype)], [left, right], name, moved([left, right]))[0]


def ring_second(lay, where, turned, first):
    n = lay.tp
    up, down = ring_next(lay, turned, first)
    for step in range(1, n // 2):
        up_got, down_got = lay.along_z(up, 1), lay.along_z(down, -1)
        if step == n // 2 - 1:
            return up_got, down_got
        up = (ring_block(lay, turned, n // 2 - 1 - step).astype(f32) + up_got.astype(f32)).astype(bf16)
        down = (ring_block(lay, turned, n // 2 + 1 + step).astype(f32) + down_got.astype(f32)).astype(bf16)


def ring_block(lay, turned, m):
    size = turned.shape[0] // lay.tp
    first = (m % lay.tp) * size
    return turned[first : first + size]


def ring_start(lay, turned):
    far = ring_block(lay, turned, lay.tp // 2)
    half = far.shape[0] // 2
    return lay.along_z(far[:half], 1), lay.along_z(far[half:], -1)


def params(limit=SCOPED):
    return pltpu.CompilerParams(vmem_limit_bytes=limit)


def cost(microseconds, share=None):
    return pl.CostEstimate(flops=int(microseconds * (share or SHARE) * 1.15e9), bytes_accessed=0, transcendentals=0)


VMEM = pl.BlockSpec(memory_space=pltpu.VMEM)
SMEM = pl.BlockSpec(memory_space=pltpu.SMEM)


def array(shape, dtype):
    return jax.ShapeDtypeStruct(shape, dtype)


def listed(refs):
    return [(ref, k) for ref in refs for k in range(ref.shape[0])]


def aligned(value, size):
    return pl.multiple_of(value, size)


def column(where, n, width):
    return pl.ds(aligned(where[n] * width, width), width)


def stacked(refs, first, size, axis=0):
    return jnp.concatenate([ref[k, first : first + size, :] for ref, k in listed(refs)], axis=axis)


def turn(value, keep, ahead, behind):
    half = ROTARY // 2
    parts = []
    for chunk in range(value.shape[1] // LANES):
        v = value[:, chunk * LANES : (chunk + 1) * LANES]
        parts.append(
            v * keep
            + pltpu.roll(v, LANES - half, 1) * ahead
            + pltpu.roll(v, half, 1) * behind
        )
    return parts[0] if len(parts) == 1 else jnp.concatenate(parts, axis=1)


NORM_ROWS = 32
EXTRA = 16


def on_chip(kernel, outs, ins, name, estimate=None, scalars=0, scratch=(), grid=None, limit=SCOPED):
    more = {} if grid is None else {"grid": grid}
    return pl.pallas_call(
        kernel,
        out_shape=tuple(outs),
        in_specs=[SMEM] * scalars + [VMEM] * (len(ins) - scalars),
        out_specs=(VMEM,) * len(outs),
        scratch_shapes=list(scratch),
        compiler_params=params(limit),
        cost_estimate=estimate,
        name=name,
        **more,
    )(*ins)


def moved(values):
    return cost(1.5)


def stack_blocks(p_row, q_row):
    count = len(p_row)

    def kernel(*refs):
        ins, outs = refs[:-2], refs[-2:]
        for k, ref in enumerate(ins):
            if k < count:
                outs[0][k] = ref[...]
            else:
                outs[1][k - count] = ref[...]

    ins = list(p_row) + list(q_row)
    shape, dtype = ins[0].shape, ins[0].dtype
    outs = [array((count,) + shape, dtype), array((len(q_row),) + shape, dtype)]
    return on_chip(kernel, outs, ins, "stack_blocks", moved(ins))


def add_blocks(near, p_got, q_got):
    p_row, q_row = near
    counts = (p_row.shape[0], q_row.shape[0])
    ins = [p_row, q_row] + list(p_got) + list(q_got)

    def kernel(*refs):
        outs = refs[len(ins) :]
        groups = ((refs[0], refs[2 : 2 + len(p_got)]), (refs[1], refs[2 + len(p_got) : len(ins)]))
        at = 0
        for (own, got), count in zip(groups, counts):
            for k in range(count):
                total = own[k].astype(f32)
                for ref in got:
                    total = total + ref[k].astype(f32)
                outs[at][...] = total.astype(outs[at].dtype)
                at += 1

    shape = p_row.shape[1:]
    outs = [array(shape, bf16 if k else f32) for count in counts for k in range(count)]
    done = on_chip(kernel, outs, ins, "add_blocks", moved(ins))
    return list(done[: counts[0]]), list(done[counts[0] :])


def add_groups(groups):
    (p_row, q_row), p_got, q_got = groups[0]
    counts = (p_row.shape[0], q_row.shape[0])
    ins, spans = [], []
    for near, p_in, q_in in groups:
        spans.append((len(ins), len(p_in), len(q_in)))
        ins += [*near, *p_in, *q_in]

    def kernel(*refs):
        outs = refs[len(ins) :]
        for g, (first, p_count, q_count) in enumerate(spans):
            p_ins = refs[first + 2 : first + 2 + p_count]
            q_ins = refs[first + 2 + p_count : first + 2 + p_count + q_count]
            at = 2 * len(groups)
            for side, (own, got) in enumerate(((refs[first], p_ins), (refs[first + 1], q_ins))):
                for k in range(counts[side]):
                    total = own[k].astype(f32)
                    for ref in got:
                        total = total + ref[k].astype(f32)
                    if k == 0:
                        outs[2 * g + side][...] = total
                    else:
                        outs[at][g] = total.astype(bf16)
                        at += 1

    shape = p_row.shape[1:]
    onward = array((len(groups),) + shape, bf16)
    outs = [array(shape, f32)] * (2 * len(groups)) + [onward] * (counts[0] + counts[1] - 2)
    done = on_chip(kernel, outs, ins, "add_groups", moved(ins))
    own, rest = done[: 2 * len(groups)], done[2 * len(groups) :]
    return list(own), list(rest[: counts[0] - 1]), list(rest[counts[0] - 1 :])


def last_groups(lay, where, own, p_next, q_next):
    p_got = [lay.along_b(p, j + 1) for j, p in enumerate(p_next)]
    q_got = [lay.along_a(q, i + 1) for i, q in enumerate(q_next)]
    count = len(own) // 2
    ins = [where, *own, *p_got, *q_got]

    def kernel(where, *refs):
        got, outs = refs[len(own) : len(ins) - 1], refs[len(ins) - 1 :]
        first = where[2 * lay.fs] == 0
        for g in range(count):
            p, q = refs[2 * g][...], refs[2 * g + 1][...]
            for ref in got[: len(p_got)]:
                p = p + ref[g].astype(f32)
            for ref in got[len(p_got) :]:
                q = q + ref[g].astype(f32)
            outs[g][...] = jnp.where(first, p, q)
            outs[-1][g] = jnp.where(first, q, p).astype(bf16)

    shape = own[0].shape
    outs = [array(shape, f32)] * count + [array((count,) + shape, bf16)]
    done = on_chip(kernel, outs, ins, "last_groups", moved(ins[1:]), 1)
    return done[:count], done[count]


def last_sums(where, p_own, q_own, p_got, q_got, fs):
    ins = [where, p_own, q_own] + list(p_got) + list(q_got)

    def kernel(where, p_ref, q_ref, *refs):
        keep, send = refs[-2:]
        p, q = p_ref[...], q_ref[...]
        for ref in refs[: len(p_got)]:
            p = p + ref[...].astype(f32)
        for ref in refs[len(p_got) : len(p_got) + len(q_got)]:
            q = q + ref[...].astype(f32)
        first = where[2 * fs] == 0
        keep[...] = jnp.where(first, p, q)
        send[...] = jnp.where(first, q, p).astype(bf16)

    shape = p_own.shape
    return on_chip(kernel, [array(shape, f32), array(shape, bf16)], ins, "last_sums", moved(ins[1:]), 1)


def ring_next(lay, turned, first):
    n = lay.tp
    size = turned.shape[0] // n
    half = size // 2
    D = turned.shape[1]
    above, below = (n // 2 - 1) * size, (n // 2 + 1) % n * size

    def kernel(turned_ref, up_ref, down_ref, up_out, down_out):
        up_out[:half] = (turned_ref[above : above + half].astype(f32) + up_ref[...].astype(f32)).astype(bf16)
        up_out[half:] = turned_ref[above + half : above + size]
        down_out[:half] = turned_ref[below : below + half]
        low = turned_ref[below + half : below + size].astype(f32) + down_ref[...].astype(f32)
        down_out[half:] = low.astype(bf16)

    outs = [array((size, D), bf16)] * 2
    return on_chip(kernel, outs, [turned, *first], "ring_next", cost(1.0))


def add_cores(keep, got):
    def kernel(keep_ref, got_ref, out_ref):
        out_ref[...] = (keep_ref[...].astype(f32) + got_ref[...].astype(f32)).astype(bf16)

    return on_chip(kernel, [array(keep.shape, bf16)], [keep, got], "add_cores", moved([keep, got]))[0]


def unstack(lay, where, gathered):
    devices, _, size, D = gathered.shape
    T = devices * size
    BD = D // lay.fs

    def kernel(where, row_ref, cot_in, rows_ref, cot_ref):
        at = pl.ds(aligned(pl.program_id(0) * size, size), size)
        rows_ref[at, :] = row_ref[0, 0]
        for n in range(lay.fs):
            cot_ref[at, n * BD : (n + 1) * BD] = cot_in[0, 0, :, column(where, n, BD)]

    return pl.pallas_call(
        kernel,
        out_shape=(array((T, D), bf16), array((T, D), bf16)),
        grid_spec=pltpu.PrefetchScalarGridSpec(
            num_scalar_prefetch=1,
            grid=(devices,),
            in_specs=[
                pl.BlockSpec((1, 1, size, D), lambda d, where: (d, 0, 0, 0)),
                pl.BlockSpec((1, 1, size, D), lambda d, where: (d, 1, 0, 0)),
            ],
            out_specs=(VMEM, VMEM),
        ),
        compiler_params=params(44 * 1024 * 1024),
        name="unstack",
    )(where, gathered, gathered)


def unpack(lay, where, pieces, first):
    BD = pieces[0].shape[2]

    def kernel(where, p0, p1, q0, q1, out_ref):
        for n, (ref, k) in enumerate(listed((p0, p1, q0, q1))):
            out_ref[where[n]] = ref[k, first : first + EXTRA, :]

    return on_chip(kernel, [array((lay.fs, EXTRA, BD), bf16)], [where, *pieces], "unpack", None, 1)[0]


def project(lay, where, rows, gain, shift, bias, tables, pieces):
    T, D = rows.shape
    H = bias.shape[1] // 3
    BD = D // lay.fs

    def kernel(where, rows_ref, gain_ref, shift_ref, bias_ref, tab_ref, p0, p1, q0, q1, normed_ref, stat_ref, q_ref, kv_ref):
        def some_rows(r, carry):
            at = pl.ds(aligned(r * NORM_ROWS, NORM_ROWS), NORM_ROWS)
            x = rows_ref[at, :].astype(f32)
            mean = jnp.sum(x, axis=1, keepdims=True) * (1.0 / D)
            x = x - mean
            var = jnp.sum(x * x, axis=1, keepdims=True) * (1.0 / D)
            scale = lax.rsqrt(var + EPSILON)
            normed = (x * scale * gain_ref[...] + shift_ref[...]).astype(bf16)
            for n in range(lay.fs):
                block = where[lay.fs + n]
                normed_ref[at, pl.ds(aligned(block * BD, BD), BD)] = normed[:, n * BD : (n + 1) * BD]
            stat_ref[0, at, :] = jnp.broadcast_to(mean, (NORM_ROWS, LANES))
            stat_ref[1, at, :] = jnp.broadcast_to(scale, (NORM_ROWS, LANES))
            return carry

        lax.fori_loop(0, T // NORM_ROWS, some_rows, 0, unroll=4)
        keep, ahead, behind = tab_ref[0], tab_ref[1], tab_ref[2]
        for s in range(3):
            total = dot(normed_ref[...], stacked((p0, p1, q0, q1), s * BD, BD)) + bias_ref[:, s * H : (s + 1) * H]
            if s == 0:
                q_ref[...] = (turn(total, keep, ahead, behind).astype(bf16) * (HEAD_DIM**-0.5)).astype(bf16)
            elif s == 1:
                kv_ref[0] = turn(total, keep, ahead, behind).astype(bf16)
            else:
                kv_ref[1] = total.astype(bf16)

    outs = [array((T, D), bf16), array((2, T, LANES), f32), array((T, H), bf16), array((2, T, H), bf16)]
    estimate = cost(12)
    ins = [where, rows, gain, shift, bias, tables, *pieces]
    return on_chip(kernel, outs, ins, "project", estimate, 1)


def attention(lay, queries, kv_own, kv_prev, cot, pieces, paths, codes, tables):
    T, H = queries.shape
    D = cot.shape[1]
    BD = D // lay.fs
    QB = T // QROWS
    SPAN = T + QROWS
    KB = SPAN // KROWS
    pairs = H // LANES
    scaling = HEAD_DIM**-0.5

    def kernel(
        q_ref, own_ref, prev_ref, cot_ref, path_ref, code_ref, tab_ref, p0, p1, q0, q1,
        att_ref, att_t_ref, dq_ref, dq_t_ref, dprev_ref, down_ref,
        k_sc, v_sc, kt_sc, vt_sc, dk_sc, dv_sc, bias_sc, e_sc, g_sc, p_sc, d_sc,
    ):
        pair = pl.program_id(0)
        i = pl.program_id(1)
        across = pl.ds(aligned(pair * LANES, LANES), LANES)

        @pl.when(i == 0)
        def _():
            k_sc[:T] = prev_ref[0, :, across]
            k_sc[T:] = own_ref[0, :, across]
            v_sc[:T] = prev_ref[1, :, across]
            v_sc[T:] = own_ref[1, :, across]
            for c in range(2 * T // KROWS):
                rows = slice(c * KROWS, (c + 1) * KROWS)
                kt_sc[:, rows] = k_sc[rows].T
                vt_sc[:, rows] = v_sc[rows].T
            dk_sc[...] = jnp.zeros_like(dk_sc)
            dv_sc[...] = jnp.zeros_like(dv_sc)

        base = pl.multiple_of(i * QROWS, QROWS)
        own_rows = pl.ds(base, QROWS)
        heads = pl.ds(aligned(3 * BD + pair * LANES, LANES), LANES)
        weight = jnp.concatenate([ref[k, heads, :] for ref, k in listed((p0, p1, q0, q1))], axis=1)
        grad = dot(cot_ref[own_rows, :], weight, NT).astype(bf16)
        queries_pair = q_ref[own_rows, across]

        key_at = lax.broadcasted_iota(jnp.int32, (KROWS, QROWS), 0)
        query_at = lax.broadcasted_iota(jnp.int32, (KROWS, QROWS), 1) + T
        path0, path1, path2 = path_ref[0:1, own_rows], path_ref[1:2, own_rows], path_ref[2:3, own_rows]
        for c in range(KB):
            start = pl.multiple_of(base + c * KROWS, KROWS)
            code = code_ref[pl.ds(start, KROWS), :]
            code = jnp.concatenate([code, code], axis=1)
            at = key_at + c * KROWS
            linked = (code == path0) | (code == path1) | (code == path2)
            seen = (linked & (at <= query_at)) | (at == query_at)
            bias_sc[c] = jnp.where(seen, 0.0, MASKED)

        lane = lax.broadcasted_iota(jnp.int32, (QROWS, LANES), 1)
        att_t, dq_t = [], []
        for head in range(2):
            mine = (lane >= head * HEAD_DIM) & (lane < (head + 1) * HEAD_DIM)
            qh = jnp.where(mine, queries_pair, jnp.zeros_like(queries_pair))
            gh = jnp.where(mine, grad, jnp.zeros_like(grad))
            top = jnp.full((1, QROWS), MASKED, f32)
            for c in range(KB):
                start = pl.multiple_of(base + c * KROWS, KROWS)
                s = dot(k_sc[pl.ds(start, KROWS), :], qh, NT) + bias_sc[c]
                e_sc[c] = s
                top = jnp.maximum(top, jnp.max(s, axis=0, keepdims=True))
            summed = jnp.zeros((1, QROWS), f32)
            mixed = jnp.zeros((1, QROWS), f32)
            for c in range(KB):
                start = pl.multiple_of(base + c * KROWS, KROWS)
                e = jnp.exp(e_sc[c] - top)
                g = dot(v_sc[pl.ds(start, KROWS), :], gh, NT)
                e_sc[c] = e
                g_sc[c] = g
                summed = summed + jnp.sum(e, axis=0, keepdims=True)
                mixed = mixed + jnp.sum(e * g, axis=0, keepdims=True)
            inverse = 1.0 / summed
            mixed = mixed * inverse
            for c in range(KB):
                probs = e_sc[c] * inverse
                p_sc[c * KROWS : (c + 1) * KROWS] = probs.astype(bf16)
                d_sc[c * KROWS : (c + 1) * KROWS] = (probs * (g_sc[c] - mixed)).astype(bf16)
            span = pl.ds(base, SPAN)
            hrow = slice(head * HEAD_DIM, (head + 1) * HEAD_DIM)
            att_t.append(dot(vt_sc[hrow, span], p_sc[...]))
            dq_t.append(dot(kt_sc[hrow, span], d_sc[...]))
            dv_sc[span, :] += dot(p_sc[...], gh)
            dk_sc[span, :] += dot(d_sc[...], qh)
        att = jnp.concatenate(att_t, axis=0)
        att_t_ref[across, own_rows] = att.astype(bf16)
        att_ref[own_rows, across] = att.T.astype(bf16)
        dq = jnp.concatenate(dq_t, axis=0).T * scaling
        dq = turn(dq, tab_ref[0, own_rows, :], -tab_ref[1, own_rows, :], -tab_ref[2, own_rows, :])
        dq_ref[own_rows, across] = dq.astype(bf16)
        dq_t_ref[across, own_rows] = dq.T.astype(bf16)

        @pl.when(i == QB - 1)
        def _():
            dprev_ref[0, :, across] = dk_sc[:T].astype(bf16)
            dprev_ref[1, :, across] = dv_sc[:T].astype(bf16)
            down_ref[0, :, across] = dk_sc[T:]
            down_ref[1, :, across] = dv_sc[T:]

    outs = [
        array((T, H), bf16),
        array((H, T), bf16),
        array((T, H), bf16),
        array((H, T), bf16),
        array((2, T, H), bf16),
        array((2, T, H), f32),
    ]
    scratch = [
        pltpu.VMEM((2 * T, LANES), bf16),
        pltpu.VMEM((2 * T, LANES), bf16),
        pltpu.VMEM((LANES, 2 * T), bf16),
        pltpu.VMEM((LANES, 2 * T), bf16),
        pltpu.VMEM((2 * T, LANES), f32),
        pltpu.VMEM((2 * T, LANES), f32),
        pltpu.VMEM((KB, KROWS, QROWS), f32),
        pltpu.VMEM((KB, KROWS, QROWS), f32),
        pltpu.VMEM((KB, KROWS, QROWS), f32),
        pltpu.VMEM((SPAN, QROWS), bf16),
        pltpu.VMEM((SPAN, QROWS), bf16),
    ]
    ins = [queries, kv_own, kv_prev, cot, paths, codes, tables, *pieces]
    estimate = cost(0.5)
    return on_chip(kernel, outs, ins, "attention", estimate, 0, scratch, (pairs, QB), 18 * 1024 * 1024)


def inner_forward(lay, normed, bias, pieces):
    T, D = normed.shape
    F = bias.shape[1]
    BD = D // lay.fs

    def kernel(x_ref, bias_ref, p0, p1, q0, q1, act_ref, act_t_ref, slope_ref):
        scale = (2.0 / jnp.pi) ** 0.5
        for c in range(F // BD):
            at = slice(c * BD, (c + 1) * BD)
            weight = stacked((p0, p1, q0, q1), c * BD, BD)
            for r in range(T // KROWS):
                rows = slice(r * KROWS, (r + 1) * KROWS)
                u = dot(x_ref[rows, :], weight) + bias_ref[:, at]
                square = u * u
                t = jnp.tanh(scale * (u + 0.044715 * (square * u)))
                act = (0.5 * u * (1.0 + t)).astype(bf16)
                act_ref[rows, at] = act
                act_t_ref[at, rows] = act.T
                slope = 0.5 * (1.0 + t) + 0.5 * u * (1.0 - t * t) * (scale * (1.0 + (3 * 0.044715) * square))
                slope_ref[rows, at] = slope

    outs = [array((T, F), bf16), array((F, T), bf16), array((T, F), f32)]
    estimate = cost(1.0)
    return on_chip(kernel, outs, [normed, bias, *pieces], "inner_forward", estimate)


def inner_backward(lay, cot, slope, pieces):
    T, D = cot.shape
    F = slope.shape[1]
    BD = D // lay.fs

    def kernel(c_ref, slope_ref, p0, p1, q0, q1, grad_ref, grad_t_ref, bias_ref):
        for c in range(F // BD):
            at = slice(c * BD, (c + 1) * BD)
            weight = stacked((p0, p1, q0, q1), c * BD, BD, axis=1)
            sums = jnp.zeros((1, BD), f32)
            for r in range(T // KROWS):
                rows = slice(r * KROWS, (r + 1) * KROWS)
                grad = (dot(c_ref[rows, :], weight, NT) * slope_ref[rows, at]).astype(bf16)
                grad_ref[rows, at] = grad
                grad_t_ref[at, rows] = grad.T
                sums = sums + jnp.sum(grad.astype(f32), axis=0, keepdims=True)
            bias_ref[:, at] = sums

    outs = [array((T, F), bf16), array((F, T), bf16), array((1, F), f32)]
    estimate = cost(5)
    return on_chip(kernel, outs, [cot, slope, *pieces], "inner_backward", estimate)


def block_grads(lay, turned, wide, picks, name):
    F, T = turned.shape
    BD = wide.shape[1] // lay.fs

    def kernel(turned_ref, wide_ref, *outs):
        for ref, (first, count) in zip(outs, picks):
            for k in range(count):
                n = first + k
                ref[k] = dot(turned_ref[...], wide_ref[:, n * BD : (n + 1) * BD]).astype(bf16)

    outs = [array((count, F, BD), bf16) for _, count in picks]
    estimate = cost(2.7)
    return on_chip(kernel, outs, [turned, wide], name, estimate)


def attn_weight_grads(lay, where, normed, cot, dq_t, dkv_t, att_t, sums, picks, name):
    T, D = normed.shape
    H = dq_t.shape[0]
    BD = D // lay.fs
    F = sums[3].shape[1]

    def kernel(where, x_ref, c_ref, dq_ref, dkv_ref, att_ref, sums_ref, got_ref, head_ref, hidden_ref, *refs):
        outs, held = refs[:-1], refs[-1]
        core = where[2 * lay.fs]
        for ref, (first, count) in zip(outs, picks):
            for k in range(count):
                n = first + k
                at = slice(n * BD, (n + 1) * BD)
                ref[k, :H] = dot(dq_ref[...], x_ref[:, at]).astype(bf16)
                ref[k, H : 3 * H] = dot(dkv_ref[...], x_ref[:, at]).astype(bf16)
                ref[k, 3 * H : 4 * H] = dot(att_ref[...], c_ref[:, at]).astype(bf16)
                at = column(where, n, BD)
                mine = (where[n] // (lay.fs // 2) == core).astype(f32)
                held[...] = jnp.zeros_like(held)
                held[0:3, :] = sums_ref[0:3, at] + got_ref[0:3, at]
                held[3:6, :] = head_ref[0:3, :] * mine
                for j in range(F // BD):
                    held[6 + j : 7 + j, :] = hidden_ref[:, j * BD : (j + 1) * BD] * mine
                ref[k, 4 * H :] = held[...].astype(bf16)

    outs = [array((count, 4 * H + EXTRA, BD), bf16) for _, count in picks]
    ins = [where, normed, cot, dq_t, dkv_t, att_t, *sums]
    return on_chip(kernel, outs, ins, name, cost(2.7), 1, [pltpu.VMEM((EXTRA, BD), f32)])


def output_rows(lay, where, attended, activated, attn_pieces, outer_pieces, D):
    T, F = activated.shape
    H = attended.shape[1]
    BD = D // lay.fs
    G = T // 2
    Z = G // lay.tp

    def kernel(where, att_ref, act_ref, a0, a1, b0, b1, p0, p1, q0, q1, keep_ref, send_ref):
        core, z = where[2 * lay.fs], where[2 * lay.fs + 1]
        small = listed((a0, a1, b0, b1))
        large = listed((p0, p1, q0, q1))
        for base, out_ref in ((core * G, keep_ref), ((1 - core) * G, send_ref)):
            rows = pl.ds(aligned(base, G), G)
            for n in range(lay.fs):
                (sref, sk), (lref, lk) = small[n], large[n]
                at = column(where, n, BD)
                total = dot(act_ref[rows, :], lref[lk]) + dot(att_ref[rows, :], sref[sk, 3 * BD : 3 * BD + H, :])
                low = total.astype(bf16)
                for r in range(lay.tp):
                    to = lax.rem(r + lay.tp - z, lay.tp)
                    out_ref[pl.ds(aligned(to * Z, Z), Z), at] = low[r * Z : (r + 1) * Z]

    outs = [array((G, D), bf16)] * 2
    estimate = cost(9.7)
    ins = [where, attended, activated, *attn_pieces, *outer_pieces]
    return on_chip(kernel, outs, ins, "output_rows", estimate, 1)


def normed_grads(lay, where, pre_grad, dq, dkv, rows, stats, cot_sums, attn_pieces, inner_pieces):
    T, F = pre_grad.shape
    D = rows.shape[1]
    G = T // 2
    H = dq.shape[1]
    BD = D // lay.fs
    Z = G // lay.tp

    def kernel(where, pre_ref, dq_ref, dkv_ref, rows_ref, stat_ref, cot_sums_ref, a0, a1, b0, b1, p0, p1, q0, q1, keep_ref, send_ref, sums_ref):
        sums_ref[...] = jnp.zeros_like(sums_ref)
        sums_ref[2:3, :] = cot_sums_ref[...]
        core, z = where[2 * lay.fs], where[2 * lay.fs + 1]
        small = listed((a0, a1, b0, b1))
        large = listed((p0, p1, q0, q1))
        for base, out_ref in ((core * G, keep_ref), ((1 - core) * G, send_ref)):
            rows = pl.ds(aligned(base, G), G)
            left = jnp.concatenate([dq_ref[rows, :], dkv_ref[0, rows, :], dkv_ref[1, rows, :]], axis=1)
            for n in range(lay.fs):
                (sref, sk), (lref, lk) = small[n], large[n]
                at = column(where, n, BD)
                weight = jnp.concatenate([lref[lk, c * BD : (c + 1) * BD, :] for c in range(F // BD)], axis=1)
                narrow = jnp.concatenate([sref[sk, s * BD : (s + 1) * BD, :] for s in range(3)], axis=1)
                total = dot(pre_ref[rows, :], weight, NT) + dot(left, narrow, NT)
                low = total.astype(bf16)
                for r in range(lay.tp):
                    to = lax.rem(r + lay.tp - z, lay.tp)
                    out_ref[pl.ds(aligned(to * Z, Z), Z), at] = low[r * Z : (r + 1) * Z]
                x = rows_ref[rows, at].astype(f32)
                stand = jnp.concatenate(
                    [
                        (x[:, c * LANES : (c + 1) * LANES] - stat_ref[0, rows, :]) * stat_ref[1, rows, :]
                        for c in range(BD // LANES)
                    ],
                    axis=1,
                )
                sums_ref[0:1, at] += jnp.sum(total * stand, axis=0, keepdims=True)
                sums_ref[1:2, at] += jnp.sum(total, axis=0, keepdims=True)

    outs = [array((G, D), bf16), array((G, D), bf16), array((8, D), f32)]
    estimate = cost(11.5)
    ins = [where, pre_grad, dq, dkv, rows, stats, cot_sums, *attn_pieces, *inner_pieces]
    return on_chip(kernel, outs, ins, "normed_grads", estimate, 1)


def key_value_grads(dkv_own, dkv_got, dq, tables):
    _, T, H = dkv_own.shape

    def kernel(own_ref, got_ref, dq_ref, tab_ref, out_ref, out_t_ref, bias_ref):
        dk = own_ref[0] + got_ref[0].astype(f32)
        dv = own_ref[1] + got_ref[1].astype(f32)
        dk = turn(dk, tab_ref[0], -tab_ref[1], -tab_ref[2]).astype(bf16)
        dv = dv.astype(bf16)
        out_ref[0] = dk
        out_ref[1] = dv
        out_t_ref[:H] = dk.T
        out_t_ref[H:] = dv.T
        bias_ref[...] = jnp.zeros_like(bias_ref)
        bias_ref[0:1] = jnp.sum(dq_ref[...].astype(f32), axis=0, keepdims=True)
        bias_ref[1:2] = jnp.sum(dk.astype(f32), axis=0, keepdims=True)
        bias_ref[2:3] = jnp.sum(dv.astype(f32), axis=0, keepdims=True)

    outs = [array((2, T, H), bf16), array((2 * H, T), bf16), array((8, H), f32)]
    return on_chip(kernel, outs, [dkv_own, dkv_got, dq, tables], "key_value_grads", cost(10.0, 1.0))


def body(
    residual,
    norm_gain,
    norm_shift,
    qkv_weight,
    qkv_bias,
    dense_weight,
    dense_bias,
    inner_weight,
    inner_bias,
    outer_weight,
    outer_bias,
    cotangent,
    segment,
    ancestors,
    valid_slot,
):
    lay = Layout()
    fs, tp = lay.fs, lay.tp
    D = residual.shape[1]
    T = residual.shape[0] * tp * 2
    HC = qkv_weight.shape[2] // 2
    FC = inner_weight.shape[1] // 2
    BD = qkv_weight.shape[1]
    assert T >= TREE_LEN - 1 and BD == HC
    where = lay.table()
    is0 = lay.is0

    def halves(group):
        keep, send = lay.by_core(*group)
        return lay.by_core(keep, lay.over_core(send))

    n_small, n_qkv, n_inner = norm_gain.shape[0], qkv_bias.shape[1], inner_bias.shape[0]
    strips = [inner_weight[:, c * BD : (c + 1) * BD] for c in range(2 * FC // BD)]
    count = len(strips) // 2
    inner_group = [jnp.concatenate(strips[:count]), jnp.concatenate(strips[count:])]
    outer_group = [outer_weight[:FC], outer_weight[FC:]]
    together = lax.optimization_barrier
    cot_f = cotangent.astype(f32)
    cot_sums = jnp.sum(cot_f, axis=0, keepdims=True)
    gathered = lax.all_gather(jnp.stack([residual, cotangent]), ("c", "z"), axis=0)
    four = jnp.stack([norm_gain, norm_shift, dense_bias, outer_bias])
    inner_near = gather_near(lay, *halves(inner_group))
    four = small_gather(lay, four[None]).transpose(1, 0, 2).reshape(4, BD)
    biases = jnp.stack(
        [
            jnp.pad(qkv_bias.reshape(-1), (0, BD - 3 * n_qkv)),
            jnp.pad(inner_bias, (0, BD - n_inner)),
        ]
    )
    extra = jnp.concatenate([four, biases, jnp.zeros((EXTRA - 6, BD), bf16)])
    attn_group = [
        jnp.concatenate(
            [
                qkv_weight[:, :, c * HC : (c + 1) * HC].reshape(3 * BD, HC),
                dense_weight[c * HC : (c + 1) * HC],
                extra,
            ]
        )
        for c in range(2)
    ]

    attn_group, outer_group, inner_near = together((attn_group, outer_group, inner_near))
    attn_first, outer_first = halves(attn_group), halves(outer_group)
    attn_near = gather_near(lay, *attn_first)
    outer_near = gather_near(lay, *outer_first)
    attn_near, outer_near = together((attn_near, outer_near))
    attn_pieces = gather_far(lay, *attn_near)
    attn_pieces, inner_near, gathered = together((attn_pieces, inner_near, gathered))
    inner_pieces = gather_far(lay, *inner_near)

    vectors = unpack(lay, where, attn_pieces, 4 * HC).astype(f32)
    gain = vectors[:, 0].reshape(1, D)
    shift = vectors[:, 1].reshape(1, D)
    bias_sum = (vectors[:, 2] + vectors[:, 3]).reshape(1, D)
    mine = lax.dynamic_slice_in_dim(vectors[:, 4:6], lay.core * (fs // 2), fs // 2, axis=0)
    my_qkv_bias = (
        mine[:, 0, : 3 * n_qkv].reshape(fs // 2, 3, n_qkv).transpose(1, 0, 2).reshape(1, 3 * HC)
    )
    my_inner_bias = mine[:, 1, :n_inner].reshape(1, FC)

    base_slot = lay.chip * T
    seg_front = jnp.concatenate([jnp.zeros((T,), jnp.int32), segment])
    valid_front = jnp.concatenate([jnp.zeros((T,), jnp.int32), valid_slot])
    window_seg = lax.dynamic_slice_in_dim(seg_front, base_slot, 2 * T)
    window_valid = lax.dynamic_slice_in_dim(valid_front, base_slot, 2 * T)
    codes = jnp.where(window_valid == 1, window_seg, -1)
    own_seg, own_valid = window_seg[T:], window_valid[T:]
    seg_ids = jnp.arange(ancestors.shape[0], dtype=jnp.int32)
    onehot = (own_seg[None, :] == seg_ids[:, None]).astype(jnp.int32)
    paths = jnp.sum(onehot[None, :, :] * ancestors.T[:, :, None], axis=1)
    paths = jnp.where(own_valid[None, :] == 1, paths, -2)
    key_at = jnp.arange(2 * T, dtype=jnp.int32)[:, None]
    query_at = T + jnp.arange(T, dtype=jnp.int32)[None, :]
    code_col = codes[:, None]
    linked = (code_col == paths[0:1]) | (code_col == paths[1:2]) | (code_col == paths[2:3])
    allowed = (linked & (key_at <= query_at)) | (key_at == query_at)
    positions = jnp.sum(allowed.astype(jnp.int32), axis=0) - 1
    paths8 = jnp.concatenate([paths, jnp.zeros((5, T), jnp.int32)])
    codes_wide = jnp.broadcast_to(code_col, (2 * T, LANES))

    half_rot = ROTARY // 2
    lane = jnp.arange(LANES, dtype=jnp.int32) % HEAD_DIM
    freq = 10000.0 ** (-((lane % half_rot).astype(f32) * 2.0 / ROTARY))
    angle = positions.astype(f32)[:, None] * jnp.where(lane < ROTARY, freq, 0.0)[None, :]
    sine = jnp.sin(angle)
    lane = lane[None, :]
    tables = jnp.stack(
        [
            jnp.cos(angle),
            jnp.where(lane < half_rot, -sine, 0.0),
            jnp.where((lane >= half_rot) & (lane < ROTARY), sine, 0.0),
        ]
    )
    part = (lay.chip * 2 + lay.core) % (fs // 2)
    gathered, part, tables, paths8, codes_wide, my_qkv_bias, my_inner_bias, bias_sum, cot_sums = together(
        (gathered, part, tables, paths8, codes_wide, my_qkv_bias, my_inner_bias, bias_sum, cot_sums)
    )
    rows, cot = unstack(lay, where, gathered)

    normed, stats, queries, kv_own = project(
        lay, where, rows, gain, shift, my_qkv_bias, tables, attn_pieces
    )
    kv_prev = lay.to_chip(kv_own, 1)
    inner_pieces, outer_near, queries = together((inner_pieces, outer_near, queries))
    outer_pieces = gather_far(lay, *outer_near)
    A, B = lay.A, lay.B
    near = ((0, B), (A * B, A))
    far = ((B, A * B - B), (A * B + A, A * B - A))

    activated, act_t, slope = inner_forward(lay, normed, my_inner_bias, inner_pieces)
    outer_far = block_grads(lay, act_t, cot, far, "outer_grads_far")
    outer_near = block_grads(lay, tie(act_t, *outer_far), cot, near, "outer_grads_near")
    queries = tie(queries, *outer_near)
    attended, att_t, dq, dq_t, dkv_prev, dkv_own = attention(
        lay, queries, kv_own, kv_prev, cot, attn_pieces, paths8, codes_wide, tables
    )
    dkv_got = lay.to_chip(dkv_prev, -1)
    outer_got = send_far(lay, outer_far)

    slope = tie(slope, dq)
    pre_grad, pre_t, inner_bias_part = inner_backward(lay, cot, slope, outer_pieces)
    inner_far = block_grads(lay, pre_t, normed, far, "inner_grads_far")
    pre_t = tie(pre_t, *inner_far)
    inner_near = block_grads(lay, pre_t, normed, near, "inner_grads_near")
    inner_got = send_far(lay, inner_far)
    activated, outer_got = together((activated, outer_got, inner_near))[:2]
    keep_out, send_out = output_rows(lay, where, attended, activated, attn_pieces, outer_pieces, D)
    got_out = lay.over_core(send_out)
    dkv_own = tie(dkv_own, keep_out)
    dkv, dkv_t, qkv_bias_part = key_value_grads(dkv_own, dkv_got, dq, tables)
    out_both = add_cores(keep_out, tie(got_out, dkv))
    pre_grad, out_both = together((pre_grad, out_both, dkv))[:2]
    out_first = ring_start(lay, out_both)
    keep_grad, send_grad, norm_sums = normed_grads(
        lay, where, pre_grad, dq, dkv, rows, stats, cot_sums, attn_pieces, inner_pieces
    )
    keep_grad, send_grad, norm_sums, out_first, inner_got = together(
        (keep_grad, send_grad, norm_sums, out_first, inner_got)
    )
    own, p_next, q_next = add_groups([(outer_near, *outer_got), (inner_near, *inner_got)])
    got_grad = lay.over_core(send_grad)
    bit = 1
    got_sums = lay.with_partner(norm_sums, "z", bit)
    while bit < tp // 2:
        norm_sums = add_two(norm_sums, got_sums, "add_two")
        bit *= 2
        got_sums = lay.with_partner(norm_sums, "z", bit)
    got_sums, got_grad = together((got_sums, got_grad))
    sums = (norm_sums, got_sums, qkv_bias_part, inner_bias_part)
    attn_far = attn_weight_grads(
        lay, where, normed, cot, dq_t, tie(dkv_t, own[0]), att_t, sums, far, "attn_grads_far"
    )
    own, attn_far = together((own, attn_far))
    both_keep, both_send = last_groups(lay, where, own, p_next, q_next)
    grad_both = add_cores(keep_grad, got_grad)
    grad_first = ring_start(lay, grad_both)
    dkv_t = tie(dkv_t, grad_both, *attn_far)
    attn_near = attn_weight_grads(lay, where, normed, cot, dq_t, dkv_t, att_t, sums, near, "attn_grads_near")
    attn_far, grad_first, both_keep, both_send = together((attn_far, grad_first, both_keep, both_send))
    both_got = lay.over_core(both_send)
    attn_row = scatter_far(lay, attn_near, attn_far)
    grad_second = ring_second(lay, where, grad_both, grad_first)
    grad_second, out_first = together((grad_second, out_first, attn_row))[:2]
    attn_keep, attn_send = scatter_near(lay, where, *attn_row)
    attn_got = lay.over_core(attn_send)
    out_second = ring_second(lay, where, out_both, out_first)

    def in_core_order(keep, got):
        return lay.by_core(keep, got.astype(f32))

    low, high = in_core_order(both_keep[0], both_got[0])
    outer_weight_grad = jnp.concatenate([low, high], axis=0)
    low, high = in_core_order(both_keep[1], both_got[1])
    inner_weight_grad = jnp.concatenate([low, high], axis=0).T
    low, high = in_core_order(attn_keep, attn_got)
    small = (low + high)[4 * HC :]
    low, high = low[: 4 * HC], high[: 4 * HC]
    qkv_weight_grad = jnp.concatenate(
        [low[: 3 * HC].reshape(3, HC, BD), high[: 3 * HC].reshape(3, HC, BD)], axis=1
    ).transpose(0, 2, 1)
    dense_weight_grad = jnp.concatenate([low[3 * HC :], high[3 * HC :]], axis=0)

    def total_rows(turned, second):
        return ring_block(lay, turned, 0).astype(f32) + second[0].astype(f32) + second[1].astype(f32)

    inputs_f = residual.astype(f32)
    output = (inputs_f + total_rows(out_both, out_second) + bias_sum).astype(bf16)
    row_grad = total_rows(grad_both, grad_second)
    row_mean = jnp.mean(inputs_f, axis=-1, keepdims=True)
    centered = inputs_f - row_mean
    scale = lax.rsqrt(jnp.mean(centered * centered, axis=-1, keepdims=True) + EPSILON)
    stand = centered * scale
    e = row_grad * gain
    e_mean = jnp.mean(e, axis=-1, keepdims=True)
    es_mean = jnp.mean(e * stand, axis=-1, keepdims=True)
    residual_grad = (cot_f + (e - e_mean - stand * es_mean) * scale).astype(bf16)

    small, part, place = together((small, part, lay.z))
    gain_grad, shift_grad, out_bias_grad = (
        lax.dynamic_slice_in_dim(small[k], place * n_small, n_small) for k in range(3)
    )
    qkv_bias_grad = lax.dynamic_slice_in_dim(small[3:6], part * n_qkv, n_qkv, axis=1)
    hidden = small[6 : 6 + FC // BD].reshape(-1)
    inner_bias_grad = lax.dynamic_slice_in_dim(hidden, part * n_inner, n_inner)

    return (
        output,
        residual_grad,
        gain_grad,
        shift_grad,
        qkv_weight_grad,
        qkv_bias_grad,
        dense_weight_grad,
        out_bias_grad,
        inner_weight_grad,
        inner_bias_grad,
        outer_weight_grad,
        out_bias_grad,
    )


def solution(mesh):
    fs, tp = mesh.devices.shape
    inside = jax.sharding.Mesh(mesh.devices.reshape(2, fs // 4, 2, tp), ("a", "b", "c", "z"))
    all_axes = ("a", "b", "c", "z")
    fsdp = ("a", "b", "c")
    crossed = ("z", "a", "b", "c")
    return jax.shard_map(
        body,
        mesh=inside,
        in_specs=(
            P(all_axes, None),
            P(all_axes),
            P(all_axes),
            P(None, fsdp, "z"),
            P(None, crossed),
            P("z", fsdp),
            P(all_axes),
            P(fsdp, "z"),
            P(crossed),
            P("z", fsdp),
            P(all_axes),
            P(all_axes, None),
            P(),
            P(),
            P(),
        ),
        out_specs=(
            P(all_axes, None),
            P(all_axes, None),
            P(all_axes),
            P(all_axes),
            P(None, fsdp, "z"),
            P(None, crossed),
            P("z", fsdp),
            P(all_axes),
            P(fsdp, "z"),
            P(crossed),
            P("z", fsdp),
            P(all_axes),
        ),
        check_vma=False,
    )
```

```python
import jax
import jax.numpy as jnp
from jax import lax
from jax.experimental import pallas as pl
from jax.experimental.pallas import tpu as pltpu
from jax.sharding import PartitionSpec as P

HEAD_DIM = 64
ROTARY = 32
TREE_LEN = 1024
EPSILON = 1e-05
LANES = 128
QROWS = 256
KROWS = 256
MASKED = -1e30
SHARE = 0.2
SCOPED = 14 * 1024 * 1024

f32 = jnp.float32
bf16 = jnp.bfloat16

NN = (((1,), (0,)), ((), ()))
NT = (((1,), (1,)), ((), ()))
TN = (((0,), (0,)), ((), ()))


def dot(left, right, dims=NN):
    return lax.dot_general(left, right, dims, preferred_element_type=f32)


class Layout:
    def __init__(self):
        self.A, self.B, self.tp = (lax.axis_size(n) for n in ("a", "b", "z"))
        self.fs = self.A * self.B * 2
        self.a, self.b, self.core, self.z = (lax.axis_index(n) for n in ("a", "b", "c", "z"))
        self.chip = self.a * self.B + self.b
        self.is0 = self.core == 0

    def blocks(self):
        A, B = self.A, self.B
        first = [(0, i, j) for i in range(A) for j in range(B)]
        second = [(1, i, j) for j in range(B) for i in range(A)]
        return first + second

    def table(self):
        A, B = self.A, self.B
        device = []
        for core, i, j in self.blocks():
            chip = ((self.a + i) % A) * B + (self.b + j) % B
            device.append(chip * 2 + core)
        block = []
        for chip in range(A * B):
            i = (chip // B + A - self.a) % A
            j = (chip % B + B - self.b) % B
            block.append(i * B + j)
            block.append(A * B + j * A + i)
        return jnp.stack(device + block + [self.core, self.z]).astype(jnp.int32)

    def over(self, value, axis, steps):
        n = lax.axis_size(axis)
        return lax.ppermute(value, axis, [(s, (s + steps) % n) for s in range(n)])

    def over_core(self, value):
        return self.over(value, "c", 1)

    def along_a(self, value, steps):
        return self.over(value, "a", steps)

    def along_b(self, value, steps):
        return self.over(value, "b", steps)

    def along_z(self, value, steps):
        return self.over(value, "z", steps)

    def to_chip(self, value, steps):
        pairs = [(s, s + steps) for s in range(self.A * self.B) if 0 <= s + steps < self.A * self.B]
        return lax.ppermute(value, ("a", "b"), pairs)

    def with_partner(self, value, axis, bit):
        return lax.ppermute(value, axis, [(s, s ^ bit) for s in range(lax.axis_size(axis))])

    def by_core(self, own, other):
        return jnp.where(self.is0, own, other), jnp.where(self.is0, other, own)


def tie(value, *others):
    return lax.optimization_barrier((value,) + others)[0]


def gather_near(lay, first, second):
    p_row = [first] + [lay.along_b(first, -j) for j in range(1, lay.B)]
    q_row = [second] + [lay.along_a(second, -i) for i in range(1, lay.A)]
    return stack_blocks(p_row, q_row)


def gather_far(lay, p_row, q_row):
    p_far = [lay.along_a(p_row, -i) for i in range(1, lay.A)]
    q_far = [lay.along_b(q_row, -j) for j in range(1, lay.B)]
    p_far = p_far[0] if lay.A == 2 else jnp.concatenate(p_far)
    q_far = q_far[0] if lay.B == 2 else jnp.concatenate(q_far)
    return (p_row, p_far, q_row, q_far)


def send_far(lay, far):
    A, B = lay.A, lay.B
    p_far, q_far = far
    p_got = [lay.along_a(p_far[(i - 1) * B : i * B], i) for i in range(1, A)]
    q_got = [lay.along_b(q_far[(j - 1) * A : j * A], j) for j in range(1, B)]
    return p_got, q_got


def scatter_far(lay, near, far):
    return add_blocks(near, *send_far(lay, far))


def scatter_near(lay, where, p_sums, q_sums):
    p_got = [lay.along_b(p_sums[j], j) for j in range(1, lay.B)]
    q_got = [lay.along_a(q_sums[i], i) for i in range(1, lay.A)]
    return last_sums(where, p_sums[0], q_sums[0], p_got, q_got, lay.fs)


def small_gather(lay, rows):
    held = rows
    bit = 1
    while bit < lay.tp:
        upper = (lay.z // bit) % 2 == 1
        got = lay.with_partner(held, "z", bit)
        held = jnp.concatenate([jnp.where(upper, got, held), jnp.where(upper, held, got)])
        bit *= 2
    return held


def add_two(left, right, name):
    def kernel(left_ref, right_ref, out_ref):
        out_ref[...] = left_ref[...] + right_ref[...]

    return on_chip(kernel, [array(left.shape, left.dtype)], [left, right], name, moved([left, right]))[0]


def ring_second(lay, turned, onward):
    n = lay.tp
    up, down = onward
    for step in range(1, n // 2):
        up_got, down_got = lay.along_z(up, 1), lay.along_z(down, -1)
        if step == n // 2 - 1:
            return up_got, down_got
        up = (ring_block(lay, turned, n // 2 - 1 - step).astype(f32) + up_got.astype(f32)).astype(bf16)
        down = (ring_block(lay, turned, n // 2 + 1 + step).astype(f32) + down_got.astype(f32)).astype(bf16)


def ring_block(lay, turned, m):
    size = turned.shape[0] // lay.tp
    first = (m % lay.tp) * size
    return turned[first : first + size]


def ring_start(lay, turned):
    far = ring_block(lay, turned, lay.tp // 2)
    half = far.shape[0] // 2
    return lay.along_z(far[:half], 1), lay.along_z(far[half:], -1)


def params(limit=SCOPED):
    return pltpu.CompilerParams(vmem_limit_bytes=limit)


def cost(microseconds, share=None):
    return pl.CostEstimate(flops=int(microseconds * (share or SHARE) * 1.15e9), bytes_accessed=0, transcendentals=0)


VMEM = pl.BlockSpec(memory_space=pltpu.VMEM)
SMEM = pl.BlockSpec(memory_space=pltpu.SMEM)


def array(shape, dtype):
    return jax.ShapeDtypeStruct(shape, dtype)


def listed(refs):
    return [(ref, k) for ref in refs for k in range(ref.shape[0])]


def aligned(value, size):
    return pl.multiple_of(value, size)


def column(where, n, width):
    return pl.ds(aligned(where[n] * width, width), width)


def stacked(refs, first, size, axis=0):
    return jnp.concatenate([ref[k, first : first + size, :] for ref, k in listed(refs)], axis=axis)


def turn(value, keep, ahead, behind):
    half = ROTARY // 2
    parts = []
    for chunk in range(value.shape[1] // LANES):
        v = value[:, chunk * LANES : (chunk + 1) * LANES]
        parts.append(
            v * keep
            + pltpu.roll(v, LANES - half, 1) * ahead
            + pltpu.roll(v, half, 1) * behind
        )
    return parts[0] if len(parts) == 1 else jnp.concatenate(parts, axis=1)


NORM_ROWS = 32
EXTRA = 16


def on_chip(kernel, outs, ins, name, estimate=None, scalars=0, scratch=(), grid=None, limit=SCOPED):
    more = {} if grid is None else {"grid": grid}
    return pl.pallas_call(
        kernel,
        out_shape=tuple(outs),
        in_specs=[SMEM] * scalars + [VMEM] * (len(ins) - scalars),
        out_specs=(VMEM,) * len(outs),
        scratch_shapes=list(scratch),
        compiler_params=params(limit),
        cost_estimate=estimate,
        name=name,
        **more,
    )(*ins)


def moved(values):
    return cost(1.5)


def stack_blocks(p_row, q_row):
    count = len(p_row)

    def kernel(*refs):
        ins, outs = refs[:-2], refs[-2:]
        for k, ref in enumerate(ins):
            if k < count:
                outs[0][k] = ref[...]
            else:
                outs[1][k - count] = ref[...]

    ins = list(p_row) + list(q_row)
    shape, dtype = ins[0].shape, ins[0].dtype
    outs = [array((count,) + shape, dtype), array((len(q_row),) + shape, dtype)]
    return on_chip(kernel, outs, ins, "stack_blocks", moved(ins))


def add_blocks(near, p_got, q_got):
    p_row, q_row = near
    counts = (p_row.shape[0], q_row.shape[0])
    ins = [p_row, q_row] + list(p_got) + list(q_got)

    def kernel(*refs):
        outs = refs[len(ins) :]
        groups = ((refs[0], refs[2 : 2 + len(p_got)]), (refs[1], refs[2 + len(p_got) : len(ins)]))
        at = 0
        for (own, got), count in zip(groups, counts):
            for k in range(count):
                total = own[k].astype(f32)
                for ref in got:
                    total = total + ref[k].astype(f32)
                outs[at][...] = total.astype(outs[at].dtype)
                at += 1

    shape = p_row.shape[1:]
    outs = [array(shape, bf16 if k else f32) for count in counts for k in range(count)]
    done = on_chip(kernel, outs, ins, "add_blocks", moved(ins))
    return list(done[: counts[0]]), list(done[counts[0] :])


def add_groups(groups):
    (p_row, q_row), p_got, q_got = groups[0]
    counts = (p_row.shape[0], q_row.shape[0])
    ins, spans = [], []
    for near, p_in, q_in in groups:
        spans.append((len(ins), len(p_in), len(q_in)))
        ins += [*near, *p_in, *q_in]

    def kernel(*refs):
        outs = refs[len(ins) :]
        for g, (first, p_count, q_count) in enumerate(spans):
            p_ins = refs[first + 2 : first + 2 + p_count]
            q_ins = refs[first + 2 + p_count : first + 2 + p_count + q_count]
            at = 2 * len(groups)
            for side, (own, got) in enumerate(((refs[first], p_ins), (refs[first + 1], q_ins))):
                for k in range(counts[side]):
                    total = own[k].astype(f32)
                    for ref in got:
                        total = total + ref[k].astype(f32)
                    if k == 0:
                        outs[2 * g + side][...] = total
                    else:
                        outs[at][g] = total.astype(bf16)
                        at += 1

    shape = p_row.shape[1:]
    onward = array((len(groups),) + shape, bf16)
    outs = [array(shape, f32)] * (2 * len(groups)) + [onward] * (counts[0] + counts[1] - 2)
    done = on_chip(kernel, outs, ins, "add_groups", moved(ins))
    own, rest = done[: 2 * len(groups)], done[2 * len(groups) :]
    return list(own), list(rest[: counts[0] - 1]), list(rest[counts[0] - 1 :])


def last_groups(lay, where, own, p_next, q_next):
    p_got = [lay.along_b(p, j + 1) for j, p in enumerate(p_next)]
    q_got = [lay.along_a(q, i + 1) for i, q in enumerate(q_next)]
    count = len(own) // 2
    ins = [where, *own, *p_got, *q_got]

    def kernel(where, *refs):
        got, outs = refs[len(own) : len(ins) - 1], refs[len(ins) - 1 :]
        first = where[2 * lay.fs] == 0
        for g in range(count):
            p, q = refs[2 * g][...], refs[2 * g + 1][...]
            for ref in got[: len(p_got)]:
                p = p + ref[g].astype(f32)
            for ref in got[len(p_got) :]:
                q = q + ref[g].astype(f32)
            outs[g][...] = jnp.where(first, p, q)
            outs[-1][g] = jnp.where(first, q, p).astype(bf16)

    shape = own[0].shape
    outs = [array(shape, f32)] * count + [array((count,) + shape, bf16)]
    done = on_chip(kernel, outs, ins, "last_groups", moved(ins[1:]), 1)
    return done[:count], done[count]


def last_sums(where, p_own, q_own, p_got, q_got, fs):
    ins = [where, p_own, q_own] + list(p_got) + list(q_got)

    def kernel(where, p_ref, q_ref, *refs):
        keep, send = refs[-2:]
        p, q = p_ref[...], q_ref[...]
        for ref in refs[: len(p_got)]:
            p = p + ref[...].astype(f32)
        for ref in refs[len(p_got) : len(p_got) + len(q_got)]:
            q = q + ref[...].astype(f32)
        first = where[2 * fs] == 0
        keep[...] = jnp.where(first, p, q)
        send[...] = jnp.where(first, q, p).astype(bf16)

    shape = p_own.shape
    return on_chip(kernel, [array(shape, f32), array(shape, bf16)], ins, "last_sums", moved(ins[1:]), 1)


def ring_next(lay, turned, first):
    n = lay.tp
    size = turned.shape[0] // n
    half = size // 2
    D = turned.shape[1]
    above, below = (n // 2 - 1) * size, (n // 2 + 1) % n * size

    def kernel(turned_ref, up_ref, down_ref, up_out, down_out):
        up_out[:half] = (turned_ref[above : above + half].astype(f32) + up_ref[...].astype(f32)).astype(bf16)
        up_out[half:] = turned_ref[above + half : above + size]
        down_out[:half] = turned_ref[below : below + half]
        low = turned_ref[below + half : below + size].astype(f32) + down_ref[...].astype(f32)
        down_out[half:] = low.astype(bf16)

    outs = [array((size, D), bf16)] * 2
    return on_chip(kernel, outs, [turned, *first], "ring_next", cost(1.0))


def add_cores(keep, got):
    def kernel(keep_ref, got_ref, out_ref):
        out_ref[...] = (keep_ref[...].astype(f32) + got_ref[...].astype(f32)).astype(bf16)

    return on_chip(kernel, [array(keep.shape, bf16)], [keep, got], "add_cores", moved([keep, got]))[0]


def unstack(lay, where, gathered):
    devices, _, size, D = gathered.shape
    T = devices * size
    BD = D // lay.fs

    def kernel(where, row_ref, cot_in, rows_ref, cot_ref):
        at = pl.ds(aligned(pl.program_id(0) * size, size), size)
        rows_ref[at, :] = row_ref[0, 0]
        for n in range(lay.fs):
            cot_ref[at, n * BD : (n + 1) * BD] = cot_in[0, 0, :, column(where, n, BD)]

    return pl.pallas_call(
        kernel,
        out_shape=(array((T, D), bf16), array((T, D), bf16)),
        grid_spec=pltpu.PrefetchScalarGridSpec(
            num_scalar_prefetch=1,
            grid=(devices,),
            in_specs=[
                pl.BlockSpec((1, 1, size, D), lambda d, where: (d, 0, 0, 0)),
                pl.BlockSpec((1, 1, size, D), lambda d, where: (d, 1, 0, 0)),
            ],
            out_specs=(VMEM, VMEM),
        ),
        compiler_params=params(44 * 1024 * 1024),
        name="unstack",
    )(where, gathered, gathered)


def unpack(lay, where, pieces, first):
    BD = pieces[0].shape[2]

    def kernel(where, p0, p1, q0, q1, out_ref):
        for n, (ref, k) in enumerate(listed((p0, p1, q0, q1))):
            out_ref[where[n]] = ref[k, first : first + EXTRA, :]

    return on_chip(kernel, [array((lay.fs, EXTRA, BD), bf16)], [where, *pieces], "unpack", None, 1)[0]


def project(lay, where, rows, gain, shift, bias, tables, pieces):
    T, D = rows.shape
    H = bias.shape[1] // 3
    BD = D // lay.fs

    def kernel(where, rows_ref, gain_ref, shift_ref, bias_ref, tab_ref, p0, p1, q0, q1, normed_ref, stat_ref, q_ref, kv_ref):
        def some_rows(r, carry):
            at = pl.ds(aligned(r * NORM_ROWS, NORM_ROWS), NORM_ROWS)
            x = rows_ref[at, :].astype(f32)
            mean = jnp.sum(x, axis=1, keepdims=True) * (1.0 / D)
            x = x - mean
            var = jnp.sum(x * x, axis=1, keepdims=True) * (1.0 / D)
            scale = lax.rsqrt(var + EPSILON)
            normed = (x * scale * gain_ref[...] + shift_ref[...]).astype(bf16)
            for n in range(lay.fs):
                block = where[lay.fs + n]
                normed_ref[at, pl.ds(aligned(block * BD, BD), BD)] = normed[:, n * BD : (n + 1) * BD]
            stat_ref[0, at, :] = jnp.broadcast_to(mean, (NORM_ROWS, LANES))
            stat_ref[1, at, :] = jnp.broadcast_to(scale, (NORM_ROWS, LANES))
            return carry

        lax.fori_loop(0, T // NORM_ROWS, some_rows, 0, unroll=4)
        keep, ahead, behind = tab_ref[0], tab_ref[1], tab_ref[2]
        for s in range(3):
            total = dot(normed_ref[...], stacked((p0, p1, q0, q1), s * BD, BD)) + bias_ref[:, s * H : (s + 1) * H]
            if s == 0:
                q_ref[...] = (turn(total, keep, ahead, behind).astype(bf16) * (HEAD_DIM**-0.5)).astype(bf16)
            elif s == 1:
                kv_ref[0] = turn(total, keep, ahead, behind).astype(bf16)
            else:
                kv_ref[1] = total.astype(bf16)

    outs = [array((T, D), bf16), array((2, T, LANES), f32), array((T, H), bf16), array((2, T, H), bf16)]
    estimate = cost(12)
    ins = [where, rows, gain, shift, bias, tables, *pieces]
    return on_chip(kernel, outs, ins, "project", estimate, 1)


def attention(lay, queries, kv_own, kv_prev, cot, pieces, paths, codes, tables):
    T, H = queries.shape
    D = cot.shape[1]
    BD = D // lay.fs
    QB = T // QROWS
    SPAN = T + QROWS
    KB = SPAN // KROWS
    pairs = H // LANES
    scaling = HEAD_DIM**-0.5

    def kernel(
        q_ref, own_ref, prev_ref, cot_ref, path_ref, code_ref, tab_ref, p0, p1, q0, q1,
        att_ref, att_t_ref, dq_ref, dq_t_ref, dprev_ref, down_ref,
        k_sc, v_sc, kt_sc, vt_sc, dk_sc, dv_sc, bias_sc, e_sc, g_sc, p_sc, d_sc,
    ):
        pair = pl.program_id(0)
        i = pl.program_id(1)
        across = pl.ds(aligned(pair * LANES, LANES), LANES)

        @pl.when(i == 0)
        def _():
            k_sc[:T] = prev_ref[0, :, across]
            k_sc[T:] = own_ref[0, :, across]
            v_sc[:T] = prev_ref[1, :, across]
            v_sc[T:] = own_ref[1, :, across]
            for c in range(2 * T // KROWS):
                rows = slice(c * KROWS, (c + 1) * KROWS)
                kt_sc[:, rows] = k_sc[rows].T
                vt_sc[:, rows] = v_sc[rows].T
            dk_sc[...] = jnp.zeros_like(dk_sc)
            dv_sc[...] = jnp.zeros_like(dv_sc)

        base = pl.multiple_of(i * QROWS, QROWS)
        own_rows = pl.ds(base, QROWS)
        heads = pl.ds(aligned(3 * BD + pair * LANES, LANES), LANES)
        weight = jnp.concatenate([ref[k, heads, :] for ref, k in listed((p0, p1, q0, q1))], axis=1)
        grad = dot(cot_ref[own_rows, :], weight, NT).astype(bf16)
        queries_pair = q_ref[own_rows, across]

        key_at = lax.broadcasted_iota(jnp.int32, (KROWS, QROWS), 0)
        query_at = lax.broadcasted_iota(jnp.int32, (KROWS, QROWS), 1) + T
        path0, path1, path2 = path_ref[0:1, own_rows], path_ref[1:2, own_rows], path_ref[2:3, own_rows]
        for c in range(KB):
            start = pl.multiple_of(base + c * KROWS, KROWS)
            code = code_ref[pl.ds(start, KROWS), :]
            code = jnp.concatenate([code, code], axis=1)
            at = key_at + c * KROWS
            linked = (code == path0) | (code == path1) | (code == path2)
            seen = (linked & (at <= query_at)) | (at == query_at)
            bias_sc[c] = jnp.where(seen, 0.0, MASKED)

        lane = lax.broadcasted_iota(jnp.int32, (QROWS, LANES), 1)
        att_t, dq_t = [], []
        for head in range(2):
            mine = (lane >= head * HEAD_DIM) & (lane < (head + 1) * HEAD_DIM)
            qh = jnp.where(mine, queries_pair, jnp.zeros_like(queries_pair))
            gh = jnp.where(mine, grad, jnp.zeros_like(grad))
            top = jnp.full((1, QROWS), MASKED, f32)
            for c in range(KB):
                start = pl.multiple_of(base + c * KROWS, KROWS)
                s = dot(k_sc[pl.ds(start, KROWS), :], qh, NT) + bias_sc[c]
                e_sc[c] = s
                top = jnp.maximum(top, jnp.max(s, axis=0, keepdims=True))
            summed = jnp.zeros((1, QROWS), f32)
            mixed = jnp.zeros((1, QROWS), f32)
            for c in range(KB):
                start = pl.multiple_of(base + c * KROWS, KROWS)
                e = jnp.exp(e_sc[c] - top)
                g = dot(v_sc[pl.ds(start, KROWS), :], gh, NT)
                e_sc[c] = e
                g_sc[c] = g
                summed = summed + jnp.sum(e, axis=0, keepdims=True)
                mixed = mixed + jnp.sum(e * g, axis=0, keepdims=True)
            inverse = 1.0 / summed
            mixed = mixed * inverse
            for c in range(KB):
                probs = e_sc[c] * inverse
                p_sc[c * KROWS : (c + 1) * KROWS] = probs.astype(bf16)
                d_sc[c * KROWS : (c + 1) * KROWS] = (probs * (g_sc[c] - mixed)).astype(bf16)
            span = pl.ds(base, SPAN)
            hrow = slice(head * HEAD_DIM, (head + 1) * HEAD_DIM)
            att_t.append(dot(vt_sc[hrow, span], p_sc[...]))
            dq_t.append(dot(kt_sc[hrow, span], d_sc[...]))
            dv_sc[span, :] += dot(p_sc[...], gh)
            dk_sc[span, :] += dot(d_sc[...], qh)
        att = jnp.concatenate(att_t, axis=0)
        att_t_ref[across, own_rows] = att.astype(bf16)
        att_ref[own_rows, across] = att.T.astype(bf16)
        dq = jnp.concatenate(dq_t, axis=0).T * scaling
        dq = turn(dq, tab_ref[0, own_rows, :], -tab_ref[1, own_rows, :], -tab_ref[2, own_rows, :])
        dq_ref[own_rows, across] = dq.astype(bf16)
        dq_t_ref[across, own_rows] = dq.T.astype(bf16)

        @pl.when(i == QB - 1)
        def _():
            dprev_ref[0, :, across] = dk_sc[:T].astype(bf16)
            dprev_ref[1, :, across] = dv_sc[:T].astype(bf16)
            down_ref[0, :, across] = dk_sc[T:]
            down_ref[1, :, across] = dv_sc[T:]

    outs = [
        array((T, H), bf16),
        array((H, T), bf16),
        array((T, H), bf16),
        array((H, T), bf16),
        array((2, T, H), bf16),
        array((2, T, H), f32),
    ]
    scratch = [
        pltpu.VMEM((2 * T, LANES), bf16),
        pltpu.VMEM((2 * T, LANES), bf16),
        pltpu.VMEM((LANES, 2 * T), bf16),
        pltpu.VMEM((LANES, 2 * T), bf16),
        pltpu.VMEM((2 * T, LANES), f32),
        pltpu.VMEM((2 * T, LANES), f32),
        pltpu.VMEM((KB, KROWS, QROWS), f32),
        pltpu.VMEM((KB, KROWS, QROWS), f32),
        pltpu.VMEM((KB, KROWS, QROWS), f32),
        pltpu.VMEM((SPAN, QROWS), bf16),
        pltpu.VMEM((SPAN, QROWS), bf16),
    ]
    ins = [queries, kv_own, kv_prev, cot, paths, codes, tables, *pieces]
    estimate = cost(0.5)
    return on_chip(kernel, outs, ins, "attention", estimate, 0, scratch, (pairs, QB), 18 * 1024 * 1024)


def inner_forward(lay, normed, bias, pieces):
    T, D = normed.shape
    F = bias.shape[1]
    BD = D // lay.fs

    def kernel(x_ref, bias_ref, p0, p1, q0, q1, act_ref, act_t_ref, slope_ref):
        scale = (2.0 / jnp.pi) ** 0.5
        for c in range(F // BD):
            at = slice(c * BD, (c + 1) * BD)
            weight = stacked((p0, p1, q0, q1), c * BD, BD)
            for r in range(T // KROWS):
                rows = slice(r * KROWS, (r + 1) * KROWS)
                u = dot(x_ref[rows, :], weight) + bias_ref[:, at]
                square = u * u
                t = jnp.tanh(scale * (u + 0.044715 * (square * u)))
                act = (0.5 * u * (1.0 + t)).astype(bf16)
                act_ref[rows, at] = act
                act_t_ref[at, rows] = act.T
                slope = 0.5 * (1.0 + t) + 0.5 * u * (1.0 - t * t) * (scale * (1.0 + (3 * 0.044715) * square))
                slope_ref[rows, at] = slope

    outs = [array((T, F), bf16), array((F, T), bf16), array((T, F), f32)]
    estimate = cost(1.0)
    return on_chip(kernel, outs, [normed, bias, *pieces], "inner_forward", estimate)


def inner_backward(lay, cot, slope, pieces):
    T, D = cot.shape
    F = slope.shape[1]
    BD = D // lay.fs

    def kernel(c_ref, slope_ref, p0, p1, q0, q1, grad_ref, grad_t_ref, bias_ref):
        for c in range(F // BD):
            at = slice(c * BD, (c + 1) * BD)
            weight = stacked((p0, p1, q0, q1), c * BD, BD, axis=1)
            sums = jnp.zeros((1, BD), f32)
            for r in range(T // KROWS):
                rows = slice(r * KROWS, (r + 1) * KROWS)
                grad = (dot(c_ref[rows, :], weight, NT) * slope_ref[rows, at]).astype(bf16)
                grad_ref[rows, at] = grad
                grad_t_ref[at, rows] = grad.T
                sums = sums + jnp.sum(grad.astype(f32), axis=0, keepdims=True)
            bias_ref[:, at] = sums

    outs = [array((T, F), bf16), array((F, T), bf16), array((1, F), f32)]
    estimate = cost(5)
    return on_chip(kernel, outs, [cot, slope, *pieces], "inner_backward", estimate)


def block_grads(lay, turned, wide, picks, name):
    F, T = turned.shape
    BD = wide.shape[1] // lay.fs

    def kernel(turned_ref, wide_ref, *outs):
        for ref, (first, count) in zip(outs, picks):
            for k in range(count):
                n = first + k
                ref[k] = dot(turned_ref[...], wide_ref[:, n * BD : (n + 1) * BD]).astype(bf16)

    outs = [array((count, F, BD), bf16) for _, count in picks]
    estimate = cost(2.7)
    return on_chip(kernel, outs, [turned, wide], name, estimate)


def attn_weight_grads(lay, where, normed, cot, dq_t, dkv_t, att_t, sums, picks, name):
    T, D = normed.shape
    H = dq_t.shape[0]
    BD = D // lay.fs
    F = sums[3].shape[1]

    def kernel(where, x_ref, c_ref, dq_ref, dkv_ref, att_ref, sums_ref, got_ref, head_ref, hidden_ref, *refs):
        outs, held = refs[:-1], refs[-1]
        core = where[2 * lay.fs]
        for ref, (first, count) in zip(outs, picks):
            for k in range(count):
                n = first + k
                at = slice(n * BD, (n + 1) * BD)
                ref[k, :H] = dot(dq_ref[...], x_ref[:, at]).astype(bf16)
                ref[k, H : 3 * H] = dot(dkv_ref[...], x_ref[:, at]).astype(bf16)
                ref[k, 3 * H : 4 * H] = dot(att_ref[...], c_ref[:, at]).astype(bf16)
                at = column(where, n, BD)
                mine = (where[n] // (lay.fs // 2) == core).astype(f32)
                held[...] = jnp.zeros_like(held)
                held[0:3, :] = sums_ref[0:3, at] + got_ref[0:3, at]
                held[3:6, :] = head_ref[0:3, :] * mine
                for j in range(F // BD):
                    held[6 + j : 7 + j, :] = hidden_ref[:, j * BD : (j + 1) * BD] * mine
                ref[k, 4 * H :] = held[...].astype(bf16)

    outs = [array((count, 4 * H + EXTRA, BD), bf16) for _, count in picks]
    ins = [where, normed, cot, dq_t, dkv_t, att_t, *sums]
    return on_chip(kernel, outs, ins, name, cost(2.7), 1, [pltpu.VMEM((EXTRA, BD), f32)])


def output_rows(lay, where, attended, activated, attn_pieces, outer_pieces, D):
    T, F = activated.shape
    H = attended.shape[1]
    BD = D // lay.fs
    G = T // 2
    Z = G // lay.tp

    def kernel(where, att_ref, act_ref, a0, a1, b0, b1, p0, p1, q0, q1, keep_ref, send_ref):
        core, z = where[2 * lay.fs], where[2 * lay.fs + 1]
        small = listed((a0, a1, b0, b1))
        large = listed((p0, p1, q0, q1))
        for base, out_ref in ((core * G, keep_ref), ((1 - core) * G, send_ref)):
            rows = pl.ds(aligned(base, G), G)
            for n in range(lay.fs):
                (sref, sk), (lref, lk) = small[n], large[n]
                at = column(where, n, BD)
                total = dot(act_ref[rows, :], lref[lk]) + dot(att_ref[rows, :], sref[sk, 3 * BD : 3 * BD + H, :])
                low = total.astype(bf16)
                for r in range(lay.tp):
                    to = lax.rem(r + lay.tp - z, lay.tp)
                    out_ref[pl.ds(aligned(to * Z, Z), Z), at] = low[r * Z : (r + 1) * Z]

    outs = [array((G, D), bf16)] * 2
    estimate = cost(9.7)
    ins = [where, attended, activated, *attn_pieces, *outer_pieces]
    return on_chip(kernel, outs, ins, "output_rows", estimate, 1)


def normed_grads(lay, where, pre_grad, dq, dkv, rows, stats, cot_sums, attn_pieces, inner_pieces):
    T, F = pre_grad.shape
    D = rows.shape[1]
    G = T // 2
    H = dq.shape[1]
    BD = D // lay.fs
    Z = G // lay.tp

    def kernel(where, pre_ref, dq_ref, dkv_ref, rows_ref, stat_ref, cot_sums_ref, a0, a1, b0, b1, p0, p1, q0, q1, keep_ref, send_ref, sums_ref):
        sums_ref[...] = jnp.zeros_like(sums_ref)
        sums_ref[2:3, :] = cot_sums_ref[...]
        core, z = where[2 * lay.fs], where[2 * lay.fs + 1]
        small = listed((a0, a1, b0, b1))
        large = listed((p0, p1, q0, q1))
        for base, out_ref in ((core * G, keep_ref), ((1 - core) * G, send_ref)):
            rows = pl.ds(aligned(base, G), G)
            left = jnp.concatenate([dq_ref[rows, :], dkv_ref[0, rows, :], dkv_ref[1, rows, :]], axis=1)
            for n in range(lay.fs):
                (sref, sk), (lref, lk) = small[n], large[n]
                at = column(where, n, BD)
                weight = jnp.concatenate([lref[lk, c * BD : (c + 1) * BD, :] for c in range(F // BD)], axis=1)
                narrow = jnp.concatenate([sref[sk, s * BD : (s + 1) * BD, :] for s in range(3)], axis=1)
                total = dot(pre_ref[rows, :], weight, NT) + dot(left, narrow, NT)
                low = total.astype(bf16)
                for r in range(lay.tp):
                    to = lax.rem(r + lay.tp - z, lay.tp)
                    out_ref[pl.ds(aligned(to * Z, Z), Z), at] = low[r * Z : (r + 1) * Z]
                x = rows_ref[rows, at].astype(f32)
                stand = jnp.concatenate(
                    [
                        (x[:, c * LANES : (c + 1) * LANES] - stat_ref[0, rows, :]) * stat_ref[1, rows, :]
                        for c in range(BD // LANES)
                    ],
                    axis=1,
                )
                sums_ref[0:1, at] += jnp.sum(total * stand, axis=0, keepdims=True)
                sums_ref[1:2, at] += jnp.sum(total, axis=0, keepdims=True)

    outs = [array((G, D), bf16), array((G, D), bf16), array((8, D), f32)]
    estimate = cost(11.5)
    ins = [where, pre_grad, dq, dkv, rows, stats, cot_sums, *attn_pieces, *inner_pieces]
    return on_chip(kernel, outs, ins, "normed_grads", estimate, 1)


def key_value_grads(dkv_own, dkv_got, dq, tables):
    _, T, H = dkv_own.shape

    def kernel(own_ref, got_ref, dq_ref, tab_ref, out_ref, out_t_ref, bias_ref):
        dk = own_ref[0] + got_ref[0].astype(f32)
        dv = own_ref[1] + got_ref[1].astype(f32)
        dk = turn(dk, tab_ref[0], -tab_ref[1], -tab_ref[2]).astype(bf16)
        dv = dv.astype(bf16)
        out_ref[0] = dk
        out_ref[1] = dv
        out_t_ref[:H] = dk.T
        out_t_ref[H:] = dv.T
        bias_ref[...] = jnp.zeros_like(bias_ref)
        bias_ref[0:1] = jnp.sum(dq_ref[...].astype(f32), axis=0, keepdims=True)
        bias_ref[1:2] = jnp.sum(dk.astype(f32), axis=0, keepdims=True)
        bias_ref[2:3] = jnp.sum(dv.astype(f32), axis=0, keepdims=True)

    outs = [array((2, T, H), bf16), array((2 * H, T), bf16), array((8, H), f32)]
    return on_chip(kernel, outs, [dkv_own, dkv_got, dq, tables], "key_value_grads", cost(10.0, 1.0))


def body(
    residual,
    norm_gain,
    norm_shift,
    qkv_weight,
    qkv_bias,
    dense_weight,
    dense_bias,
    inner_weight,
    inner_bias,
    outer_weight,
    outer_bias,
    cotangent,
    segment,
    ancestors,
    valid_slot,
):
    lay = Layout()
    fs, tp = lay.fs, lay.tp
    D = residual.shape[1]
    T = residual.shape[0] * tp * 2
    HC = qkv_weight.shape[2] // 2
    FC = inner_weight.shape[1] // 2
    BD = qkv_weight.shape[1]
    assert T >= TREE_LEN - 1 and BD == HC
    where = lay.table()
    is0 = lay.is0

    def halves(group):
        keep, send = lay.by_core(*group)
        return lay.by_core(keep, lay.over_core(send))

    n_small, n_qkv, n_inner = norm_gain.shape[0], qkv_bias.shape[1], inner_bias.shape[0]
    strips = [inner_weight[:, c * BD : (c + 1) * BD] for c in range(2 * FC // BD)]
    count = len(strips) // 2
    inner_group = [jnp.concatenate(strips[:count]), jnp.concatenate(strips[count:])]
    outer_group = [outer_weight[:FC], outer_weight[FC:]]
    together = lax.optimization_barrier
    cot_f = cotangent.astype(f32)
    cot_sums = jnp.sum(cot_f, axis=0, keepdims=True)
    gathered = lax.all_gather(jnp.stack([residual, cotangent]), ("c", "z"), axis=0)
    four = jnp.stack([norm_gain, norm_shift, dense_bias, outer_bias])
    inner_near = gather_near(lay, *halves(inner_group))
    four = small_gather(lay, four[None]).transpose(1, 0, 2).reshape(4, BD)
    biases = jnp.stack(
        [
            jnp.pad(qkv_bias.reshape(-1), (0, BD - 3 * n_qkv)),
            jnp.pad(inner_bias, (0, BD - n_inner)),
        ]
    )
    extra = jnp.concatenate([four, biases, jnp.zeros((EXTRA - 6, BD), bf16)])
    attn_group = [
        jnp.concatenate(
            [
                qkv_weight[:, :, c * HC : (c + 1) * HC].reshape(3 * BD, HC),
                dense_weight[c * HC : (c + 1) * HC],
                extra,
            ]
        )
        for c in range(2)
    ]

    attn_group, outer_group, inner_near = together((attn_group, outer_group, inner_near))
    attn_first, outer_first = halves(attn_group), halves(outer_group)
    attn_near = gather_near(lay, *attn_first)
    outer_near = gather_near(lay, *outer_first)
    attn_near, outer_near = together((attn_near, outer_near))
    attn_pieces = gather_far(lay, *attn_near)
    attn_pieces, inner_near, gathered = together((attn_pieces, inner_near, gathered))
    inner_pieces = gather_far(lay, *inner_near)

    vectors = unpack(lay, where, attn_pieces, 4 * HC).astype(f32)
    gain = vectors[:, 0].reshape(1, D)
    shift = vectors[:, 1].reshape(1, D)
    bias_sum = (vectors[:, 2] + vectors[:, 3]).reshape(1, D)
    mine = lax.dynamic_slice_in_dim(vectors[:, 4:6], lay.core * (fs // 2), fs // 2, axis=0)
    my_qkv_bias = (
        mine[:, 0, : 3 * n_qkv].reshape(fs // 2, 3, n_qkv).transpose(1, 0, 2).reshape(1, 3 * HC)
    )
    my_inner_bias = mine[:, 1, :n_inner].reshape(1, FC)

    base_slot = lay.chip * T
    seg_front = jnp.concatenate([jnp.zeros((T,), jnp.int32), segment])
    valid_front = jnp.concatenate([jnp.zeros((T,), jnp.int32), valid_slot])
    window_seg = lax.dynamic_slice_in_dim(seg_front, base_slot, 2 * T)
    window_valid = lax.dynamic_slice_in_dim(valid_front, base_slot, 2 * T)
    codes = jnp.where(window_valid == 1, window_seg, -1)
    own_seg, own_valid = window_seg[T:], window_valid[T:]
    seg_ids = jnp.arange(ancestors.shape[0], dtype=jnp.int32)
    onehot = (own_seg[None, :] == seg_ids[:, None]).astype(jnp.int32)
    paths = jnp.sum(onehot[None, :, :] * ancestors.T[:, :, None], axis=1)
    paths = jnp.where(own_valid[None, :] == 1, paths, -2)
    key_at = jnp.arange(2 * T, dtype=jnp.int32)[:, None]
    query_at = T + jnp.arange(T, dtype=jnp.int32)[None, :]
    code_col = codes[:, None]
    linked = (code_col == paths[0:1]) | (code_col == paths[1:2]) | (code_col == paths[2:3])
    allowed = (linked & (key_at <= query_at)) | (key_at == query_at)
    positions = jnp.sum(allowed.astype(jnp.int32), axis=0) - 1
    paths8 = jnp.concatenate([paths, jnp.zeros((5, T), jnp.int32)])
    codes_wide = jnp.broadcast_to(code_col, (2 * T, LANES))

    half_rot = ROTARY // 2
    lane = jnp.arange(LANES, dtype=jnp.int32) % HEAD_DIM
    freq = 10000.0 ** (-((lane % half_rot).astype(f32) * 2.0 / ROTARY))
    angle = positions.astype(f32)[:, None] * jnp.where(lane < ROTARY, freq, 0.0)[None, :]
    sine = jnp.sin(angle)
    lane = lane[None, :]
    tables = jnp.stack(
        [
            jnp.cos(angle),
            jnp.where(lane < half_rot, -sine, 0.0),
            jnp.where((lane >= half_rot) & (lane < ROTARY), sine, 0.0),
        ]
    )
    part = (lay.chip * 2 + lay.core) % (fs // 2)
    gathered, part, tables, paths8, codes_wide, my_qkv_bias, my_inner_bias, bias_sum, cot_sums = together(
        (gathered, part, tables, paths8, codes_wide, my_qkv_bias, my_inner_bias, bias_sum, cot_sums)
    )
    rows, cot = unstack(lay, where, gathered)

    normed, stats, queries, kv_own = project(
        lay, where, rows, gain, shift, my_qkv_bias, tables, attn_pieces
    )
    kv_prev = lay.to_chip(kv_own, 1)
    inner_pieces, outer_near, queries = together((inner_pieces, outer_near, queries))
    outer_pieces = gather_far(lay, *outer_near)
    A, B = lay.A, lay.B
    near = ((0, B), (A * B, A))
    far = ((B, A * B - B), (A * B + A, A * B - A))

    activated, act_t, slope = inner_forward(lay, normed, my_inner_bias, inner_pieces)
    outer_far = block_grads(lay, act_t, cot, far, "outer_grads_far")
    outer_near = block_grads(lay, tie(act_t, *outer_far), cot, near, "outer_grads_near")
    queries = tie(queries, *outer_near)
    attended, att_t, dq, dq_t, dkv_prev, dkv_own = attention(
        lay, queries, kv_own, kv_prev, cot, attn_pieces, paths8, codes_wide, tables
    )
    dkv_got = lay.to_chip(dkv_prev, -1)
    outer_got = send_far(lay, outer_far)

    slope = tie(slope, dq)
    pre_grad, pre_t, inner_bias_part = inner_backward(lay, cot, slope, outer_pieces)
    inner_far = block_grads(lay, pre_t, normed, far, "inner_grads_far")
    pre_t = tie(pre_t, *inner_far)
    inner_near = block_grads(lay, pre_t, normed, near, "inner_grads_near")
    inner_got = send_far(lay, inner_far)
    activated, outer_got = together((activated, outer_got, inner_near))[:2]
    keep_out, send_out = output_rows(lay, where, attended, activated, attn_pieces, outer_pieces, D)
    got_out = lay.over_core(send_out)
    dkv_own = tie(dkv_own, keep_out)
    dkv, dkv_t, qkv_bias_part = key_value_grads(dkv_own, dkv_got, dq, tables)
    out_both = add_cores(keep_out, tie(got_out, dkv))
    pre_grad, out_both = together((pre_grad, out_both, dkv))[:2]
    out_first = ring_start(lay, out_both)
    keep_grad, send_grad, norm_sums = normed_grads(
        lay, where, pre_grad, dq, dkv, rows, stats, cot_sums, attn_pieces, inner_pieces
    )
    keep_grad, send_grad, norm_sums, out_first, inner_got = together(
        (keep_grad, send_grad, norm_sums, out_first, inner_got)
    )
    own, p_next, q_next = add_groups([(outer_near, *outer_got), (inner_near, *inner_got)])
    got_grad = lay.over_core(send_grad)
    bit = 1
    got_sums = lay.with_partner(norm_sums, "z", bit)
    while bit < tp // 2:
        norm_sums = add_two(norm_sums, got_sums, "add_two")
        bit *= 2
        got_sums = lay.with_partner(norm_sums, "z", bit)
    got_sums, got_grad = together((got_sums, got_grad))
    sums = (norm_sums, got_sums, qkv_bias_part, inner_bias_part)
    attn_far = attn_weight_grads(
        lay, where, normed, cot, dq_t, tie(dkv_t, own[0]), att_t, sums, far, "attn_grads_far"
    )
    own, attn_far = together((own, attn_far))
    both_keep, both_send = last_groups(lay, where, own, p_next, q_next)
    grad_both = add_cores(keep_grad, got_grad)
    grad_first = ring_start(lay, grad_both)
    attn_far, grad_first, both_keep, both_send = together((attn_far, grad_first, both_keep, both_send))
    onward = tuple(ring_next(lay, grad_both, grad_first))
    dkv_t, onward = together((dkv_t, onward))
    attn_near = attn_weight_grads(lay, where, normed, cot, dq_t, dkv_t, att_t, sums, near, "attn_grads_near")
    both_got = lay.over_core(both_send)
    attn_row = scatter_far(lay, attn_near, attn_far)
    grad_second = ring_second(lay, grad_both, onward)
    grad_second, out_first = together((grad_second, out_first, attn_row))[:2]
    attn_keep, attn_send = scatter_near(lay, where, *attn_row)
    attn_got = lay.over_core(attn_send)
    out_second = ring_second(lay, out_both, ring_next(lay, out_both, out_first))

    def in_core_order(keep, got):
        return lay.by_core(keep, got.astype(f32))

    low, high = in_core_order(both_keep[0], both_got[0])
    outer_weight_grad = jnp.concatenate([low, high], axis=0)
    low, high = in_core_order(both_keep[1], both_got[1])
    inner_weight_grad = jnp.concatenate([low, high], axis=0).T
    low, high = in_core_order(attn_keep, attn_got)
    small = (low + high)[4 * HC :]
    low, high = low[: 4 * HC], high[: 4 * HC]
    qkv_weight_grad = jnp.concatenate(
        [low[: 3 * HC].reshape(3, HC, BD), high[: 3 * HC].reshape(3, HC, BD)], axis=1
    ).transpose(0, 2, 1)
    dense_weight_grad = jnp.concatenate([low[3 * HC :], high[3 * HC :]], axis=0)

    def total_rows(turned, second):
        return ring_block(lay, turned, 0).astype(f32) + second[0].astype(f32) + second[1].astype(f32)

    inputs_f = residual.astype(f32)
    output = (inputs_f + total_rows(out_both, out_second) + bias_sum).astype(bf16)
    row_grad = total_rows(grad_both, grad_second)
    row_mean = jnp.mean(inputs_f, axis=-1, keepdims=True)
    centered = inputs_f - row_mean
    scale = lax.rsqrt(jnp.mean(centered * centered, axis=-1, keepdims=True) + EPSILON)
    stand = centered * scale
    e = row_grad * gain
    e_mean = jnp.mean(e, axis=-1, keepdims=True)
    es_mean = jnp.mean(e * stand, axis=-1, keepdims=True)
    residual_grad = (cot_f + (e - e_mean - stand * es_mean) * scale).astype(bf16)

    small, part, place = together((small, part, lay.z))
    gain_grad, shift_grad, out_bias_grad = (
        lax.dynamic_slice_in_dim(small[k], place * n_small, n_small) for k in range(3)
    )
    qkv_bias_grad = lax.dynamic_slice_in_dim(small[3:6], part * n_qkv, n_qkv, axis=1)
    hidden = small[6 : 6 + FC // BD].reshape(-1)
    inner_bias_grad = lax.dynamic_slice_in_dim(hidden, part * n_inner, n_inner)

    return (
        output,
        residual_grad,
        gain_grad,
        shift_grad,
        qkv_weight_grad,
        qkv_bias_grad,
        dense_weight_grad,
        out_bias_grad,
        inner_weight_grad,
        inner_bias_grad,
        outer_weight_grad,
        out_bias_grad,
    )


def solution(mesh):
    fs, tp = mesh.devices.shape
    inside = jax.sharding.Mesh(mesh.devices.reshape(2, fs // 4, 2, tp), ("a", "b", "c", "z"))
    all_axes = ("a", "b", "c", "z")
    fsdp = ("a", "b", "c")
    crossed = ("z", "a", "b", "c")
    return jax.shard_map(
        body,
        mesh=inside,
        in_specs=(
            P(all_axes, None),
            P(all_axes),
            P(all_axes),
            P(None, fsdp, "z"),
            P(None, crossed),
            P("z", fsdp),
            P(all_axes),
            P(fsdp, "z"),
            P(crossed),
            P("z", fsdp),
            P(all_axes),
            P(all_axes, None),
            P(),
            P(),
            P(),
        ),
        out_specs=(
            P(all_axes, None),
            P(all_axes, None),
            P(all_axes),
            P(all_axes),
            P(None, fsdp, "z"),
            P(None, crossed),
            P("z", fsdp),
            P(all_axes),
            P(fsdp, "z"),
            P(crossed),
            P("z", fsdp),
            P(all_axes),
        ),
        check_vma=False,
    )
```
